32 devices in a mesh: dp: 16 (over z, x, core), tensor: 2 (over y).
Axes of the slice: x: 2, y: 2, z: 4, core: 2. Of those that a mesh axis runs over, the one named last changes fastest.
Arguments:
- tokens: bfloat16 [32, 512, 1024], P('dp', 'tensor'), may hold values from -6 to 6
- seq_counts: int32 [16], replicated, may hold values from 1 to 2, as said below
- mix_gain: bfloat16 [1024], replicated, may hold values from 0.5 to 1.5
- query_key_value_gate_weight: bfloat16 [1024, 6144], P(None, 'tensor'), may hold values from -0.1875 to 0.1875
- beta_decay_weight: bfloat16 [1024, 16], P(None, 'tensor'), may hold values from -0.1875 to 0.1875
- conv_w: float32 [4, 4096], P(None, 'tensor'), may hold values from -3 to 3
- a_log: float32 [8], P('tensor'), may hold values from -7 to -0.7
- dt_bias: float32 [8], P('tensor'), may hold values from -1 to 1
- o_gain: bfloat16 [256], replicated, may hold values from 0.5 to 1.5
- output_weight: bfloat16 [1024, 2048], P(None, 'tensor'), may hold values from -0.125 to 0.125
- ffn_gain: bfloat16 [1024], replicated, may hold values from 0.5 to 1.5
- gate_weight: bfloat16 [1024, 2816], P(None, 'tensor'), may hold values from -0.1875 to 0.1875
- up_weight: bfloat16 [1024, 2816], P(None, 'tensor'), may hold values from -0.1875 to 0.1875
- down_weight: bfloat16 [1024, 2816], P(None, 'tensor'), may hold values from -0.109375 to 0.109375
- cotangent: bfloat16 [32, 512, 1024], P('dp', 'tensor'), may hold values from -6 to 6
Outputs:
- output: bfloat16 [32, 512, 1024], P('dp', 'tensor')
- tokens_grad: float32 [32, 512, 1024], P('dp', 'tensor')
- mix_gain_grad: float32 [1024], replicated
- w_qkvg_grad: float32 [1024, 6144], P('dp', 'tensor')
- w_ba_grad: float32 [1024, 16], P('dp', 'tensor')
- conv_grad: float32 [4, 4096], P(None, 'tensor')
- a_log_grad: float32 [8], P('tensor')
- dt_bias_grad: float32 [8], P('tensor')
- o_gain_grad: float32 [256], replicated
- w_out_grad: float32 [1024, 2048], P('dp', 'tensor')
- ffn_gain_grad: float32 [1024], replicated
- w_gate_grad: float32 [1024, 2816], P('dp', 'tensor')
- w_up_grad: float32 [1024, 2816], P('dp', 'tensor')
- w_down_grad: float32 [1024, 2816], P('dp', 'tensor')
The draws below stay inside these ranges and needn't reach their ends.
Inputs may be any that keep to these rules, and one draw needn't show every extreme that they name: Data group g holds seq_counts[g] sequences in its first slots; exactly 1 group hold 2, the others one.
All inputs are finite; a program needn't handle non-finite values.
Results may differ from the reference program's by a relative error of at most 0.018.
Values may be sent and summed in bfloat16 or wider, within the bound.
No kernel may reach another device: no remote copies, remote signals or barrier semaphores. Data moves between devices by JAX's collectives and lax.ppermute only.
A program may use at most 256 MiB of HBM per device.

```python
import jax
import jax.numpy as jnp
from jax import lax

D = 1024
H = 8
DK = 128
DV = 256
FF = 2816
CONV = 4
SPAN = 64
CAP = 2
EXTRA = 1
LEN = 512
SEQS = 17
SLOTS = 32
N_DP = 16


def draw_seq_counts(key, part):
    order = jax.random.permutation(key, N_DP)
    return jnp.where(order < EXTRA, CAP, 1).astype(jnp.int32)


def levels(own_key, shape, shards, smallest, largest):
    factor_of = 1.0
    for dim, parts in shards:
        draws = jax.random.uniform(jax.random.fold_in(jax.random.fold_in(own_key, 6), dim), (parts,), jnp.float32, smallest / len(shards), largest / len(shards))
        factor_of = factor_of * jnp.repeat(jnp.exp(draws), shape[dim] // parts).reshape((-1,) + (1,) * (len(shape) - 1 - dim))
    return factor_of


def bell_draw(key, extent, scale, bound, cuts=(), kind=jnp.bfloat16):
    values = jax.random.normal(key, extent, jnp.float32) * scale
    if len(cuts) > 0:
        values = levels(key, extent, cuts, -0.22, 0.18) * values
    return jnp.clip(values, min=-bound, max=bound).astype(kind)


def setup_inputs(seed: int = 0) -> dict:
    key_of = jax.random.split(jax.random.key(seed), 16)
    tokens = bell_draw(key_of[0], (SLOTS, LEN, D), 1.0, 6.0, ((0, 16), (1, 2)))
    seq_counts = draw_seq_counts(jax.random.fold_in(key_of[15], 71), 0)
    mix_gain = jnp.clip(1.0 + 0.1 * jax.random.normal(key_of[2], (D,), jnp.float32), 0.5, 1.5).astype(jnp.bfloat16)
    query_key_value_gate_weight = bell_draw(key_of[3], (D, H * (2 * DK + 2 * DV)), D ** -0.5, 0.1875, ((1, 2),))
    beta_decay_weight = bell_draw(key_of[4], (D, 2 * H), D ** -0.5, 0.1875, ((1, 2),))
    conv_w = bell_draw(key_of[5], (CONV, H * (2 * DK + DV)), CONV ** -0.5, 3.0, ((1, 2),), jnp.float32)
    a_log = jnp.clip(-7.0 + 6.3 * jax.random.uniform(key_of[6], (H,), jnp.float32) ** levels(key_of[6], (H,), ((0, 2),), -0.2, 0.2), -7.0, -0.7)
    dt_bias = jnp.clip(jax.random.uniform(key_of[7], (H,), jnp.float32, -1.0, 1.0) * levels(key_of[7], (H,), ((0, 2),), -0.4, 0.0), -1.0, 1.0)
    o_gain = jnp.clip(1.0 + 0.1 * jax.random.normal(key_of[8], (DV,), jnp.float32), 0.5, 1.5).astype(jnp.bfloat16)
    output_weight = bell_draw(key_of[9], (D, H * DV), (H * DV) ** -0.5, 0.125, ((1, 2),))
    ffn_gain = jnp.clip(1.0 + 0.1 * jax.random.normal(key_of[10], (D,), jnp.float32), 0.5, 1.5).astype(jnp.bfloat16)
    gate_weight = bell_draw(key_of[11], (D, FF), D ** -0.5, 0.1875, ((1, 2),))
    up_weight = bell_draw(key_of[12], (D, FF), D ** -0.5, 0.1875, ((1, 2),))
    down_weight = bell_draw(key_of[13], (D, FF), FF ** -0.5, 0.109375, ((1, 2),))
    cotangent = bell_draw(key_of[14], (SLOTS, LEN, D), 1.0, 6.0, ((0, 16), (1, 2)))
    return dict(tokens=tokens, seq_counts=seq_counts, mix_gain=mix_gain, query_key_value_gate_weight=query_key_value_gate_weight, beta_decay_weight=beta_decay_weight, conv_w=conv_w, a_log=a_log, dt_bias=dt_bias, o_gain=o_gain, output_weight=output_weight, ffn_gain=ffn_gain, gate_weight=gate_weight, up_weight=up_weight, down_weight=down_weight, cotangent=cotangent)


EPS_ROW = 1e-06
EPS_HEAD = 1e-05
EPS_UNIT = 1e-06
EXACT_MATMUL = lax.Precision.HIGHEST

@jax.custom_vjp
def low(v):
    return lax.optimization_barrier(v.astype(jnp.bfloat16)).astype(jnp.float32)

@jax.custom_vjp
def low_back(v):
    return v

def low_keep(v):
    return (low(v), None)

def low_pass(kept, grad):
    return (grad,)

def back_keep(v):
    return (v, None)

def back_low(kept, grad):
    return (low(grad),)
low.defvjp(low_keep, low_pass)
low_back.defvjp(back_keep, back_low)

def delta_block(state, block):
    queries, key_rows, val_rows, betas, decays = block
    cumulative = jnp.cumsum(decays)
    block_len = decays.shape[0]
    rowpos = jnp.arange(block_len)[:, None]
    colpos = jnp.arange(block_len)[None, :]
    lower_mask = rowpos >= colpos
    strict = rowpos > colpos
    decay_mat = jnp.where(lower_mask, jnp.exp(jnp.where(lower_mask, cumulative[:, None] - cumulative[None, :], 0.0)), 0.0)
    key_gram = jnp.dot(key_rows, key_rows.T, precision=EXACT_MATMUL)
    lower_mat = jnp.where(strict, betas[:, None] * key_gram * decay_mat, 0.0)
    right_side = jnp.concatenate([(betas * jnp.exp(cumulative))[:, None] * key_rows, betas[:, None] * val_rows], axis=1)
    solved = lax.linalg.triangular_solve(lower_mat, right_side, left_side=True, lower=True, unit_diagonal=True)
    key_width = key_rows.shape[1]
    fresh_vals = solved[:, key_width:] - jnp.dot(solved[:, :key_width], state, precision=EXACT_MATMUL)
    scores = jnp.dot(queries, key_rows.T, precision=EXACT_MATMUL) * decay_mat
    outputs = jnp.dot(queries * jnp.exp(cumulative)[:, None], state, precision=EXACT_MATMUL) + jnp.dot(scores, fresh_vals, precision=EXACT_MATMUL)
    tail_decay = jnp.exp(cumulative[-1] - cumulative)
    new_state = jnp.exp(cumulative[-1]) * state + jnp.dot((key_rows * tail_decay[:, None]).T, fresh_vals, precision=EXACT_MATMUL)
    return (new_state, outputs)

def one_head(queries, key_rows, val_rows, betas, decays):
    length = queries.shape[0]
    blocks = length // SPAN
    pieces = (queries.reshape(blocks, SPAN, -1), key_rows.reshape(blocks, SPAN, -1), val_rows.reshape(blocks, SPAN, -1), betas.reshape(blocks, SPAN), decays.reshape(blocks, SPAN))
    initial = jnp.zeros((queries.shape[1], val_rows.shape[1]), queries.dtype)
    final_state, outputs = lax.scan(jax.checkpoint(delta_block), initial, pieces)
    return outputs.reshape(length, -1)

def delta_rule(queries, key_rows, val_rows, betas, decays):
    return jax.vmap(jax.vmap(one_head, in_axes=1, out_axes=1))(queries, key_rows, val_rows, betas, decays)

def prepare(projected_rows, scalar_input, conv_w, a_log, dt_bias):
    heads = scalar_input.shape[-1] // 2
    batch = projected_rows.shape[0]
    length = projected_rows.shape[1]
    conv_width = 2 * DK + DV
    per_head = projected_rows.reshape(batch, length, heads, 2 * DK + 2 * DV)
    mixing = per_head[..., :conv_width]
    out_gate = per_head[..., conv_width:]
    kernel = conv_w.reshape(CONV, heads, conv_width)
    padded = jnp.pad(mixing, ((0, 0), (CONV - 1, 0), (0, 0), (0, 0)))
    summed = kernel[0] * padded[:, 0:length]
    for offset in range(1, CONV):
        summed = summed + kernel[offset] * padded[:, offset:offset + length]
    active = jax.nn.silu(summed)
    query_raw = active[..., :DK]
    key_raw = active[..., DK:2 * DK]
    val_rows = active[..., 2 * DK:]
    queries = query_raw * lax.rsqrt(lax.optimization_barrier(jnp.sum(query_raw * query_raw, axis=-1, keepdims=True)) + EPS_UNIT) * DK ** (-0.5)
    key_rows = key_raw * lax.rsqrt(lax.optimization_barrier(jnp.sum(key_raw * key_raw, axis=-1, keepdims=True)) + EPS_UNIT)
    scalars = scalar_input.reshape(batch, length, heads, 2)
    betas = jax.nn.sigmoid(scalars[..., 0])
    decays = -jnp.exp(a_log) * jax.nn.softplus(scalars[..., 1] + dt_bias)
    return (queries, key_rows, val_rows, betas, decays, out_gate)

def finish(queries, key_rows, val_rows, betas, decays, out_gate, o_gain):
    mixed = delta_rule(queries, key_rows, val_rows, betas, decays)
    scale = lax.rsqrt(lax.optimization_barrier(jnp.mean(mixed * mixed, axis=-1, keepdims=True)) + EPS_HEAD)
    normed = mixed * scale * o_gain * jax.nn.silu(out_gate)
    return normed.reshape(normed.shape[0], normed.shape[1], -1)

def forward(states, mix_gain, query_key_value_gate_weight, beta_decay_weight, conv_w, a_log, dt_bias, o_gain, output_weight, ffn_gain, gate_weight, up_weight, down_weight):
    normed = states * lax.rsqrt(lax.optimization_barrier(jnp.mean(states * states, axis=-1, keepdims=True)) + EPS_ROW)
    mixer_input = low(normed * mix_gain)
    projected_rows = low_back(jnp.einsum('xwn,nj->xwj', mixer_input, query_key_value_gate_weight, precision=EXACT_MATMUL))
    scalar_input = low_back(jnp.einsum('xwn,nj->xwj', mixer_input, beta_decay_weight, precision=EXACT_MATMUL))
    queries, key_rows, val_rows, betas, decays, out_gate = prepare(projected_rows, scalar_input, conv_w, a_log, dt_bias)
    head_output = low(finish(low(queries), low(key_rows), low(val_rows), betas, decays, out_gate, o_gain))
    branch_output = low_back(jnp.einsum('oaz,kz->oak', head_output, output_weight, precision=EXACT_MATMUL))
    middle_activation = states + branch_output
    feedforward_input = low(middle_activation * lax.rsqrt(lax.optimization_barrier(jnp.mean(middle_activation * middle_activation, axis=-1, keepdims=True)) + EPS_ROW) * ffn_gain)
    gate_activation = low_back(jnp.einsum('eyv,vi->eyi', feedforward_input, gate_weight, precision=EXACT_MATMUL))
    up_activation = low_back(jnp.einsum('eyv,vi->eyi', feedforward_input, up_weight, precision=EXACT_MATMUL))
    hidden_units = low(jax.nn.silu(gate_activation) * up_activation)
    return middle_activation + jnp.einsum('oqi,ti->oqt', hidden_units, down_weight, precision=EXACT_MATMUL)

def reference(tokens, seq_counts, mix_gain, query_key_value_gate_weight, beta_decay_weight, conv_w, a_log, dt_bias, o_gain, output_weight, ffn_gain, gate_weight, up_weight, down_weight, cotangent):
    slot_ids = jnp.arange(N_DP * CAP, dtype=jnp.int32)
    owners = slot_ids // CAP
    places = slot_ids % CAP
    live_slots = (places < seq_counts[owners]).astype(jnp.int32)
    order = jnp.argsort(1 - live_slots, stable=True)[:SEQS].astype(jnp.int32)
    states = tokens[order].astype(jnp.float32)
    grads_in = cotangent[order].astype(jnp.float32)
    weights = (mix_gain, query_key_value_gate_weight, beta_decay_weight, conv_w, a_log, dt_bias, o_gain, output_weight, ffn_gain, gate_weight, up_weight, down_weight)
    params = tuple((param.astype(jnp.float32) for param in weights))
    result, pullback = jax.vjp(forward, states, *params)
    grads = pullback(grads_in)
    output = jnp.zeros(tokens.shape, jnp.bfloat16).at[order].set(result.astype(jnp.bfloat16))
    tokens_grad = jnp.zeros(tokens.shape, jnp.float32).at[order].set(grads[0])
    return (output, tokens_grad, grads[1], grads[2], grads[3], grads[4], grads[5], grads[6], grads[7], grads[8], grads[9], grads[10], grads[11], grads[12])
```

```python
import jax
import jax.numpy as jnp
from jax import lax
from jax.experimental import pallas as pl
from jax.experimental.pallas import tpu as pltpu
from jax.sharding import PartitionSpec as P

DK = 128
DV = 256
CONV = 4
SPAN = 64
PRE = 2 * DK + DV
HEAD = PRE + DV
TILE = 4 * SPAN
F32 = jnp.float32
BF16 = jnp.bfloat16

EPS_ROW = 1e-06
EPS_HEAD = 1e-05
EPS_UNIT = 1e-06

NN = (((1,), (0,)), ((), ()))
NT = (((1,), (1,)), ((), ()))
TN = (((0,), (0,)), ((), ()))


def mm(left, right, dims=NN):
    return lax.dot_general(
        left.astype(BF16), right.astype(BF16), dims, preferred_element_type=F32
    )


def split(value):
    high = value.astype(BF16)
    return high, (value - high.astype(F32)).astype(BF16)


def mm3(left, right):
    left_high, left_low = left
    right_high, right_low = right
    return (
        mm(left_high, right_high) + mm(left_high, right_low) + mm(left_low, right_high)
    )


def tile_masks():
    row = lax.broadcasted_iota(jnp.int32, (TILE, TILE), 0)
    col = lax.broadcasted_iota(jnp.int32, (TILE, TILE), 1)
    same = (row // SPAN) == (col // SPAN)
    return row, col, same


def shifted(rows, steps):
    length = rows.shape[0]
    if steps == 0:
        return rows
    pos = lax.broadcasted_iota(jnp.int32, rows.shape, 0)
    rolled = pltpu.roll(rows, steps % length, axis=0)
    keep = pos >= steps if steps > 0 else pos < length + steps
    return jnp.where(keep, rolled, 0.0)


def convolve(pre, taps):
    summed = taps[CONV - 1 : CONV] * pre
    for back in range(1, CONV):
        tap = CONV - 1 - back
        summed = summed + taps[tap : tap + 1] * shifted(pre, back)
    return summed


def unit_rows(raw):
    scale = lax.rsqrt(jnp.sum(raw * raw, axis=1, keepdims=True) + EPS_UNIT)
    return raw * scale, scale


def decay_rows(scalars, a_log, dt_bias):
    rate = jnp.exp(jnp.full((1, 1), a_log, F32))
    shifted_in = scalars[1:2] + dt_bias
    soft = jnp.maximum(shifted_in, 0.0) + jnp.log1p(jnp.exp(-jnp.abs(shifted_in)))
    return lax.logistic(scalars[0:1]), -rate * soft, -rate * lax.logistic(shifted_in)


def tile_scalars(row, col, same, beta_row, decay_row):
    lower = same & (row >= col)
    eye = row == col
    cum_col = jnp.sum(jnp.where(lower, decay_row, 0.0), axis=1, keepdims=True)
    beta_col = jnp.sum(jnp.where(eye, beta_row, 0.0), axis=1, keepdims=True)
    cum_row = jnp.sum(jnp.where(eye, cum_col, 0.0), axis=0, keepdims=True)
    last = (row // SPAN) * SPAN + (SPAN - 1)
    last_col = jnp.sum(jnp.where(col == last, cum_row, 0.0), axis=1, keepdims=True)
    decay = jnp.where(lower, jnp.exp(jnp.where(lower, cum_col - cum_row, 0.0)), 0.0)
    return cum_col, beta_col, last_col, decay


def invert(row, col, coupling):
    inverse = None
    size = 1
    while size < SPAN:
        level = (
            ((row // (2 * size)) == (col // (2 * size)))
            & (((row // size) % 2) == 1)
            & (((col // size) % 2) == 0)
        )
        part = jnp.where(level, coupling, 0.0)
        if size == 1:
            inverse = jnp.where(row == col, 1.0, 0.0) - part
        else:
            pieces = split(inverse)
            inner = mm3(split(part), pieces)
            inverse = inverse - mm3(pieces, split(inner))
        size *= 2
    return inverse


def mixer_kernel(
    a_log_ref,
    dt_bias_ref,
    mix_ref,
    weight_ref,
    scalar_weight_ref,
    taps_ref,
    gain_ref,
    head_ref,
    proj_ref,
    scalar_ref,
    inverse_ref,
    state_ref,
    mixed_ref,
    fresh_ref,
):
    head = pl.program_id(1)
    inputs = mix_ref[0]
    projected = mm(inputs, weight_ref[...])
    proj_ref[0] = projected
    scalars = mm(scalar_weight_ref[0], inputs, NT)
    scalar_ref[0, 0] = scalars
    beta_all, decay_all, _ = decay_rows(scalars, a_log_ref[0, head], dt_bias_ref[0, head])
    summed = convolve(projected[:, :PRE], taps_ref[...])
    active = summed * lax.logistic(summed)
    queries = (unit_rows(active[:, :DK])[0] * DK ** (-0.5)).astype(BF16)
    keys = unit_rows(active[:, DK : 2 * DK])[0].astype(BF16)
    vals = active[:, 2 * DK :].astype(BF16)
    row, col, same = tile_masks()
    strict = same & (row > col)
    length = inputs.shape[0]
    state = jnp.zeros((DK, DV), F32)
    for tile in range(length // TILE):
        span = slice(tile * TILE, (tile + 1) * TILE)
        cum_col, beta_col, last_col, decay = tile_scalars(
            row, col, same, beta_all[:, span], decay_all[:, span]
        )
        q = queries[span]
        k = keys[span]
        k_f = k.astype(F32)
        coupling = jnp.where(strict, beta_col * mm(k, k, NT) * decay, 0.0)
        inverse = invert(row, col, coupling)
        inverse_ref[0, 0, tile] = inverse
        grow = jnp.exp(cum_col)
        solved_w = mm(inverse, (beta_col * grow) * k_f)
        solved_u = mm(inverse, beta_col * vals[span].astype(F32))
        scores = mm(q, k, NT) * decay
        grown = q.astype(F32) * grow
        tail = k_f * jnp.exp(last_col - cum_col)
        both = jnp.concatenate([solved_w, solved_u], axis=1).astype(BF16)
        fresh = []
        read = []
        for block in range(TILE // SPAN):
            part = slice(block * SPAN, (block + 1) * SPAN)
            state_ref[0, 0, tile * (TILE // SPAN) + block] = state
            step = mm(tail[part], both[part], TN)
            used = mm(jnp.concatenate([solved_w[part], grown[part]], axis=0), state)
            fresh.append(solved_u[part] - used[:SPAN])
            read.append(used[SPAN:])
            carry = jnp.exp(last_col[block * SPAN : block * SPAN + 1])
            state = carry * state + step[:, DK:] - mm(step[:, :DK], state)
        fresh = jnp.concatenate(fresh, axis=0)
        mixed = jnp.concatenate(read, axis=0) + mm(scores, fresh)
        fresh_ref[0, 0, span] = fresh
        mixed_ref[0, 0, span] = mixed
        scale = lax.rsqrt(jnp.mean(mixed * mixed, axis=1, keepdims=True) + EPS_HEAD)
        gate = projected[span, PRE:]
        head_ref[0, span] = (
            mixed * scale * gain_ref[...] * (gate * lax.logistic(gate))
        ).astype(BF16)


def mixer_forward(a_log, dt_bias, mix, weight, scalar_weight, taps, gain):
    slots, length, width = mix.shape
    heads = weight.shape[1] // HEAD
    blocks = length // SPAN
    tiles = length // TILE
    unit = lambda s, h: (s, h, 0, 0)
    unit5 = lambda s, h: (s, h, 0, 0, 0)
    return pl.pallas_call(
        mixer_kernel,
        name="mixer_forward",
        grid=(slots, heads),
        in_specs=[
            pl.BlockSpec(memory_space=pltpu.SMEM),
            pl.BlockSpec(memory_space=pltpu.SMEM),
            pl.BlockSpec((1, length, width), lambda s, h: (s, 0, 0)),
            pl.BlockSpec((width, HEAD), lambda s, h: (0, h)),
            pl.BlockSpec((1, 8, width), lambda s, h: (h, 0, 0)),
            pl.BlockSpec((CONV, PRE), lambda s, h: (0, h)),
            pl.BlockSpec((1, DV), lambda s, h: (0, 0)),
        ],
        out_specs=[
            pl.BlockSpec((1, length, DV), lambda s, h: (s, 0, h)),
            pl.BlockSpec((1, length, HEAD), lambda s, h: (s, 0, h)),
            pl.BlockSpec((1, 1, 8, length), unit),
            pl.BlockSpec((1, 1, tiles, TILE, TILE), unit5),
            pl.BlockSpec((1, 1, blocks, DK, DV), unit5),
            pl.BlockSpec((1, 1, length, DV), unit),
            pl.BlockSpec((1, 1, length, DV), unit),
        ],
        out_shape=[
            jax.ShapeDtypeStruct((slots, length, heads * DV), BF16),
            jax.ShapeDtypeStruct((slots, length, heads * HEAD), F32),
            jax.ShapeDtypeStruct((slots, heads, 8, length), F32),
            jax.ShapeDtypeStruct((slots, heads, tiles, TILE, TILE), F32),
            jax.ShapeDtypeStruct((slots, heads, blocks, DK, DV), F32),
            jax.ShapeDtypeStruct((slots, heads, length, DV), F32),
            jax.ShapeDtypeStruct((slots, heads, length, DV), F32),
        ],
        compiler_params=pltpu.CompilerParams(
            dimension_semantics=("arbitrary", "arbitrary"), vmem_limit_bytes=56 << 20
        ),
    )(a_log, dt_bias, mix, weight, scalar_weight, taps, gain)


def mixer_back_kernel(
    a_log_ref,
    dt_bias_ref,
    grad_ref,
    proj_ref,
    scalar_ref,
    inverse_ref,
    state_ref,
    mixed_ref,
    fresh_ref,
    taps_ref,
    gain_ref,
    grad_proj_ref,
    grad_scalar_ref,
    grad_taps_ref,
    grad_gain_ref,
):
    head = pl.program_id(1)
    length = grad_ref.shape[1]
    pre = proj_ref[0, :, :PRE]
    taps = taps_ref[...]
    gain = gain_ref[...]
    scalars = scalar_ref[0, 0]
    beta_all, decay_all, slope_all = decay_rows(
        scalars, a_log_ref[0, head], dt_bias_ref[0, head]
    )
    summed = convolve(pre, taps)
    sig = lax.logistic(summed)
    active = summed * sig
    query_unit, query_scale = unit_rows(active[:, :DK])
    key_unit, key_scale = unit_rows(active[:, DK : 2 * DK])
    queries = (query_unit * DK ** (-0.5)).astype(BF16)
    keys = key_unit.astype(BF16)
    vals = active[:, 2 * DK :].astype(BF16)
    row, col, same = tile_masks()
    lower = same & (row >= col)
    strict = same & (row > col)
    eye = row == col
    is_last = (row[:, :1] % SPAN) == (SPAN - 1)
    per = TILE // SPAN
    grad_gain = jnp.zeros((1, DV), F32)
    carried = jnp.zeros((DK, DV), F32)
    grad_active = [None] * (length // TILE)
    grad_beta_rows = [None] * (length // TILE)
    grad_decay_rows = [None] * (length // TILE)
    for tile in reversed(range(length // TILE)):
        span = slice(tile * TILE, (tile + 1) * TILE)
        cum_col, beta_col, last_col, decay = tile_scalars(
            row, col, same, beta_all[:, span], decay_all[:, span]
        )
        gate = proj_ref[0, span, PRE:]
        gate_sig = lax.logistic(gate)
        gate_act = gate * gate_sig
        mixed = mixed_ref[0, 0, span]
        scale = lax.rsqrt(jnp.mean(mixed * mixed, axis=1, keepdims=True) + EPS_HEAD)
        normed = mixed * scale
        grad = grad_ref[0, span]
        grad_normed = grad * normed
        grad_gain = grad_gain + jnp.sum(grad_normed * gate_act, axis=0, keepdims=True)
        grad_proj_ref[0, span, PRE:] = (
            grad_normed * gain * (gate_sig * (1.0 + gate * (1.0 - gate_sig)))
        ).astype(BF16)
        weighted = grad * gain * gate_act
        grad_mixed = scale * (
            weighted - normed * jnp.mean(weighted * normed, axis=1, keepdims=True)
        )
        q = queries[span]
        k = keys[span]
        v = vals[span]
        q_f = q.astype(F32)
        k_f = k.astype(F32)
        v_f = v.astype(F32)
        gram = mm(k, k, NT)
        coupling = jnp.where(strict, beta_col * gram * decay, 0.0)
        scores = mm(q, k, NT) * decay
        inverse = inverse_ref[0, 0, tile].astype(BF16)
        grow = jnp.exp(cum_col)
        fall = jnp.exp(last_col - cum_col)
        beta_grow = beta_col * grow
        key_in = beta_grow * k_f
        solved_w = mm(inverse, key_in)
        solved_u = mm(inverse, beta_col * v_f)
        grown = q_f * grow
        tail = k_f * fall
        fresh = fresh_ref[0, 0, span]
        grad_low = grad_mixed.astype(BF16)
        local = mm(scores, grad_low, TN)
        grad_fresh = [None] * per
        grad_grown = [None] * per
        grad_tail = [None] * per
        grad_w = [None] * per
        carry_terms = [None] * per
        for block in reversed(range(per)):
            part = slice(block * SPAN, (block + 1) * SPAN)
            state = state_ref[0, 0, tile * per + block]
            carry = jnp.exp(last_col[block * SPAN : block * SPAN + 1])
            here = local[part] + mm(tail[part], carried)
            grad_fresh[block] = here
            both = mm(jnp.concatenate([grad_low[part], here.astype(BF16)], axis=0), state, NT)
            grad_grown[block] = both[:SPAN]
            grad_w[block] = -both[SPAN:]
            grad_tail[block] = mm(fresh[part], carried, NT)
            product = jnp.sum(state * carried, axis=0, keepdims=True)
            carry_terms[block] = carry * jnp.sum(product, axis=1, keepdims=True)
            carried = carry * carried + mm(
                jnp.concatenate([grown[part], -solved_w[part]], axis=0),
                jnp.concatenate([grad_low[part], here.astype(BF16)], axis=0),
                TN,
            )
        grad_fresh = jnp.concatenate(grad_fresh, axis=0)
        grad_grown = jnp.concatenate(grad_grown, axis=0)
        grad_tail = jnp.concatenate(grad_tail, axis=0)
        grad_w = jnp.concatenate(grad_w, axis=0)
        grad_key_in = mm(inverse, grad_w, TN)
        grad_val_in = mm(inverse, grad_fresh, TN)
        grad_coupling = jnp.where(
            strict, -(mm(grad_key_in, solved_w, NT) + mm(grad_val_in, solved_u, NT)), 0.0
        )
        grad_scores = mm(grad_low, fresh, NT)
        score_term = grad_scores * decay
        gram_term = grad_coupling * decay
        grad_beta = (
            jnp.sum(gram_term * gram, axis=1, keepdims=True)
            + grow * jnp.sum(grad_key_in * k_f, axis=1, keepdims=True)
            + jnp.sum(grad_val_in * v_f, axis=1, keepdims=True)
        )
        gram_term = gram_term * beta_col
        exponent = grad_coupling * coupling + grad_scores * scores
        tail_sum = jnp.sum(grad_tail * tail, axis=1, keepdims=True)
        grad_cum = (
            jnp.sum(exponent, axis=1, keepdims=True)
            + jnp.sum(grad_grown * grown, axis=1, keepdims=True)
            + jnp.sum(grad_key_in * key_in, axis=1, keepdims=True)
            - tail_sum
        )
        ends = []
        for block in range(per):
            part = slice(block * SPAN, (block + 1) * SPAN)
            total = jnp.sum(tail_sum[part], axis=0, keepdims=True) + carry_terms[block]
            ends.append(jnp.broadcast_to(total, (SPAN, 1)))
        grad_cum = grad_cum + jnp.where(is_last, jnp.concatenate(ends, axis=0), 0.0)
        column_sum = jnp.sum(exponent, axis=0, keepdims=True)
        cum_back = jnp.sum(jnp.where(eye, column_sum, 0.0), axis=1, keepdims=True)
        grad_cum = grad_cum - cum_back
        grad_decay_rows[tile] = jnp.sum(jnp.where(lower, grad_cum, 0.0), axis=0, keepdims=True)
        grad_beta_rows[tile] = jnp.sum(jnp.where(eye, grad_beta, 0.0), axis=0, keepdims=True)
        grad_q = mm(score_term, k) + grad_grown * grow
        grad_k = (
            mm(score_term, q, TN)
            + mm(gram_term, k)
            + mm(gram_term, k, TN)
            + grad_tail * fall
            + beta_grow * grad_key_in
        )
        grad_v = beta_col * grad_val_in
        q_u = query_unit[span]
        k_u = key_unit[span]
        grad_query_raw = (query_scale[span] * DK ** (-0.5)) * (
            grad_q - q_u * jnp.sum(grad_q * q_u, axis=1, keepdims=True)
        )
        grad_key_raw = key_scale[span] * (
            grad_k - k_u * jnp.sum(grad_k * k_u, axis=1, keepdims=True)
        )
        grad_active[tile] = jnp.concatenate([grad_query_raw, grad_key_raw, grad_v], axis=1)
    grad_gain_ref[0, 0] = jnp.broadcast_to(grad_gain, (8, DV))
    grad_summed = jnp.concatenate(grad_active, axis=0) * (sig * (1.0 + summed * (1.0 - sig)))
    grad_pre = taps[CONV - 1 : CONV] * grad_summed
    grad_taps = [None] * CONV
    grad_taps[CONV - 1] = jnp.sum(grad_summed * pre, axis=0, keepdims=True)
    for back in range(1, CONV):
        tap = CONV - 1 - back
        ahead = shifted(grad_summed, -back)
        grad_pre = grad_pre + taps[tap : tap + 1] * ahead
        grad_taps[tap] = jnp.sum(ahead * pre, axis=0, keepdims=True)
    grad_proj_ref[0, :, :PRE] = grad_pre.astype(BF16)
    grad_taps_ref[0, 0] = jnp.concatenate(grad_taps + [jnp.zeros((8 - CONV, PRE), F32)], axis=0)
    grad_beta_all = jnp.concatenate(grad_beta_rows, axis=1)
    grad_decay_all = jnp.concatenate(grad_decay_rows, axis=1)
    grad_scalar_ref[0, 0] = jnp.concatenate(
        [
            grad_beta_all * beta_all * (1.0 - beta_all),
            grad_decay_all * slope_all,
            grad_decay_all * decay_all,
            jnp.zeros((5, length), F32),
        ],
        axis=0,
    )


def mixer_backward(
    a_log, dt_bias, grad_head, projected, scalars, inverse, states, mixed, fresh, taps, gain
):
    slots, length, _ = grad_head.shape
    heads = scalars.shape[1]
    blocks = length // SPAN
    tiles = length // TILE
    unit = lambda s, h: (s, h, 0, 0)
    unit5 = lambda s, h: (s, h, 0, 0, 0)
    return pl.pallas_call(
        mixer_back_kernel,
        name="mixer_backward",
        grid=(slots, heads),
        in_specs=[
            pl.BlockSpec(memory_space=pltpu.SMEM),
            pl.BlockSpec(memory_space=pltpu.SMEM),
            pl.BlockSpec((1, length, DV), lambda s, h: (s, 0, h)),
            pl.BlockSpec((1, length, HEAD), lambda s, h: (s, 0, h)),
            pl.BlockSpec((1, 1, 8, length), unit),
            pl.BlockSpec((1, 1, tiles, TILE, TILE), unit5),
            pl.BlockSpec((1, 1, blocks, DK, DV), unit5),
            pl.BlockSpec((1, 1, length, DV), unit),
            pl.BlockSpec((1, 1, length, DV), unit),
            pl.BlockSpec((CONV, PRE), lambda s, h: (0, h)),
            pl.BlockSpec((1, DV), lambda s, h: (0, 0)),
        ],
        out_specs=[
            pl.BlockSpec((1, length, HEAD), lambda s, h: (s, 0, h)),
            pl.BlockSpec((1, 1, 8, length), unit),
            pl.BlockSpec((1, 1, 8, PRE), unit),
            pl.BlockSpec((1, 1, 8, DV), unit),
        ],
        out_shape=[
            jax.ShapeDtypeStruct((slots, length, heads * HEAD), BF16),
            jax.ShapeDtypeStruct((slots, heads, 8, length), F32),
            jax.ShapeDtypeStruct((slots, heads, 8, PRE), F32),
            jax.ShapeDtypeStruct((slots, heads, 8, DV), F32),
        ],
        compiler_params=pltpu.CompilerParams(
            dimension_semantics=("arbitrary", "arbitrary"), vmem_limit_bytes=56 << 20
        ),
    )(
        a_log,
        dt_bias,
        grad_head,
        projected,
        scalars,
        inverse,
        states,
        mixed,
        fresh,
        taps,
        gain,
    )


def row_scale(values):
    return lax.rsqrt(jnp.mean(values * values, axis=-1, keepdims=True) + EPS_ROW)


def norm_back(grad_out, normed, scale, gain_vec):
    weighted = grad_out * gain_vec
    return scale * (weighted - normed * jnp.mean(weighted * normed, axis=-1, keepdims=True))


def contract_rows(left, right):
    return lax.dot_general(
        left, right, (((0, 1), (0, 1)), ((), ())), preferred_element_type=jnp.float32
    )


def contract_last(left, right):
    return lax.dot_general(
        left, right, (((2,), (1,)), ((), ())), preferred_element_type=jnp.float32
    )


def reduce_small(own_parts, shared_parts):
    ranks = lax.axis_size("tensor")
    own = jnp.concatenate([part.reshape(-1) for part in own_parts])
    shared = jnp.concatenate([part.reshape(-1) for part in shared_parts])
    rank = lax.axis_index("tensor")
    spread = jnp.where(
        (jnp.arange(ranks) == rank)[:, None], own[None, :], 0.0
    ).reshape(-1)
    total = lax.psum(jnp.concatenate([spread, shared]), ("dp", "tensor"))
    mine = lax.dynamic_slice_in_dim(total, rank * own.shape[0], own.shape[0])
    results = []
    at = 0
    for part in own_parts:
        results.append(mine[at : at + part.size].reshape(part.shape))
        at += part.size
    at = ranks * own.shape[0]
    for part in shared_parts:
        results.append(total[at : at + part.size].reshape(part.shape))
        at += part.size
    return results


def body(
    tokens,
    seq_counts,
    mix_gain,
    query_key_value_gate_weight,
    beta_decay_weight,
    conv_w,
    a_log,
    dt_bias,
    o_gain,
    output_weight,
    ffn_gain,
    gate_weight,
    up_weight,
    down_weight,
    cotangent,
):
    slots = tokens.shape[0]
    heads = a_log.shape[0]
    width = tokens.shape[2]
    group = lax.axis_index("dp")
    count_here = lax.dynamic_index_in_dim(seq_counts, group, keepdims=False)
    live = (jnp.arange(slots) < count_here).astype(jnp.float32)[:, None, None]
    states = tokens.astype(jnp.float32)
    mix_scale = row_scale(states)
    mix_normed = states * mix_scale
    mix_gain_f = mix_gain.astype(jnp.float32)
    mix_local = (mix_normed * mix_gain_f).astype(jnp.bfloat16)
    mix_full = lax.all_gather(mix_local, "tensor", axis=1, tiled=True)
    o_gain_f = o_gain.astype(jnp.float32)[None]
    scalar_weight = jnp.pad(
        beta_decay_weight.T.reshape(heads, 2, width), ((0, 0), (0, 6), (0, 0))
    )
    head_low, projected, scalars, inverse, block_states, mixed, fresh = mixer_forward(
        a_log[None],
        dt_bias[None],
        mix_full,
        query_key_value_gate_weight,
        scalar_weight,
        conv_w,
        o_gain_f,
    )
    branch_output = lax.psum_scatter(
        contract_last(head_low, output_weight), "tensor", scatter_dimension=1, tiled=True
    )
    middle_activation = states + branch_output
    ffn_scale = row_scale(middle_activation)
    ffn_normed = middle_activation * ffn_scale
    ffn_gain_f = ffn_gain.astype(jnp.float32)
    ffn_local = (ffn_normed * ffn_gain_f).astype(jnp.bfloat16)
    ffn_full = lax.all_gather(ffn_local, "tensor", axis=1, tiled=True)
    gate_activation = jnp.dot(ffn_full, gate_weight, preferred_element_type=jnp.float32)
    up_activation = jnp.dot(ffn_full, up_weight, preferred_element_type=jnp.float32)
    gate_sig = jax.nn.sigmoid(gate_activation)
    silu_gate = jax.nn.silu(gate_activation)
    hidden_units = (silu_gate * up_activation).astype(jnp.bfloat16)
    ffn_out = lax.psum_scatter(
        contract_last(hidden_units, down_weight).astype(jnp.bfloat16),
        "tensor",
        scatter_dimension=1,
        tiled=True,
    ).astype(jnp.float32)
    output = ((middle_activation + ffn_out) * live).astype(jnp.bfloat16)
    cot_low = cotangent * live.astype(jnp.bfloat16)
    cot_full = lax.all_gather(cot_low, "tensor", axis=1, tiled=True)
    grad_w_down = contract_rows(cot_full, hidden_units)
    grad_hidden = jnp.dot(cot_full, down_weight, preferred_element_type=jnp.float32)
    grad_gate = (
        grad_hidden * up_activation * gate_sig * (1.0 + gate_activation * (1.0 - gate_sig))
    ).astype(jnp.bfloat16)
    grad_up = (grad_hidden * silu_gate).astype(jnp.bfloat16)
    grad_w_gate = contract_rows(ffn_full, grad_gate)
    grad_w_up = contract_rows(ffn_full, grad_up)
    ffn_part = contract_last(grad_gate, gate_weight) + contract_last(grad_up, up_weight)
    grad_ffn_in = lax.psum_scatter(
        ffn_part.astype(jnp.bfloat16), "tensor", scatter_dimension=1, tiled=True
    ).astype(jnp.float32)
    ffn_gain_part = jnp.sum(grad_ffn_in * ffn_normed, axis=(0, 1))
    grad_middle = cotangent.astype(jnp.float32) * live + norm_back(
        grad_ffn_in, ffn_normed, ffn_scale, ffn_gain_f
    )
    branch_low = grad_middle.astype(jnp.bfloat16)
    branch_full = lax.all_gather(branch_low, "tensor", axis=1, tiled=True)
    grad_w_out = contract_rows(branch_full, head_low)
    grad_head = jnp.dot(branch_full, output_weight, preferred_element_type=jnp.float32)
    proj_low, scalar_grads, taps_grads, gain_grads = mixer_backward(
        a_log[None],
        dt_bias[None],
        grad_head,
        projected,
        scalars,
        inverse,
        block_states,
        mixed,
        fresh,
        conv_w,
        o_gain_f,
    )
    scalar_low = (
        scalar_grads[:, :, :2].transpose(0, 3, 1, 2).reshape(slots, -1, 2 * heads)
    ).astype(jnp.bfloat16)
    grad_conv = jnp.sum(taps_grads[:, :, :CONV], axis=0).transpose(1, 0, 2).reshape(CONV, -1)
    grad_dtb = jnp.sum(scalar_grads[:, :, 1], axis=(0, 2))
    grad_alog = jnp.sum(scalar_grads[:, :, 2], axis=(0, 2))
    o_gain_part = jnp.sum(gain_grads[:, :, 0], axis=(0, 1))
    grad_w_qkvg = contract_rows(mix_full, proj_low)
    grad_w_ba = contract_rows(mix_full, scalar_low)
    mix_part = contract_last(proj_low, query_key_value_gate_weight) + contract_last(
        scalar_low, beta_decay_weight
    )
    grad_mix_in = lax.psum_scatter(
        mix_part.astype(jnp.bfloat16), "tensor", scatter_dimension=1, tiled=True
    ).astype(jnp.float32)
    mix_gain_part = jnp.sum(grad_mix_in * mix_normed, axis=(0, 1))
    tokens_grad = (grad_middle + norm_back(grad_mix_in, mix_normed, mix_scale, mix_gain_f)) * live

    def scatter_sum(part):
        return lax.psum_scatter(
            part.astype(jnp.bfloat16), "dp", scatter_dimension=0, tiled=True
        ).astype(jnp.float32)

    conv_grad, alog_grad, dtb_grad, mix_gain_grad, o_gain_grad, ffn_gain_grad = reduce_small(
        (grad_conv, grad_alog, grad_dtb), (mix_gain_part, o_gain_part, ffn_gain_part)
    )
    return (
        output,
        tokens_grad,
        mix_gain_grad,
        scatter_sum(grad_w_qkvg),
        scatter_sum(grad_w_ba),
        conv_grad,
        alog_grad,
        dtb_grad,
        o_gain_grad,
        scatter_sum(grad_w_out),
        ffn_gain_grad,
        scatter_sum(grad_w_gate),
        scatter_sum(grad_w_up),
        scatter_sum(grad_w_down),
    )


def solution(mesh):
    return jax.shard_map(
        body,
        mesh=mesh,
        in_specs=(
            P("dp", "tensor", None),
            P(),
            P(),
            P(None, "tensor"),
            P(None, "tensor"),
            P(None, "tensor"),
            P("tensor"),
            P("tensor"),
            P(),
            P(None, "tensor"),
            P(),
            P(None, "tensor"),
            P(None, "tensor"),
            P(None, "tensor"),
            P("dp", "tensor", None),
        ),
        out_specs=(
            P("dp", "tensor", None),
            P("dp", "tensor", None),
            P(),
            P("dp", "tensor"),
            P("dp", "tensor"),
            P(None, "tensor"),
            P("tensor"),
            P("tensor"),
            P(),
            P("dp", "tensor"),
            P(),
            P("dp", "tensor"),
            P("dp", "tensor"),
            P("dp", "tensor"),
        ),
        check_vma=False,
    )
```

```python
import jax
import jax.numpy as jnp
from jax import lax
from jax.experimental import pallas as pl
from jax.experimental.pallas import tpu as pltpu
from jax.sharding import PartitionSpec as P

DK = 128
DV = 256
CONV = 4
SPAN = 64
PRE = 2 * DK + DV
HEAD = PRE + DV
TILE = 4 * SPAN
F32 = jnp.float32
BF16 = jnp.bfloat16

EPS_ROW = 1e-06
EPS_HEAD = 1e-05
EPS_UNIT = 1e-06

NN = (((1,), (0,)), ((), ()))
NT = (((1,), (1,)), ((), ()))
TN = (((0,), (0,)), ((), ()))


def mm(left, right, dims=NN):
    return lax.dot_general(
        left.astype(BF16), right.astype(BF16), dims, preferred_element_type=F32
    )


def split(value):
    high = value.astype(BF16)
    return high, (value - high.astype(F32)).astype(BF16)


def mm3(left, right):
    left_high, left_low = left
    right_high, right_low = right
    return (
        mm(left_high, right_high) + mm(left_high, right_low) + mm(left_low, right_high)
    )


def tile_masks():
    row = lax.broadcasted_iota(jnp.int32, (TILE, TILE), 0)
    col = lax.broadcasted_iota(jnp.int32, (TILE, TILE), 1)
    same = (row // SPAN) == (col // SPAN)
    return row, col, same


def shifted(rows, steps):
    length = rows.shape[0]
    if steps == 0:
        return rows
    pos = lax.broadcasted_iota(jnp.int32, rows.shape, 0)
    rolled = pltpu.roll(rows, steps % length, axis=0)
    keep = pos >= steps if steps > 0 else pos < length + steps
    return jnp.where(keep, rolled, 0.0)


def convolve(pre, taps):
    summed = taps[CONV - 1 : CONV] * pre
    for back in range(1, CONV):
        tap = CONV - 1 - back
        summed = summed + taps[tap : tap + 1] * shifted(pre, back)
    return summed


def unit_rows(raw):
    scale = lax.rsqrt(jnp.sum(raw * raw, axis=1, keepdims=True) + EPS_UNIT)
    return raw * scale, scale


def decay_rows(scalars, a_log, dt_bias):
    rate = jnp.exp(jnp.full((1, 1), a_log, F32))
    shifted_in = scalars[1:2] + dt_bias
    soft = jnp.maximum(shifted_in, 0.0) + jnp.log1p(jnp.exp(-jnp.abs(shifted_in)))
    return lax.logistic(scalars[0:1]), -rate * soft, -rate * lax.logistic(shifted_in)


def tile_scalars(row, col, same, beta_row, decay_row):
    lower = same & (row >= col)
    eye = row == col
    cum_col = jnp.sum(jnp.where(lower, decay_row, 0.0), axis=1, keepdims=True)
    beta_col = jnp.sum(jnp.where(eye, beta_row, 0.0), axis=1, keepdims=True)
    cum_row = jnp.sum(jnp.where(eye, cum_col, 0.0), axis=0, keepdims=True)
    last = (row // SPAN) * SPAN + (SPAN - 1)
    last_col = jnp.sum(jnp.where(col == last, cum_row, 0.0), axis=1, keepdims=True)
    decay = jnp.where(lower, jnp.exp(jnp.where(lower, cum_col - cum_row, 0.0)), 0.0)
    return cum_col, beta_col, last_col, decay


def invert(row, col, coupling):
    inverse = None
    size = 1
    while size < SPAN:
        level = (
            ((row // (2 * size)) == (col // (2 * size)))
            & (((row // size) % 2) == 1)
            & (((col // size) % 2) == 0)
        )
        part = jnp.where(level, coupling, 0.0)
        if size == 1:
            inverse = jnp.where(row == col, 1.0, 0.0) - part
        else:
            pieces = split(inverse)
            inner = mm3(split(part), pieces)
            inverse = inverse - mm3(pieces, split(inner))
        size *= 2
    return inverse


def mixer_kernel(
    a_log_ref,
    dt_bias_ref,
    mix_ref,
    weight_ref,
    scalar_weight_ref,
    taps_ref,
    gain_ref,
    head_ref,
    proj_ref,
    scalar_ref,
    inverse_ref,
    state_ref,
    mixed_ref,
    fresh_ref,
):
    head = pl.program_id(1)
    inputs = mix_ref[0]
    projected = mm(inputs, weight_ref[...])
    proj_ref[0] = projected
    scalars = mm(scalar_weight_ref[0], inputs, NT)
    scalar_ref[0, 0] = scalars
    beta_all, decay_all, _ = decay_rows(scalars, a_log_ref[0, head], dt_bias_ref[0, head])
    summed = convolve(projected[:, :PRE], taps_ref[...])
    active = summed * lax.logistic(summed)
    queries = (unit_rows(active[:, :DK])[0] * DK ** (-0.5)).astype(BF16)
    keys = unit_rows(active[:, DK : 2 * DK])[0].astype(BF16)
    vals = active[:, 2 * DK :].astype(BF16)
    row, col, same = tile_masks()
    strict = same & (row > col)
    length = inputs.shape[0]
    state = jnp.zeros((DK, DV), F32)
    for tile in range(length // TILE):
        span = slice(tile * TILE, (tile + 1) * TILE)
        cum_col, beta_col, last_col, decay = tile_scalars(
            row, col, same, beta_all[:, span], decay_all[:, span]
        )
        q = queries[span]
        k = keys[span]
        k_f = k.astype(F32)
        coupling = jnp.where(strict, beta_col * mm(k, k, NT) * decay, 0.0)
        inverse = invert(row, col, coupling)
        inverse_ref[0, 0, tile] = inverse
        grow = jnp.exp(cum_col)
        solved_w = mm(inverse, (beta_col * grow) * k_f)
        solved_u = mm(inverse, beta_col * vals[span].astype(F32))
        scores = mm(q, k, NT) * decay
        grown = q.astype(F32) * grow
        tail = k_f * jnp.exp(last_col - cum_col)
        both = jnp.concatenate([solved_w, solved_u], axis=1).astype(BF16)
        fresh = []
        read = []
        for block in range(TILE // SPAN):
            part = slice(block * SPAN, (block + 1) * SPAN)
            state_ref[0, 0, tile * (TILE // SPAN) + block] = state
            step = mm(tail[part], both[part], TN)
            used = mm(jnp.concatenate([solved_w[part], grown[part]], axis=0), state)
            fresh.append(solved_u[part] - used[:SPAN])
            read.append(used[SPAN:])
            carry = jnp.exp(last_col[block * SPAN : block * SPAN + 1])
            state = carry * state + step[:, DK:] - mm(step[:, :DK], state)
        fresh = jnp.concatenate(fresh, axis=0)
        mixed = jnp.concatenate(read, axis=0) + mm(scores, fresh)
        fresh_ref[0, 0, span] = fresh
        mixed_ref[0, 0, span] = mixed
        scale = lax.rsqrt(jnp.mean(mixed * mixed, axis=1, keepdims=True) + EPS_HEAD)
        gate = projected[span, PRE:]
        head_ref[0, span] = (
            mixed * scale * gain_ref[...] * (gate * lax.logistic(gate))
        ).astype(BF16)


def mixer_forward(a_log, dt_bias, mix, weight, scalar_weight, taps, gain):
    slots, length, width = mix.shape
    heads = weight.shape[1] // HEAD
    blocks = length // SPAN
    tiles = length // TILE
    unit = lambda s, h: (s, h, 0, 0)
    unit5 = lambda s, h: (s, h, 0, 0, 0)
    return pl.pallas_call(
        mixer_kernel,
        name="mixer_forward",
        grid=(slots, heads),
        in_specs=[
            pl.BlockSpec(memory_space=pltpu.SMEM),
            pl.BlockSpec(memory_space=pltpu.SMEM),
            pl.BlockSpec((1, length, width), lambda s, h: (s, 0, 0)),
            pl.BlockSpec((width, HEAD), lambda s, h: (0, h)),
            pl.BlockSpec((1, 8, width), lambda s, h: (h, 0, 0)),
            pl.BlockSpec((CONV, PRE), lambda s, h: (0, h)),
            pl.BlockSpec((1, DV), lambda s, h: (0, 0)),
        ],
        out_specs=[
            pl.BlockSpec((1, length, DV), lambda s, h: (s, 0, h)),
            pl.BlockSpec((1, length, HEAD), lambda s, h: (s, 0, h)),
            pl.BlockSpec((1, 1, 8, length), unit),
            pl.BlockSpec((1, 1, tiles, TILE, TILE), unit5),
            pl.BlockSpec((1, 1, blocks, DK, DV), unit5),
            pl.BlockSpec((1, 1, length, DV), unit),
            pl.BlockSpec((1, 1, length, DV), unit),
        ],
        out_shape=[
            jax.ShapeDtypeStruct((slots, length, heads * DV), BF16),
            jax.ShapeDtypeStruct((slots, length, heads * HEAD), F32),
            jax.ShapeDtypeStruct((slots, heads, 8, length), F32),
            jax.ShapeDtypeStruct((slots, heads, tiles, TILE, TILE), F32),
            jax.ShapeDtypeStruct((slots, heads, blocks, DK, DV), F32),
            jax.ShapeDtypeStruct((slots, heads, length, DV), F32),
            jax.ShapeDtypeStruct((slots, heads, length, DV), F32),
        ],
        cost_estimate=pl.CostEstimate(
            flops=slots * heads * length * 24_000_000,
            transcendentals=slots * heads * length * 2_000,
            bytes_accessed=slots * heads * length * 9_000,
        ),
        compiler_params=pltpu.CompilerParams(
            dimension_semantics=("arbitrary", "arbitrary"), vmem_limit_bytes=56 << 20
        ),
    )(a_log, dt_bias, mix, weight, scalar_weight, taps, gain)


def mixer_back_kernel(
    a_log_ref,
    dt_bias_ref,
    grad_ref,
    proj_ref,
    scalar_ref,
    inverse_ref,
    state_ref,
    mixed_ref,
    fresh_ref,
    taps_ref,
    gain_ref,
    grad_proj_ref,
    grad_scalar_ref,
    grad_taps_ref,
    grad_gain_ref,
):
    head = pl.program_id(1)
    length = grad_ref.shape[1]
    pre = proj_ref[0, :, :PRE]
    taps = taps_ref[...]
    gain = gain_ref[...]
    scalars = scalar_ref[0, 0]
    beta_all, decay_all, slope_all = decay_rows(
        scalars, a_log_ref[0, head], dt_bias_ref[0, head]
    )
    summed = convolve(pre, taps)
    sig = lax.logistic(summed)
    active = summed * sig
    query_unit, query_scale = unit_rows(active[:, :DK])
    key_unit, key_scale = unit_rows(active[:, DK : 2 * DK])
    queries = (query_unit * DK ** (-0.5)).astype(BF16)
    keys = key_unit.astype(BF16)
    vals = active[:, 2 * DK :].astype(BF16)
    row, col, same = tile_masks()
    lower = same & (row >= col)
    strict = same & (row > col)
    eye = row == col
    is_last = (row[:, :1] % SPAN) == (SPAN - 1)
    per = TILE // SPAN
    grad_gain = jnp.zeros((1, DV), F32)
    carried = jnp.zeros((DK, DV), F32)
    grad_active = [None] * (length // TILE)
    grad_beta_rows = [None] * (length // TILE)
    grad_decay_rows = [None] * (length // TILE)
    for tile in reversed(range(length // TILE)):
        span = slice(tile * TILE, (tile + 1) * TILE)
        cum_col, beta_col, last_col, decay = tile_scalars(
            row, col, same, beta_all[:, span], decay_all[:, span]
        )
        gate = proj_ref[0, span, PRE:]
        gate_sig = lax.logistic(gate)
        gate_act = gate * gate_sig
        mixed = mixed_ref[0, 0, span]
        scale = lax.rsqrt(jnp.mean(mixed * mixed, axis=1, keepdims=True) + EPS_HEAD)
        normed = mixed * scale
        grad = grad_ref[0, span]
        grad_normed = grad * normed
        grad_gain = grad_gain + jnp.sum(grad_normed * gate_act, axis=0, keepdims=True)
        grad_proj_ref[0, span, PRE:] = (
            grad_normed * gain * (gate_sig * (1.0 + gate * (1.0 - gate_sig)))
        ).astype(BF16)
        weighted = grad * gain * gate_act
        grad_mixed = scale * (
            weighted - normed * jnp.mean(weighted * normed, axis=1, keepdims=True)
        )
        q = queries[span]
        k = keys[span]
        v = vals[span]
        q_f = q.astype(F32)
        k_f = k.astype(F32)
        v_f = v.astype(F32)
        gram = mm(k, k, NT)
        coupling = jnp.where(strict, beta_col * gram * decay, 0.0)
        scores = mm(q, k, NT) * decay
        inverse = inverse_ref[0, 0, tile].astype(BF16)
        grow = jnp.exp(cum_col)
        fall = jnp.exp(last_col - cum_col)
        beta_grow = beta_col * grow
        key_in = beta_grow * k_f
        solved_w = mm(inverse, key_in)
        solved_u = mm(inverse, beta_col * v_f)
        grown = q_f * grow
        tail = k_f * fall
        fresh = fresh_ref[0, 0, span]
        grad_low = grad_mixed.astype(BF16)
        local = mm(scores, grad_low, TN)
        grad_fresh = [None] * per
        grad_grown = [None] * per
        grad_tail = [None] * per
        grad_w = [None] * per
        carry_terms = [None] * per
        for block in reversed(range(per)):
            part = slice(block * SPAN, (block + 1) * SPAN)
            state = state_ref[0, 0, tile * per + block]
            carry = jnp.exp(last_col[block * SPAN : block * SPAN + 1])
            here = local[part] + mm(tail[part], carried)
            grad_fresh[block] = here
            both = mm(jnp.concatenate([grad_low[part], here.astype(BF16)], axis=0), state, NT)
            grad_grown[block] = both[:SPAN]
            grad_w[block] = -both[SPAN:]
            grad_tail[block] = mm(fresh[part], carried, NT)
            product = jnp.sum(state * carried, axis=0, keepdims=True)
            carry_terms[block] = carry * jnp.sum(product, axis=1, keepdims=True)
            carried = carry * carried + mm(
                jnp.concatenate([grown[part], -solved_w[part]], axis=0),
                jnp.concatenate([grad_low[part], here.astype(BF16)], axis=0),
                TN,
            )
        grad_fresh = jnp.concatenate(grad_fresh, axis=0)
        grad_grown = jnp.concatenate(grad_grown, axis=0)
        grad_tail = jnp.concatenate(grad_tail, axis=0)
        grad_w = jnp.concatenate(grad_w, axis=0)
        grad_key_in = mm(inverse, grad_w, TN)
        grad_val_in = mm(inverse, grad_fresh, TN)
        grad_coupling = jnp.where(
            strict, -(mm(grad_key_in, solved_w, NT) + mm(grad_val_in, solved_u, NT)), 0.0
        )
        grad_scores = mm(grad_low, fresh, NT)
        score_term = grad_scores * decay
        gram_term = grad_coupling * decay
        grad_beta = (
            jnp.sum(gram_term * gram, axis=1, keepdims=True)
            + grow * jnp.sum(grad_key_in * k_f, axis=1, keepdims=True)
            + jnp.sum(grad_val_in * v_f, axis=1, keepdims=True)
        )
        gram_term = gram_term * beta_col
        exponent = grad_coupling * coupling + grad_scores * scores
        tail_sum = jnp.sum(grad_tail * tail, axis=1, keepdims=True)
        grad_cum = (
            jnp.sum(exponent, axis=1, keepdims=True)
            + jnp.sum(grad_grown * grown, axis=1, keepdims=True)
            + jnp.sum(grad_key_in * key_in, axis=1, keepdims=True)
            - tail_sum
        )
        ends = []
        for block in range(per):
            part = slice(block * SPAN, (block + 1) * SPAN)
            total = jnp.sum(tail_sum[part], axis=0, keepdims=True) + carry_terms[block]
            ends.append(jnp.broadcast_to(total, (SPAN, 1)))
        grad_cum = grad_cum + jnp.where(is_last, jnp.concatenate(ends, axis=0), 0.0)
        column_sum = jnp.sum(exponent, axis=0, keepdims=True)
        cum_back = jnp.sum(jnp.where(eye, column_sum, 0.0), axis=1, keepdims=True)
        grad_cum = grad_cum - cum_back
        grad_decay_rows[tile] = jnp.sum(jnp.where(lower, grad_cum, 0.0), axis=0, keepdims=True)
        grad_beta_rows[tile] = jnp.sum(jnp.where(eye, grad_beta, 0.0), axis=0, keepdims=True)
        grad_q = mm(score_term, k) + grad_grown * grow
        grad_k = (
            mm(score_term, q, TN)
            + mm(gram_term, k)
            + mm(gram_term, k, TN)
            + grad_tail * fall
            + beta_grow * grad_key_in
        )
        grad_v = beta_col * grad_val_in
        q_u = query_unit[span]
        k_u = key_unit[span]
        grad_query_raw = (query_scale[span] * DK ** (-0.5)) * (
            grad_q - q_u * jnp.sum(grad_q * q_u, axis=1, keepdims=True)
        )
        grad_key_raw = key_scale[span] * (
            grad_k - k_u * jnp.sum(grad_k * k_u, axis=1, keepdims=True)
        )
        grad_active[tile] = jnp.concatenate([grad_query_raw, grad_key_raw, grad_v], axis=1)
    grad_gain_ref[0, 0] = jnp.broadcast_to(grad_gain, (8, DV))
    grad_summed = jnp.concatenate(grad_active, axis=0) * (sig * (1.0 + summed * (1.0 - sig)))
    grad_pre = taps[CONV - 1 : CONV] * grad_summed
    grad_taps = [None] * CONV
    grad_taps[CONV - 1] = jnp.sum(grad_summed * pre, axis=0, keepdims=True)
    for back in range(1, CONV):
        tap = CONV - 1 - back
        ahead = shifted(grad_summed, -back)
        grad_pre = grad_pre + taps[tap : tap + 1] * ahead
        grad_taps[tap] = jnp.sum(ahead * pre, axis=0, keepdims=True)
    grad_proj_ref[0, :, :PRE] = grad_pre.astype(BF16)
    grad_taps_ref[0, 0] = jnp.concatenate(grad_taps + [jnp.zeros((8 - CONV, PRE), F32)], axis=0)
    grad_beta_all = jnp.concatenate(grad_beta_rows, axis=1)
    grad_decay_all = jnp.concatenate(grad_decay_rows, axis=1)
    grad_scalar_ref[0, 0] = jnp.concatenate(
        [
            grad_beta_all * beta_all * (1.0 - beta_all),
            grad_decay_all * slope_all,
            grad_decay_all * decay_all,
            jnp.zeros((5, length), F32),
        ],
        axis=0,
    )


def mixer_backward(
    a_log, dt_bias, grad_head, projected, scalars, inverse, states, mixed, fresh, taps, gain
):
    slots, length, _ = grad_head.shape
    heads = scalars.shape[1]
    blocks = length // SPAN
    tiles = length // TILE
    unit = lambda s, h: (s, h, 0, 0)
    unit5 = lambda s, h: (s, h, 0, 0, 0)
    return pl.pallas_call(
        mixer_back_kernel,
        name="mixer_backward",
        grid=(slots, heads),
        in_specs=[
            pl.BlockSpec(memory_space=pltpu.SMEM),
            pl.BlockSpec(memory_space=pltpu.SMEM),
            pl.BlockSpec((1, length, DV), lambda s, h: (s, 0, h)),
            pl.BlockSpec((1, length, HEAD), lambda s, h: (s, 0, h)),
            pl.BlockSpec((1, 1, 8, length), unit),
            pl.BlockSpec((1, 1, tiles, TILE, TILE), unit5),
            pl.BlockSpec((1, 1, blocks, DK, DV), unit5),
            pl.BlockSpec((1, 1, length, DV), unit),
            pl.BlockSpec((1, 1, length, DV), unit),
            pl.BlockSpec((CONV, PRE), lambda s, h: (0, h)),
            pl.BlockSpec((1, DV), lambda s, h: (0, 0)),
        ],
        out_specs=[
            pl.BlockSpec((1, length, HEAD), lambda s, h: (s, 0, h)),
            pl.BlockSpec((1, 1, 8, length), unit),
            pl.BlockSpec((1, 1, 8, PRE), unit),
            pl.BlockSpec((1, 1, 8, DV), unit),
        ],
        out_shape=[
            jax.ShapeDtypeStruct((slots, length, heads * HEAD), BF16),
            jax.ShapeDtypeStruct((slots, heads, 8, length), F32),
            jax.ShapeDtypeStruct((slots, heads, 8, PRE), F32),
            jax.ShapeDtypeStruct((slots, heads, 8, DV), F32),
        ],
        cost_estimate=pl.CostEstimate(
            flops=slots * heads * length * 15_000_000,
            transcendentals=slots * heads * length * 2_000,
            bytes_accessed=slots * heads * length * 9_000,
        ),
        compiler_params=pltpu.CompilerParams(
            dimension_semantics=("arbitrary", "arbitrary"), vmem_limit_bytes=56 << 20
        ),
    )(
        a_log,
        dt_bias,
        grad_head,
        projected,
        scalars,
        inverse,
        states,
        mixed,
        fresh,
        taps,
        gain,
    )


def row_scale(values):
    return lax.rsqrt(jnp.mean(values * values, axis=-1, keepdims=True) + EPS_ROW)


def norm_back(grad_out, normed, scale, gain_vec):
    weighted = grad_out * gain_vec
    return scale * (weighted - normed * jnp.mean(weighted * normed, axis=-1, keepdims=True))


def product(left, right):
    return jnp.dot(left, right, preferred_element_type=jnp.float32)


def product_t(left, right):
    return lax.dot_general(left, right, NT, preferred_element_type=jnp.float32)


def rows_sum(lefts, rights):
    total = None
    for left, right in zip(lefts, rights):
        term = lax.dot_general(left, right, TN, preferred_element_type=jnp.float32)
        total = term if total is None else total + term
    return total


def gather_rows(rows):
    if lax.axis_size("tensor") != 2:
        return lax.all_gather(rows, "tensor", axis=0, tiled=True)
    other = lax.ppermute(rows, "tensor", [(0, 1), (1, 0)])
    first = lax.axis_index("tensor") == 0
    return jnp.concatenate(
        [jnp.where(first, rows, other), jnp.where(first, other, rows)], axis=0
    )


def scatter_rows(partial):
    if lax.axis_size("tensor") != 2:
        return lax.psum_scatter(
            partial.astype(jnp.bfloat16), "tensor", scatter_dimension=0, tiled=True
        ).astype(jnp.float32)
    half = partial.shape[0] // 2
    rank = lax.axis_index("tensor")
    sent = lax.dynamic_slice_in_dim(partial, (1 - rank) * half, half).astype(jnp.bfloat16)
    kept = lax.dynamic_slice_in_dim(partial, rank * half, half)
    other = lax.ppermute(sent, "tensor", [(0, 1), (1, 0)])
    return kept + other.astype(jnp.float32)


def pairs(ranks, bit):
    return [(rank, rank ^ bit) for rank in range(ranks)]


def scatter_sum(grads):
    ranks = lax.axis_size("dp")
    rank = lax.axis_index("dp")
    rows, columns = grads.shape
    block = rows // ranks
    held = grads.astype(jnp.bfloat16)
    bit = 1
    while bit < ranks:
        left = ranks // (2 * bit)
        mine = (rank // bit) % 2
        split_rows = held.reshape(left, 2, block, columns)
        sent = lax.dynamic_index_in_dim(split_rows, 1 - mine, 1, keepdims=False)
        kept = lax.dynamic_index_in_dim(split_rows, mine, 1, keepdims=False)
        got = lax.ppermute(sent, "dp", pairs(ranks, bit))
        total = kept.astype(jnp.float32) + got.astype(jnp.float32)
        held = total.astype(jnp.bfloat16) if left > 1 else total
        bit *= 2
    return held.reshape(block, columns)


def sum_all(values, axis):
    ranks = lax.axis_size(axis)
    bit = 1
    while bit < ranks:
        values = values + lax.ppermute(values, axis, pairs(ranks, bit))
        bit *= 2
    return values


def reduce_small(own_parts, shared_parts):
    own = jnp.concatenate([part.reshape(-1) for part in own_parts])
    shared = sum_all(jnp.concatenate([part.reshape(-1) for part in shared_parts]), "tensor")
    total = sum_all(jnp.concatenate([own, shared]), "dp")
    results = []
    at = 0
    for part in own_parts + shared_parts:
        results.append(total[at : at + part.size].reshape(part.shape))
        at += part.size
    return results


def body(
    tokens,
    seq_counts,
    mix_gain,
    query_key_value_gate_weight,
    beta_decay_weight,
    conv_w,
    a_log,
    dt_bias,
    o_gain,
    output_weight,
    ffn_gain,
    gate_weight,
    up_weight,
    down_weight,
    cotangent,
):
    slots = tokens.shape[0]
    heads = a_log.shape[0]
    width = tokens.shape[2]
    every = range(slots)
    group = lax.axis_index("dp")
    count_here = lax.dynamic_index_in_dim(seq_counts, group, keepdims=False)
    mix_gain_f = mix_gain.astype(jnp.float32)
    ffn_gain_f = ffn_gain.astype(jnp.float32)
    o_gain_f = o_gain.astype(jnp.float32)[None]
    scalar_weight = jnp.pad(
        beta_decay_weight.T.reshape(heads, 2, width), ((0, 0), (0, 6), (0, 0))
    )
    live = [(s < count_here).astype(jnp.float32) for s in every]
    states = [tokens[s].astype(jnp.float32) for s in every]
    mix_scale = [row_scale(x) for x in states]
    mix_normed = [x * r for x, r in zip(states, mix_scale)]
    mix_full = [gather_rows((n * mix_gain_f).astype(jnp.bfloat16)) for n in mix_normed]
    grad_out = [cotangent[s].astype(jnp.float32) * live[s] for s in every]
    cot_full = [gather_rows(g.astype(jnp.bfloat16)) for g in grad_out]

    kept = [
        mixer_forward(
            a_log[None],
            dt_bias[None],
            mix_full[s][None],
            query_key_value_gate_weight,
            scalar_weight,
            conv_w,
            o_gain_f,
        )
        for s in every
    ]
    head_low = [k[0][0] for k in kept]
    outputs = []
    hidden, ffn_full, grad_gates, grad_ups, branch_full = [], [], [], [], []
    grad_middle, ffn_gain_part = [], 0.0
    for s in every:
        middle = states[s] + scatter_rows(product_t(head_low[s], output_weight))
        ffn_scale = row_scale(middle)
        ffn_normed = middle * ffn_scale
        full = gather_rows((ffn_normed * ffn_gain_f).astype(jnp.bfloat16))
        gate = product(full, gate_weight)
        up = product(full, up_weight)
        sig = jax.nn.sigmoid(gate)
        act = gate * sig
        units = (act * up).astype(jnp.bfloat16)
        grad_hidden = product(cot_full[s], down_weight)
        grad_gate = (grad_hidden * up * sig * (1.0 + gate * (1.0 - sig))).astype(jnp.bfloat16)
        grad_up = (grad_hidden * act).astype(jnp.bfloat16)
        grad_ffn_in = scatter_rows(
            product_t(grad_gate, gate_weight) + product_t(grad_up, up_weight)
        )
        ffn_gain_part = ffn_gain_part + jnp.sum(grad_ffn_in * ffn_normed, axis=0)
        grad_mid = grad_out[s] + norm_back(grad_ffn_in, ffn_normed, ffn_scale, ffn_gain_f)
        branch_full.append(gather_rows(grad_mid.astype(jnp.bfloat16)))
        ffn_out = scatter_rows(product_t(units, down_weight))
        outputs.append(((middle + ffn_out) * live[s]).astype(jnp.bfloat16))
        hidden.append(units)
        ffn_full.append(full)
        grad_gates.append(grad_gate)
        grad_ups.append(grad_up)
        grad_middle.append(grad_mid)
    sum_down = scatter_sum(rows_sum(cot_full, hidden))
    sum_gate = scatter_sum(rows_sum(ffn_full, grad_gates))
    sum_up = scatter_sum(rows_sum(ffn_full, grad_ups))
    back = [
        mixer_backward(
            a_log[None],
            dt_bias[None],
            product(branch_full[s], output_weight)[None],
            *kept[s][1:],
            conv_w,
            o_gain_f,
        )
        for s in every
    ]
    sum_out = scatter_sum(rows_sum(branch_full, head_low))
    proj_low = [b[0][0] for b in back]
    scalar_grads = sum(b[1] for b in back)
    taps_grads = sum(b[2] for b in back)
    gain_grads = sum(b[3] for b in back)
    scalar_low = [
        b[1][0, :, :2].transpose(2, 0, 1).reshape(-1, 2 * heads).astype(jnp.bfloat16)
        for b in back
    ]
    grad_conv = taps_grads[0, :, :CONV].transpose(1, 0, 2).reshape(CONV, -1)
    grad_dtb = jnp.sum(scalar_grads[0, :, 1], axis=1)
    grad_alog = jnp.sum(scalar_grads[0, :, 2], axis=1)
    o_gain_part = jnp.sum(gain_grads[0, :, 0], axis=0)
    grad_w_ba = rows_sum(mix_full, scalar_low)
    tokens_grad, mix_gain_part = [], 0.0
    for s in every:
        grad_mix_in = scatter_rows(
            product_t(proj_low[s], query_key_value_gate_weight)
            + product_t(scalar_low[s], beta_decay_weight)
        )
        mix_gain_part = mix_gain_part + jnp.sum(grad_mix_in * mix_normed[s], axis=0)
        back_in = norm_back(grad_mix_in, mix_normed[s], mix_scale[s], mix_gain_f)
        tokens_grad.append((grad_middle[s] + back_in) * live[s])
    chunk = HEAD
    sum_qkvg = jnp.concatenate(
        [
            scatter_sum(rows_sum(mix_full, [p[:, at : at + chunk] for p in proj_low]))
            for at in range(0, heads * HEAD, chunk)
        ],
        axis=1,
    )
    conv_grad, alog_grad, dtb_grad, ba_grad, mix_gain_grad, o_gain_grad, ffn_gain_grad = (
        reduce_small(
            (grad_conv, grad_alog, grad_dtb, grad_w_ba),
            (mix_gain_part, o_gain_part, ffn_gain_part),
        )
    )
    block = width // lax.axis_size("dp")
    sum_ba = lax.dynamic_slice_in_dim(ba_grad, group * block, block)
    return (
        jnp.stack(outputs),
        jnp.stack(tokens_grad),
        mix_gain_grad,
        sum_qkvg,
        sum_ba,
        conv_grad,
        alog_grad,
        dtb_grad,
        o_gain_grad,
        sum_out,
        ffn_gain_grad,
        sum_gate,
        sum_up,
        sum_down,
    )


def solution(mesh):
    return jax.shard_map(
        body,
        mesh=mesh,
        in_specs=(
            P("dp", "tensor", None),
            P(),
            P(),
            P(None, "tensor"),
            P(None, "tensor"),
            P(None, "tensor"),
            P("tensor"),
            P("tensor"),
            P(),
            P(None, "tensor"),
            P(),
            P(None, "tensor"),
            P(None, "tensor"),
            P(None, "tensor"),
            P("dp", "tensor", None),
        ),
        out_specs=(
            P("dp", "tensor", None),
            P("dp", "tensor", None),
            P(),
            P("dp", "tensor"),
            P("dp", "tensor"),
            P(None, "tensor"),
            P("tensor"),
            P("tensor"),
            P(),
            P("dp", "tensor"),
            P(),
            P("dp", "tensor"),
            P("dp", "tensor"),
            P("dp", "tensor"),
        ),
        check_vma=False,
    )
```

```python
import jax
import jax.numpy as jnp
from jax import lax
from jax.experimental import pallas as pl
from jax.experimental.pallas import tpu as pltpu
from jax.sharding import PartitionSpec as P

DK = 128
DV = 256
CONV = 4
SPAN = 64
PRE = 2 * DK + DV
HEAD = PRE + DV
TILE = 2 * SPAN
F32 = jnp.float32
BF16 = jnp.bfloat16

EPS_ROW = 1e-06
EPS_HEAD = 1e-05
EPS_UNIT = 1e-06

NN = (((1,), (0,)), ((), ()))
NT = (((1,), (1,)), ((), ()))
TN = (((0,), (0,)), ((), ()))


def mm(left, right, dims=NN):
    return lax.dot_general(
        left.astype(BF16), right.astype(BF16), dims, preferred_element_type=F32
    )


def tile_masks():
    row = lax.broadcasted_iota(jnp.int32, (TILE, TILE), 0)
    col = lax.broadcasted_iota(jnp.int32, (TILE, TILE), 1)
    return row, col, row ^ col


def shifted(rows, steps):
    length = rows.shape[0]
    if steps == 0:
        return rows
    pos = lax.broadcasted_iota(jnp.int32, rows.shape, 0)
    rolled = pltpu.roll(rows, steps % length, axis=0)
    keep = pos >= steps if steps > 0 else pos < length + steps
    return jnp.where(keep, rolled, 0.0)


def convolve(pre, taps):
    summed = taps[CONV - 1 : CONV] * pre
    for back in range(1, CONV):
        tap = CONV - 1 - back
        summed = summed + taps[tap : tap + 1] * shifted(pre, back)
    return summed


def unit_rows(raw):
    scale = lax.rsqrt(jnp.sum(raw * raw, axis=1, keepdims=True) + EPS_UNIT)
    return raw * scale, scale


def decay_rows(scalars, a_log, dt_bias):
    rate = jnp.exp(jnp.full((1, 1), a_log, F32))
    shifted_in = scalars[1:2] + dt_bias
    soft = jnp.maximum(shifted_in, 0.0) + jnp.log1p(jnp.exp(-jnp.abs(shifted_in)))
    return lax.logistic(scalars[0:1]), -rate * soft, -rate * lax.logistic(shifted_in)


def tile_scalars(row, col, apart, beta_row, decay_row):
    lower = (apart < SPAN) & (row >= col)
    eye = apart == 0
    cum_col = jnp.sum(jnp.where(lower, decay_row, 0.0), axis=1, keepdims=True)
    beta_col = jnp.sum(jnp.where(eye, beta_row, 0.0), axis=1, keepdims=True)
    cum_row = jnp.sum(jnp.where(eye, cum_col, 0.0), axis=0, keepdims=True)
    last = row | (SPAN - 1)
    last_col = jnp.sum(jnp.where(col == last, cum_row, 0.0), axis=1, keepdims=True)
    decay = jnp.where(lower, jnp.exp(jnp.where(lower, cum_col - cum_row, 0.0)), 0.0)
    return cum_col, beta_col, last_col, decay


def invert(apart, couplings):
    eye = jnp.where(apart == 0, 1.0, 0.0)
    inverses = [eye - jnp.where(apart == 1, coupling, 0.0) for coupling in couplings]
    size = 2
    while size < SPAN:
        level = (apart >= size) & (apart < 2 * size)
        inner = [
            mm(jnp.where(level, coupling, 0.0), inverse)
            for coupling, inverse in zip(couplings, inverses)
        ]
        inverses = [inverse - mm(inverse, part) for inverse, part in zip(inverses, inner)]
        size *= 2
    return inverses


def mixer_kernel(
    a_log_ref,
    dt_bias_ref,
    mix_ref,
    weight_ref,
    scalar_weight_ref,
    taps_ref,
    gain_ref,
    head_ref,
    proj_ref,
    scalar_ref,
    inverse_ref,
    state_ref,
    mixed_ref,
    fresh_ref,
):
    head = pl.program_id(1)
    inputs = mix_ref[0]
    projected = mm(inputs, weight_ref[...])
    proj_ref[0] = projected
    scalars = mm(scalar_weight_ref[0], inputs, NT)
    scalar_ref[0, 0] = scalars
    beta_all, decay_all, _ = decay_rows(scalars, a_log_ref[0, head], dt_bias_ref[0, head])
    summed = convolve(projected[:, :PRE], taps_ref[...])
    active = summed * lax.logistic(summed)
    queries = (unit_rows(active[:, :DK])[0] * DK ** (-0.5)).astype(BF16)
    keys = unit_rows(active[:, DK : 2 * DK])[0].astype(BF16)
    vals = active[:, 2 * DK :].astype(BF16)
    row, col, apart = tile_masks()
    strict = (apart < SPAN) & (row > col)
    length = inputs.shape[0]
    per = TILE // SPAN
    tiles = range(length // TILE)
    spans = [slice(tile * TILE, (tile + 1) * TILE) for tile in tiles]
    facts = [
        tile_scalars(row, col, apart, beta_all[:, span], decay_all[:, span]) for span in spans
    ]
    couplings = [
        jnp.where(strict, fact[1] * mm(keys[span], keys[span], NT) * fact[3], 0.0)
        for span, fact in zip(spans, facts)
    ]
    inverses = invert(apart, couplings)
    prepared = []
    for tile in tiles:
        span = spans[tile]
        cum_col, beta_col, last_col, decay = facts[tile]
        inverse_ref[0, 0, tile] = inverses[tile]
        k_f = keys[span].astype(F32)
        grow = jnp.exp(cum_col)
        solved_w = mm(inverses[tile], (beta_col * grow) * k_f)
        solved_u = mm(inverses[tile], beta_col * vals[span].astype(F32))
        scores = mm(queries[span], keys[span], NT) * decay
        grown = queries[span].astype(F32) * grow
        tail = k_f * jnp.exp(last_col - cum_col)
        both = jnp.concatenate([solved_w, solved_u], axis=1).astype(BF16)
        steps = [
            mm(tail[block * SPAN : (block + 1) * SPAN], both[block * SPAN : (block + 1) * SPAN], TN)
            for block in range(per)
        ]
        prepared.append((solved_w, solved_u, scores, grown, steps))
    state = jnp.zeros((DK, DV), F32)
    states = []
    for tile in tiles:
        for block in range(per):
            states.append(state.astype(BF16))
            state_ref[0, 0, tile * per + block] = state
            step = prepared[tile][4][block]
            carry = jnp.exp(facts[tile][2][block * SPAN : block * SPAN + 1])
            state = carry * state + step[:, DK:] - mm(step[:, :DK], state)
    for tile in tiles:
        span = spans[tile]
        solved_w, solved_u, scores, grown, _ = prepared[tile]
        fresh = []
        read = []
        for block in range(per):
            part = slice(block * SPAN, (block + 1) * SPAN)
            used = mm(
                jnp.concatenate([solved_w[part], grown[part]], axis=0), states[tile * per + block]
            )
            fresh.append(solved_u[part] - used[:SPAN])
            read.append(used[SPAN:])
        fresh = jnp.concatenate(fresh, axis=0)
        mixed = jnp.concatenate(read, axis=0) + mm(scores, fresh)
        fresh_ref[0, 0, span] = fresh
        mixed_ref[0, 0, span] = mixed
        scale = lax.rsqrt(jnp.mean(mixed * mixed, axis=1, keepdims=True) + EPS_HEAD)
        gate = projected[span, PRE:]
        head_ref[0, span] = (
            mixed * scale * gain_ref[...] * (gate * lax.logistic(gate))
        ).astype(BF16)


def mixer_forward(a_log, dt_bias, mix, weight, scalar_weight, taps, gain):
    slots, length, width = mix.shape
    heads = weight.shape[1] // HEAD
    blocks = length // SPAN
    tiles = length // TILE
    unit = lambda s, h: (s, h, 0, 0)
    unit5 = lambda s, h: (s, h, 0, 0, 0)
    return pl.pallas_call(
        mixer_kernel,
        name="mixer_forward",
        grid=(slots, heads),
        in_specs=[
            pl.BlockSpec(memory_space=pltpu.SMEM),
            pl.BlockSpec(memory_space=pltpu.SMEM),
            pl.BlockSpec((1, length, width), lambda s, h: (s, 0, 0)),
            pl.BlockSpec((width, HEAD), lambda s, h: (0, h)),
            pl.BlockSpec((1, 8, width), lambda s, h: (h, 0, 0)),
            pl.BlockSpec((CONV, PRE), lambda s, h: (0, h)),
            pl.BlockSpec((1, DV), lambda s, h: (0, 0)),
        ],
        out_specs=[
            pl.BlockSpec((1, length, DV), lambda s, h: (s, 0, h)),
            pl.BlockSpec((1, length, HEAD), lambda s, h: (s, 0, h)),
            pl.BlockSpec((1, 1, 8, length), unit),
            pl.BlockSpec((1, 1, tiles, TILE, TILE), unit5),
            pl.BlockSpec((1, 1, blocks, DK, DV), unit5),
            pl.BlockSpec((1, 1, length, DV), unit),
            pl.BlockSpec((1, 1, length, DV), unit),
        ],
        out_shape=[
            jax.ShapeDtypeStruct((slots, length, heads * DV), BF16),
            jax.ShapeDtypeStruct((slots, length, heads * HEAD), F32),
            jax.ShapeDtypeStruct((slots, heads, 8, length), F32),
            jax.ShapeDtypeStruct((slots, heads, tiles, TILE, TILE), F32),
            jax.ShapeDtypeStruct((slots, heads, blocks, DK, DV), F32),
            jax.ShapeDtypeStruct((slots, heads, length, DV), F32),
            jax.ShapeDtypeStruct((slots, heads, length, DV), F32),
        ],
        cost_estimate=pl.CostEstimate(
            flops=slots * heads * length * 24_000_000,
            transcendentals=slots * heads * length * 2_000,
            bytes_accessed=slots * heads * length * 9_000,
        ),
        compiler_params=pltpu.CompilerParams(
            dimension_semantics=("arbitrary", "arbitrary"), vmem_limit_bytes=56 << 20
        ),
    )(a_log, dt_bias, mix, weight, scalar_weight, taps, gain)


def mixer_back_kernel(
    a_log_ref,
    dt_bias_ref,
    grad_ref,
    proj_ref,
    scalar_ref,
    inverse_ref,
    state_ref,
    mixed_ref,
    fresh_ref,
    taps_ref,
    gain_ref,
    grad_proj_ref,
    grad_scalar_ref,
    grad_taps_ref,
    grad_gain_ref,
):
    head = pl.program_id(1)
    length = grad_ref.shape[1]
    pre = proj_ref[0, :, :PRE]
    taps = taps_ref[...]
    gain = gain_ref[...]
    scalars = scalar_ref[0, 0]
    beta_all, decay_all, slope_all = decay_rows(
        scalars, a_log_ref[0, head], dt_bias_ref[0, head]
    )
    summed = convolve(pre, taps)
    sig = lax.logistic(summed)
    active = summed * sig
    query_unit, query_scale = unit_rows(active[:, :DK])
    key_unit, key_scale = unit_rows(active[:, DK : 2 * DK])
    queries = (query_unit * DK ** (-0.5)).astype(BF16)
    keys = key_unit.astype(BF16)
    vals = active[:, 2 * DK :].astype(BF16)
    row, col, apart = tile_masks()
    lower = (apart < SPAN) & (row >= col)
    strict = (apart < SPAN) & (row > col)
    eye = apart == 0
    is_last = (row[:, :1] & (SPAN - 1)) == (SPAN - 1)
    per = TILE // SPAN
    grad_gain = jnp.zeros((1, DV), F32)
    carried = jnp.zeros((DK, DV), F32)
    grad_active = [None] * (length // TILE)
    grad_beta_rows = [None] * (length // TILE)
    grad_decay_rows = [None] * (length // TILE)
    for tile in reversed(range(length // TILE)):
        span = slice(tile * TILE, (tile + 1) * TILE)
        cum_col, beta_col, last_col, decay = tile_scalars(
            row, col, apart, beta_all[:, span], decay_all[:, span]
        )
        gate = proj_ref[0, span, PRE:]
        gate_sig = lax.logistic(gate)
        gate_act = gate * gate_sig
        mixed = mixed_ref[0, 0, span]
        scale = lax.rsqrt(jnp.mean(mixed * mixed, axis=1, keepdims=True) + EPS_HEAD)
        normed = mixed * scale
        grad = grad_ref[0, span]
        grad_normed = grad * normed
        grad_gain = grad_gain + jnp.sum(grad_normed * gate_act, axis=0, keepdims=True)
        grad_proj_ref[0, span, PRE:] = (
            grad_normed * gain * (gate_sig * (1.0 + gate * (1.0 - gate_sig)))
        ).astype(BF16)
        weighted = grad * gain * gate_act
        grad_mixed = scale * (
            weighted - normed * jnp.mean(weighted * normed, axis=1, keepdims=True)
        )
        q = queries[span]
        k = keys[span]
        v = vals[span]
        q_f = q.astype(F32)
        k_f = k.astype(F32)
        v_f = v.astype(F32)
        gram = mm(k, k, NT)
        coupling = jnp.where(strict, beta_col * gram * decay, 0.0)
        scores = mm(q, k, NT) * decay
        inverse = inverse_ref[0, 0, tile].astype(BF16)
        grow = jnp.exp(cum_col)
        fall = jnp.exp(last_col - cum_col)
        beta_grow = beta_col * grow
        key_in = beta_grow * k_f
        solved_w = mm(inverse, key_in)
        solved_u = mm(inverse, beta_col * v_f)
        grown = q_f * grow
        tail = k_f * fall
        fresh = fresh_ref[0, 0, span]
        grad_low = grad_mixed.astype(BF16)
        local = mm(scores, grad_low, TN)
        grad_fresh = [None] * per
        grad_grown = [None] * per
        grad_tail = [None] * per
        grad_w = [None] * per
        carry_terms = [None] * per
        for block in reversed(range(per)):
            part = slice(block * SPAN, (block + 1) * SPAN)
            state = state_ref[0, 0, tile * per + block]
            carry = jnp.exp(last_col[block * SPAN : block * SPAN + 1])
            here = local[part] + mm(tail[part], carried)
            grad_fresh[block] = here
            both = mm(jnp.concatenate([grad_low[part], here.astype(BF16)], axis=0), state, NT)
            grad_grown[block] = both[:SPAN]
            grad_w[block] = -both[SPAN:]
            grad_tail[block] = mm(fresh[part], carried, NT)
            product = jnp.sum(state * carried, axis=0, keepdims=True)
            carry_terms[block] = carry * jnp.sum(product, axis=1, keepdims=True)
            carried = carry * carried + mm(
                jnp.concatenate([grown[part], -solved_w[part]], axis=0),
                jnp.concatenate([grad_low[part], here.astype(BF16)], axis=0),
                TN,
            )
        grad_fresh = jnp.concatenate(grad_fresh, axis=0)
        grad_grown = jnp.concatenate(grad_grown, axis=0)
        grad_tail = jnp.concatenate(grad_tail, axis=0)
        grad_w = jnp.concatenate(grad_w, axis=0)
        grad_key_in = mm(inverse, grad_w, TN)
        grad_val_in = mm(inverse, grad_fresh, TN)
        grad_coupling = jnp.where(
            strict, -(mm(grad_key_in, solved_w, NT) + mm(grad_val_in, solved_u, NT)), 0.0
        )
        grad_scores = mm(grad_low, fresh, NT)
        score_term = grad_scores * decay
        gram_term = grad_coupling * decay
        grad_beta = (
            jnp.sum(gram_term * gram, axis=1, keepdims=True)
            + grow * jnp.sum(grad_key_in * k_f, axis=1, keepdims=True)
            + jnp.sum(grad_val_in * v_f, axis=1, keepdims=True)
        )
        gram_term = gram_term * beta_col
        exponent = grad_coupling * coupling + grad_scores * scores
        tail_sum = jnp.sum(grad_tail * tail, axis=1, keepdims=True)
        grad_cum = (
            jnp.sum(exponent, axis=1, keepdims=True)
            + jnp.sum(grad_grown * grown, axis=1, keepdims=True)
            + jnp.sum(grad_key_in * key_in, axis=1, keepdims=True)
            - tail_sum
        )
        ends = []
        for block in range(per):
            part = slice(block * SPAN, (block + 1) * SPAN)
            total = jnp.sum(tail_sum[part], axis=0, keepdims=True) + carry_terms[block]
            ends.append(jnp.broadcast_to(total, (SPAN, 1)))
        grad_cum = grad_cum + jnp.where(is_last, jnp.concatenate(ends, axis=0), 0.0)
        column_sum = jnp.sum(exponent, axis=0, keepdims=True)
        cum_back = jnp.sum(jnp.where(eye, column_sum, 0.0), axis=1, keepdims=True)
        grad_cum = grad_cum - cum_back
        grad_decay_rows[tile] = jnp.sum(jnp.where(lower, grad_cum, 0.0), axis=0, keepdims=True)
        grad_beta_rows[tile] = jnp.sum(jnp.where(eye, grad_beta, 0.0), axis=0, keepdims=True)
        grad_q = mm(score_term, k) + grad_grown * grow
        grad_k = (
            mm(score_term, q, TN)
            + mm(gram_term, k)
            + mm(gram_term, k, TN)
            + grad_tail * fall
            + beta_grow * grad_key_in
        )
        grad_v = beta_col * grad_val_in
        q_u = query_unit[span]
        k_u = key_unit[span]
        grad_query_raw = (query_scale[span] * DK ** (-0.5)) * (
            grad_q - q_u * jnp.sum(grad_q * q_u, axis=1, keepdims=True)
        )
        grad_key_raw = key_scale[span] * (
            grad_k - k_u * jnp.sum(grad_k * k_u, axis=1, keepdims=True)
        )
        grad_active[tile] = jnp.concatenate([grad_query_raw, grad_key_raw, grad_v], axis=1)
    grad_gain_ref[0, 0] = jnp.broadcast_to(grad_gain, (8, DV))
    grad_summed = jnp.concatenate(grad_active, axis=0) * (sig * (1.0 + summed * (1.0 - sig)))
    grad_pre = taps[CONV - 1 : CONV] * grad_summed
    grad_taps = [None] * CONV
    grad_taps[CONV - 1] = jnp.sum(grad_summed * pre, axis=0, keepdims=True)
    for back in range(1, CONV):
        tap = CONV - 1 - back
        ahead = shifted(grad_summed, -back)
        grad_pre = grad_pre + taps[tap : tap + 1] * ahead
        grad_taps[tap] = jnp.sum(ahead * pre, axis=0, keepdims=True)
    grad_proj_ref[0, :, :PRE] = grad_pre.astype(BF16)
    grad_taps_ref[0, 0] = jnp.concatenate(grad_taps + [jnp.zeros((8 - CONV, PRE), F32)], axis=0)
    grad_beta_all = jnp.concatenate(grad_beta_rows, axis=1)
    grad_decay_all = jnp.concatenate(grad_decay_rows, axis=1)
    grad_scalar_ref[0, 0] = jnp.concatenate(
        [
            grad_beta_all * beta_all * (1.0 - beta_all),
            grad_decay_all * slope_all,
            grad_decay_all * decay_all,
            jnp.zeros((5, length), F32),
        ],
        axis=0,
    )


def mixer_backward(
    a_log, dt_bias, grad_head, projected, scalars, inverse, states, mixed, fresh, taps, gain
):
    slots, length, _ = grad_head.shape
    heads = scalars.shape[1]
    blocks = length // SPAN
    tiles = length // TILE
    unit = lambda s, h: (s, h, 0, 0)
    unit5 = lambda s, h: (s, h, 0, 0, 0)
    return pl.pallas_call(
        mixer_back_kernel,
        name="mixer_backward",
        grid=(slots, heads),
        in_specs=[
            pl.BlockSpec(memory_space=pltpu.SMEM),
            pl.BlockSpec(memory_space=pltpu.SMEM),
            pl.BlockSpec((1, length, DV), lambda s, h: (s, 0, h)),
            pl.BlockSpec((1, length, HEAD), lambda s, h: (s, 0, h)),
            pl.BlockSpec((1, 1, 8, length), unit),
            pl.BlockSpec((1, 1, tiles, TILE, TILE), unit5),
            pl.BlockSpec((1, 1, blocks, DK, DV), unit5),
            pl.BlockSpec((1, 1, length, DV), unit),
            pl.BlockSpec((1, 1, length, DV), unit),
            pl.BlockSpec((CONV, PRE), lambda s, h: (0, h)),
            pl.BlockSpec((1, DV), lambda s, h: (0, 0)),
        ],
        out_specs=[
            pl.BlockSpec((1, length, HEAD), lambda s, h: (s, 0, h)),
            pl.BlockSpec((1, 1, 8, length), unit),
            pl.BlockSpec((1, 1, 8, PRE), unit),
            pl.BlockSpec((1, 1, 8, DV), unit),
        ],
        out_shape=[
            jax.ShapeDtypeStruct((slots, length, heads * HEAD), BF16),
            jax.ShapeDtypeStruct((slots, heads, 8, length), F32),
            jax.ShapeDtypeStruct((slots, heads, 8, PRE), F32),
            jax.ShapeDtypeStruct((slots, heads, 8, DV), F32),
        ],
        cost_estimate=pl.CostEstimate(
            flops=slots * heads * length * 15_000_000,
            transcendentals=slots * heads * length * 2_000,
            bytes_accessed=slots * heads * length * 9_000,
        ),
        compiler_params=pltpu.CompilerParams(
            dimension_semantics=("arbitrary", "arbitrary"), vmem_limit_bytes=56 << 20
        ),
    )(
        a_log,
        dt_bias,
        grad_head,
        projected,
        scalars,
        inverse,
        states,
        mixed,
        fresh,
        taps,
        gain,
    )


def row_scale(values):
    return lax.rsqrt(jnp.mean(values * values, axis=-1, keepdims=True) + EPS_ROW)


def norm_back(grad_out, normed, scale, gain_vec):
    weighted = grad_out * gain_vec
    return scale * (weighted - normed * jnp.mean(weighted * normed, axis=-1, keepdims=True))


def product(left, right):
    return jnp.dot(left, right, preferred_element_type=jnp.float32)


def product_t(left, right):
    return lax.dot_general(left, right, NT, preferred_element_type=jnp.float32)


def rows_sum(lefts, rights):
    total = None
    for left, right in zip(lefts, rights):
        term = lax.dot_general(left, right, TN, preferred_element_type=jnp.float32)
        total = term if total is None else total + term
    return total


def after(value, *others):
    return lax.optimization_barrier((value, *others))[0]


def gather_rows(rows):
    if lax.axis_size("tensor") != 2:
        return lax.all_gather(rows, "tensor", axis=0, tiled=True)
    other = lax.ppermute(rows, "tensor", [(0, 1), (1, 0)])
    first = lax.axis_index("tensor") == 0
    return jnp.concatenate(
        [jnp.where(first, rows, other), jnp.where(first, other, rows)], axis=0
    )


def scatter_rows(partial):
    if lax.axis_size("tensor") != 2:
        return lax.psum_scatter(
            partial.astype(jnp.bfloat16), "tensor", scatter_dimension=0, tiled=True
        ).astype(jnp.float32)
    half = partial.shape[0] // 2
    rank = lax.axis_index("tensor")
    sent = lax.dynamic_slice_in_dim(partial, (1 - rank) * half, half).astype(jnp.bfloat16)
    kept = lax.dynamic_slice_in_dim(partial, rank * half, half)
    other = lax.ppermute(sent, "tensor", [(0, 1), (1, 0)])
    return kept + other.astype(jnp.float32)


def pairs(ranks, bit):
    return [(rank, rank ^ bit) for rank in range(ranks)]


def halve(held, bit):
    ranks = lax.axis_size("dp")
    left = ranks // (2 * bit)
    mine = (lax.axis_index("dp") // bit) % 2
    sends, keeps = [], []
    for grads in held:
        rows = grads.reshape(left, 2, -1, grads.shape[-1])
        sends.append(lax.dynamic_index_in_dim(rows, 1 - mine, 1, keepdims=False))
        keeps.append(lax.dynamic_index_in_dim(rows, mine, 1, keepdims=False))
    join = lambda parts: parts[0] if len(parts) == 1 else jnp.concatenate(parts, axis=-1)
    return join(sends).astype(jnp.bfloat16), join(keeps)


def swap_add(sent, kept, bit):
    ranks = lax.axis_size("dp")
    got = lax.ppermute(sent, "dp", pairs(ranks, bit))
    total = kept.astype(jnp.float32) + got.astype(jnp.float32)
    return total if 2 * bit == ranks else total.astype(jnp.bfloat16)


def sum_begin(held, steps):
    bit = 1
    for _ in range(steps):
        sent, kept = halve(held, bit)
        held = [swap_add(sent, kept, bit)]
        bit *= 2
    return halve(held, bit) + (bit,)


def sum_end(state):
    sent, kept, bit = state
    held = swap_add(sent, kept, bit)
    while 2 * bit < lax.axis_size("dp"):
        bit *= 2
        held = swap_add(*halve([held], bit), bit)
    return held.reshape(-1, held.shape[-1])


def sum_all(values, axis):
    ranks = lax.axis_size(axis)
    bit = 1
    while bit < ranks:
        values = values + lax.ppermute(values, axis, pairs(ranks, bit))
        bit *= 2
    return values


def reduce_small(own_parts, shared_parts):
    own = jnp.concatenate([part.reshape(-1) for part in own_parts])
    shared = sum_all(jnp.concatenate([part.reshape(-1) for part in shared_parts]), "tensor")
    total = sum_all(jnp.concatenate([own, shared]), "dp")
    results = []
    at = 0
    for part in own_parts + shared_parts:
        results.append(total[at : at + part.size].reshape(part.shape))
        at += part.size
    return results


def body(
    tokens,
    seq_counts,
    mix_gain,
    query_key_value_gate_weight,
    beta_decay_weight,
    conv_w,
    a_log,
    dt_bias,
    o_gain,
    output_weight,
    ffn_gain,
    gate_weight,
    up_weight,
    down_weight,
    cotangent,
):
    slots = tokens.shape[0]
    heads = a_log.shape[0]
    width = tokens.shape[2]
    every = range(slots)
    group = lax.axis_index("dp")
    count_here = lax.dynamic_index_in_dim(seq_counts, group, keepdims=False)
    mix_gain_f = mix_gain.astype(jnp.float32)
    ffn_gain_f = ffn_gain.astype(jnp.float32)
    o_gain_f = o_gain.astype(jnp.float32)[None]
    scalar_weight = jnp.pad(
        beta_decay_weight.T.reshape(heads, 2, width), ((0, 0), (0, 6), (0, 0))
    )
    live = [(s < count_here).astype(jnp.float32) for s in every]
    states = [tokens[s].astype(jnp.float32) for s in every]
    mix_scale = [row_scale(x) for x in states]
    mix_normed = [x * r for x, r in zip(states, mix_scale)]
    grad_out = [cotangent[s].astype(jnp.float32) * live[s] for s in every]
    mix_full, cot_full = [], []
    for s in every:
        rows = (mix_normed[s] * mix_gain_f).astype(jnp.bfloat16)
        mix_full.append(gather_rows(after(rows, *mix_full)))
    for s in every:
        rows = grad_out[s].astype(jnp.bfloat16)
        cot_full.append(gather_rows(after(rows, *mix_full)))

    kept = [
        mixer_forward(
            a_log[None],
            dt_bias[None],
            mix_full[s][None],
            query_key_value_gate_weight,
            scalar_weight,
            conv_w,
            o_gain_f,
        )
        for s in every
    ]
    head_low = [k[0][0] for k in kept]
    outputs = []
    hidden, ffn_full, grad_gates, grad_ups, branch_full = [], [], [], [], []
    grad_middle, ffn_gain_part = [], 0.0
    for s in every:
        middle = states[s] + scatter_rows(product_t(head_low[s], output_weight))
        ffn_scale = row_scale(middle)
        ffn_normed = middle * ffn_scale
        full = gather_rows((ffn_normed * ffn_gain_f).astype(jnp.bfloat16))
        gate = product(full, gate_weight)
        up = product(full, up_weight)
        sig = jax.nn.sigmoid(gate)
        act = gate * sig
        units = (act * up).astype(jnp.bfloat16)
        grad_hidden = product(cot_full[s], down_weight)
        grad_gate = (grad_hidden * up * sig * (1.0 + gate * (1.0 - sig))).astype(jnp.bfloat16)
        grad_up = (grad_hidden * act).astype(jnp.bfloat16)
        grad_ffn_in = scatter_rows(
            product_t(grad_gate, gate_weight) + product_t(grad_up, up_weight)
        )
        ffn_gain_part = ffn_gain_part + jnp.sum(grad_ffn_in * ffn_normed, axis=0)
        grad_mid = grad_out[s] + norm_back(grad_ffn_in, ffn_normed, ffn_scale, ffn_gain_f)
        branch_full.append(gather_rows(grad_mid.astype(jnp.bfloat16)))
        ffn_out = scatter_rows(product_t(units, down_weight))
        outputs.append(((middle + ffn_out) * live[s]).astype(jnp.bfloat16))
        hidden.append(units)
        ffn_full.append(full)
        grad_gates.append(grad_gate)
        grad_ups.append(grad_up)
        grad_middle.append(grad_mid)
    down_state = sum_begin([rows_sum(cot_full, hidden).astype(jnp.bfloat16)], 1)
    pair_state = sum_begin(
        [
            rows_sum(ffn_full, grad_gates).astype(jnp.bfloat16),
            rows_sum(ffn_full, grad_ups).astype(jnp.bfloat16),
        ],
        1,
    )
    out_state = sum_begin([rows_sum(branch_full, head_low).astype(jnp.bfloat16)], 0)
    back = []
    for s in every:
        grad_head = product(branch_full[s], output_weight)
        if s == slots - 1:
            grad_head = after(grad_head, down_state[0], pair_state[0], out_state[0])
        back.append(
            mixer_backward(
                a_log[None],
                dt_bias[None],
                grad_head[None],
                *kept[s][1:],
                conv_w,
                o_gain_f,
            )
        )
    sum_down = sum_end(down_state)
    sum_pair = sum_end(pair_state)
    sum_gate, sum_up = jnp.split(sum_pair, 2, axis=1)
    sum_out = sum_end(out_state)
    proj_low = [b[0][0] for b in back]
    scalar_grads = sum(b[1] for b in back)
    taps_grads = sum(b[2] for b in back)
    gain_grads = sum(b[3] for b in back)
    scalar_low = [
        b[1][0, :, :2].transpose(2, 0, 1).reshape(-1, 2 * heads).astype(jnp.bfloat16)
        for b in back
    ]
    grad_conv = taps_grads[0, :, :CONV].transpose(1, 0, 2).reshape(CONV, -1)
    grad_dtb = jnp.sum(scalar_grads[0, :, 1], axis=1)
    grad_alog = jnp.sum(scalar_grads[0, :, 2], axis=1)
    o_gain_part = jnp.sum(gain_grads[0, :, 0], axis=0)
    grad_w_ba = rows_sum(mix_full, scalar_low)
    tokens_grad, mix_gain_part = [], 0.0
    for s in every:
        grad_mix_in = scatter_rows(
            product_t(proj_low[s], query_key_value_gate_weight)
            + product_t(scalar_low[s], beta_decay_weight)
        )
        mix_gain_part = mix_gain_part + jnp.sum(grad_mix_in * mix_normed[s], axis=0)
        back_in = norm_back(grad_mix_in, mix_normed[s], mix_scale[s], mix_gain_f)
        tokens_grad.append((grad_middle[s] + back_in) * live[s])
    chunk = heads * HEAD // 2
    sum_qkvg = jnp.concatenate(
        [
            sum_end(
                sum_begin(
                    [rows_sum(mix_full, [p[:, at : at + chunk] for p in proj_low])], 0
                )
            )
            for at in range(0, heads * HEAD, chunk)
        ],
        axis=1,
    )
    conv_grad, alog_grad, dtb_grad, ba_grad, mix_gain_grad, o_gain_grad, ffn_gain_grad = (
        reduce_small(
            (grad_conv, grad_alog, grad_dtb, grad_w_ba),
            (mix_gain_part, o_gain_part, ffn_gain_part),
        )
    )
    block = width // lax.axis_size("dp")
    sum_ba = lax.dynamic_slice_in_dim(ba_grad, group * block, block)
    return (
        jnp.stack(outputs),
        jnp.stack(tokens_grad),
        mix_gain_grad,
        sum_qkvg,
        sum_ba,
        conv_grad,
        alog_grad,
        dtb_grad,
        o_gain_grad,
        sum_out,
        ffn_gain_grad,
        sum_gate,
        sum_up,
        sum_down,
    )


def solution(mesh):
    return jax.shard_map(
        body,
        mesh=mesh,
        in_specs=(
            P("dp", "tensor", None),
            P(),
            P(),
            P(None, "tensor"),
            P(None, "tensor"),
            P(None, "tensor"),
            P("tensor"),
            P("tensor"),
            P(),
            P(None, "tensor"),
            P(),
            P(None, "tensor"),
            P(None, "tensor"),
            P(None, "tensor"),
            P("dp", "tensor", None),
        ),
        out_specs=(
            P("dp", "tensor", None),
            P("dp", "tensor", None),
            P(),
            P("dp", "tensor"),
            P("dp", "tensor"),
            P(None, "tensor"),
            P("tensor"),
            P("tensor"),
            P(),
            P("dp", "tensor"),
            P(),
            P("dp", "tensor"),
            P("dp", "tensor"),
            P("dp", "tensor"),
        ),
        check_vma=False,
    )
```

```python
import jax
import jax.numpy as jnp
from jax import lax
from jax.experimental import pallas as pl
from jax.experimental.pallas import tpu as pltpu
from jax.sharding import PartitionSpec as P

DK = 128
DV = 256
CONV = 4
SPAN = 64
PRE = 2 * DK + DV
HEAD = PRE + DV
TILE = 2 * SPAN
F32 = jnp.float32
BF16 = jnp.bfloat16

EPS_ROW = 1e-06
EPS_HEAD = 1e-05
EPS_UNIT = 1e-06

NN = (((1,), (0,)), ((), ()))
NT = (((1,), (1,)), ((), ()))
TN = (((0,), (0,)), ((), ()))


def mm(left, right, dims=NN):
    return lax.dot_general(
        left.astype(BF16), right.astype(BF16), dims, preferred_element_type=F32
    )


def tile_masks():
    row = lax.broadcasted_iota(jnp.int32, (TILE, TILE), 0)
    col = lax.broadcasted_iota(jnp.int32, (TILE, TILE), 1)
    return row, col, row ^ col


def shifted(rows, steps):
    length = rows.shape[0]
    if steps == 0:
        return rows
    pos = lax.broadcasted_iota(jnp.int32, rows.shape, 0)
    rolled = pltpu.roll(rows, steps % length, axis=0)
    keep = pos >= steps if steps > 0 else pos < length + steps
    return jnp.where(keep, rolled, 0.0)


def convolve(pre, taps):
    summed = taps[CONV - 1 : CONV] * pre
    for back in range(1, CONV):
        tap = CONV - 1 - back
        summed = summed + taps[tap : tap + 1] * shifted(pre, back)
    return summed


def unit_rows(raw):
    scale = lax.rsqrt(jnp.sum(raw * raw, axis=1, keepdims=True) + EPS_UNIT)
    return raw * scale, scale


def decay_rows(scalars, a_log, dt_bias):
    rate = jnp.exp(jnp.full((1, 1), a_log, F32))
    shifted_in = scalars[1:2] + dt_bias
    soft = jnp.maximum(shifted_in, 0.0) + jnp.log1p(jnp.exp(-jnp.abs(shifted_in)))
    return lax.logistic(scalars[0:1]), -rate * soft, -rate * lax.logistic(shifted_in)


def tile_scalars(row, col, apart, beta_row, decay_row):
    lower = (apart < SPAN) & (row >= col)
    eye = apart == 0
    cum_col = jnp.sum(jnp.where(lower, decay_row, 0.0), axis=1, keepdims=True)
    beta_col = jnp.sum(jnp.where(eye, beta_row, 0.0), axis=1, keepdims=True)
    cum_row = jnp.sum(jnp.where(eye, cum_col, 0.0), axis=0, keepdims=True)
    last = row | (SPAN - 1)
    last_col = jnp.sum(jnp.where(col == last, cum_row, 0.0), axis=1, keepdims=True)
    decay = jnp.where(lower, jnp.exp(jnp.where(lower, cum_col - cum_row, 0.0)), 0.0)
    return cum_col, beta_col, last_col, decay


def invert(apart, couplings):
    eye = jnp.where(apart == 0, 1.0, 0.0)
    inverses = [eye - jnp.where(apart == 1, coupling, 0.0) for coupling in couplings]
    size = 2
    while size < SPAN:
        level = (apart >= size) & (apart < 2 * size)
        inner = [
            mm(jnp.where(level, coupling, 0.0), inverse)
            for coupling, inverse in zip(couplings, inverses)
        ]
        inverses = [inverse - mm(inverse, part) for inverse, part in zip(inverses, inner)]
        size *= 2
    return inverses


def mixer_kernel(
    a_log_ref,
    dt_bias_ref,
    mix_ref,
    weight_ref,
    scalar_weight_ref,
    taps_ref,
    gain_ref,
    head_ref,
    proj_ref,
    scalar_ref,
    inverse_ref,
    state_ref,
    mixed_ref,
    fresh_ref,
):
    head = pl.program_id(1)
    inputs = mix_ref[0]
    projected = mm(inputs, weight_ref[...])
    proj_ref[0] = projected
    scalars = mm(scalar_weight_ref[0], inputs, NT)
    scalar_ref[0, 0] = scalars
    beta_all, decay_all, _ = decay_rows(scalars, a_log_ref[0, head], dt_bias_ref[0, head])
    summed = convolve(projected[:, :PRE], taps_ref[...])
    active = summed * lax.logistic(summed)
    queries = (unit_rows(active[:, :DK])[0] * DK ** (-0.5)).astype(BF16)
    keys = unit_rows(active[:, DK : 2 * DK])[0].astype(BF16)
    vals = active[:, 2 * DK :].astype(BF16)
    row, col, apart = tile_masks()
    strict = (apart < SPAN) & (row > col)
    length = inputs.shape[0]
    per = TILE // SPAN
    tiles = range(length // TILE)
    spans = [slice(tile * TILE, (tile + 1) * TILE) for tile in tiles]
    facts = [
        tile_scalars(row, col, apart, beta_all[:, span], decay_all[:, span]) for span in spans
    ]
    couplings = [
        jnp.where(strict, fact[1] * mm(keys[span], keys[span], NT) * fact[3], 0.0)
        for span, fact in zip(spans, facts)
    ]
    inverses = invert(apart, couplings)
    prepared = []
    for tile in tiles:
        span = spans[tile]
        cum_col, beta_col, last_col, decay = facts[tile]
        inverse_ref[0, 0, tile] = inverses[tile]
        k_f = keys[span].astype(F32)
        grow = jnp.exp(cum_col)
        solved_w = mm(inverses[tile], (beta_col * grow) * k_f)
        solved_u = mm(inverses[tile], beta_col * vals[span].astype(F32))
        scores = mm(queries[span], keys[span], NT) * decay
        grown = queries[span].astype(F32) * grow
        tail = k_f * jnp.exp(last_col - cum_col)
        both = jnp.concatenate([solved_w, solved_u], axis=1).astype(BF16)
        steps = [
            mm(tail[block * SPAN : (block + 1) * SPAN], both[block * SPAN : (block + 1) * SPAN], TN)
            for block in range(per)
        ]
        prepared.append((solved_w, solved_u, scores, grown, steps))
    state = jnp.zeros((DK, DV), F32)
    states = []
    for tile in tiles:
        for block in range(per):
            states.append(state.astype(BF16))
            state_ref[0, 0, tile * per + block] = state
            step = prepared[tile][4][block]
            carry = jnp.exp(facts[tile][2][block * SPAN : block * SPAN + 1])
            state = carry * state + step[:, DK:] - mm(step[:, :DK], state)
    for tile in tiles:
        span = spans[tile]
        solved_w, solved_u, scores, grown, _ = prepared[tile]
        fresh = []
        read = []
        for block in range(per):
            part = slice(block * SPAN, (block + 1) * SPAN)
            used = mm(
                jnp.concatenate([solved_w[part], grown[part]], axis=0), states[tile * per + block]
            )
            fresh.append(solved_u[part] - used[:SPAN])
            read.append(used[SPAN:])
        fresh = jnp.concatenate(fresh, axis=0)
        mixed = jnp.concatenate(read, axis=0) + mm(scores, fresh)
        fresh_ref[0, 0, span] = fresh
        mixed_ref[0, 0, span] = mixed
        scale = lax.rsqrt(jnp.mean(mixed * mixed, axis=1, keepdims=True) + EPS_HEAD)
        gate = projected[span, PRE:]
        head_ref[0, span] = (
            mixed * scale * gain_ref[...] * (gate * lax.logistic(gate))
        ).astype(BF16)


def mixer_forward(a_log, dt_bias, mix, weight, scalar_weight, taps, gain):
    slots, length, width = mix.shape
    heads = weight.shape[1] // HEAD
    blocks = length // SPAN
    tiles = length // TILE
    unit = lambda s, h: (s, h, 0, 0)
    unit5 = lambda s, h: (s, h, 0, 0, 0)
    return pl.pallas_call(
        mixer_kernel,
        name="mixer_forward",
        grid=(slots, heads),
        in_specs=[
            pl.BlockSpec(memory_space=pltpu.SMEM),
            pl.BlockSpec(memory_space=pltpu.SMEM),
            pl.BlockSpec((1, length, width), lambda s, h: (s, 0, 0)),
            pl.BlockSpec((width, HEAD), lambda s, h: (0, h)),
            pl.BlockSpec((1, 8, width), lambda s, h: (h, 0, 0)),
            pl.BlockSpec((CONV, PRE), lambda s, h: (0, h)),
            pl.BlockSpec((1, DV), lambda s, h: (0, 0)),
        ],
        out_specs=[
            pl.BlockSpec((1, length, DV), lambda s, h: (s, 0, h)),
            pl.BlockSpec((1, length, HEAD), lambda s, h: (s, 0, h)),
            pl.BlockSpec((1, 1, 8, length), unit),
            pl.BlockSpec((1, 1, tiles, TILE, TILE), unit5),
            pl.BlockSpec((1, 1, blocks, DK, DV), unit5),
            pl.BlockSpec((1, 1, length, DV), unit),
            pl.BlockSpec((1, 1, length, DV), unit),
        ],
        out_shape=[
            jax.ShapeDtypeStruct((slots, length, heads * DV), BF16),
            jax.ShapeDtypeStruct((slots, length, heads * HEAD), F32),
            jax.ShapeDtypeStruct((slots, heads, 8, length), F32),
            jax.ShapeDtypeStruct((slots, heads, tiles, TILE, TILE), F32),
            jax.ShapeDtypeStruct((slots, heads, blocks, DK, DV), F32),
            jax.ShapeDtypeStruct((slots, heads, length, DV), F32),
            jax.ShapeDtypeStruct((slots, heads, length, DV), F32),
        ],
        cost_estimate=pl.CostEstimate(
            flops=slots * heads * length * 24_000_000,
            transcendentals=slots * heads * length * 2_000,
            bytes_accessed=slots * heads * length * 9_000,
        ),
        compiler_params=pltpu.CompilerParams(
            dimension_semantics=("arbitrary", "arbitrary"), vmem_limit_bytes=56 << 20
        ),
    )(a_log, dt_bias, mix, weight, scalar_weight, taps, gain)


def mixer_back_kernel(
    a_log_ref,
    dt_bias_ref,
    grad_ref,
    proj_ref,
    scalar_ref,
    inverse_ref,
    state_ref,
    mixed_ref,
    fresh_ref,
    taps_ref,
    gain_ref,
    grad_proj_ref,
    grad_scalar_ref,
    grad_taps_ref,
    grad_gain_ref,
):
    head = pl.program_id(1)
    length = grad_ref.shape[1]
    pre = proj_ref[0, :, :PRE]
    taps = taps_ref[...]
    gain = gain_ref[...]
    scalars = scalar_ref[0, 0]
    beta_all, decay_all, slope_all = decay_rows(
        scalars, a_log_ref[0, head], dt_bias_ref[0, head]
    )
    summed = convolve(pre, taps)
    sig = lax.logistic(summed)
    active = summed * sig
    query_unit, query_scale = unit_rows(active[:, :DK])
    key_unit, key_scale = unit_rows(active[:, DK : 2 * DK])
    queries = (query_unit * DK ** (-0.5)).astype(BF16)
    keys = key_unit.astype(BF16)
    vals = active[:, 2 * DK :].astype(BF16)
    row, col, apart = tile_masks()
    lower = (apart < SPAN) & (row >= col)
    strict = (apart < SPAN) & (row > col)
    eye = apart == 0
    is_last = (row[:, :1] & (SPAN - 1)) == (SPAN - 1)
    per = TILE // SPAN
    grad_gain = jnp.zeros((1, DV), F32)
    carried = jnp.zeros((DK, DV), F32)
    grad_active = [None] * (length // TILE)
    grad_beta_rows = [None] * (length // TILE)
    grad_decay_rows = [None] * (length // TILE)
    for tile in reversed(range(length // TILE)):
        span = slice(tile * TILE, (tile + 1) * TILE)
        cum_col, beta_col, last_col, decay = tile_scalars(
            row, col, apart, beta_all[:, span], decay_all[:, span]
        )
        gate = proj_ref[0, span, PRE:]
        gate_sig = lax.logistic(gate)
        gate_act = gate * gate_sig
        mixed = mixed_ref[0, 0, span]
        scale = lax.rsqrt(jnp.mean(mixed * mixed, axis=1, keepdims=True) + EPS_HEAD)
        normed = mixed * scale
        grad = grad_ref[0, span]
        grad_normed = grad * normed
        grad_gain = grad_gain + jnp.sum(grad_normed * gate_act, axis=0, keepdims=True)
        grad_proj_ref[0, span, PRE:] = (
            grad_normed * gain * (gate_sig * (1.0 + gate * (1.0 - gate_sig)))
        ).astype(BF16)
        weighted = grad * gain * gate_act
        grad_mixed = scale * (
            weighted - normed * jnp.mean(weighted * normed, axis=1, keepdims=True)
        )
        q = queries[span]
        k = keys[span]
        v = vals[span]
        q_f = q.astype(F32)
        k_f = k.astype(F32)
        v_f = v.astype(F32)
        gram = mm(k, k, NT)
        coupling = jnp.where(strict, beta_col * gram * decay, 0.0)
        scores = mm(q, k, NT) * decay
        inverse = inverse_ref[0, 0, tile].astype(BF16)
        grow = jnp.exp(cum_col)
        fall = jnp.exp(last_col - cum_col)
        beta_grow = beta_col * grow
        key_in = beta_grow * k_f
        solved_w = mm(inverse, key_in)
        solved_u = mm(inverse, beta_col * v_f)
        grown = q_f * grow
        tail = k_f * fall
        fresh = fresh_ref[0, 0, span]
        grad_low = grad_mixed.astype(BF16)
        local = mm(scores, grad_low, TN)
        grad_fresh = [None] * per
        grad_grown = [None] * per
        grad_tail = [None] * per
        grad_w = [None] * per
        carry_terms = [None] * per
        for block in reversed(range(per)):
            part = slice(block * SPAN, (block + 1) * SPAN)
            state = state_ref[0, 0, tile * per + block]
            carry = jnp.exp(last_col[block * SPAN : block * SPAN + 1])
            here = local[part] + mm(tail[part], carried)
            grad_fresh[block] = here
            both = mm(jnp.concatenate([grad_low[part], here.astype(BF16)], axis=0), state, NT)
            grad_grown[block] = both[:SPAN]
            grad_w[block] = -both[SPAN:]
            grad_tail[block] = mm(fresh[part], carried, NT)
            product = jnp.sum(state * carried, axis=0, keepdims=True)
            carry_terms[block] = carry * jnp.sum(product, axis=1, keepdims=True)
            carried = carry * carried + mm(
                jnp.concatenate([grown[part], -solved_w[part]], axis=0),
                jnp.concatenate([grad_low[part], here.astype(BF16)], axis=0),
                TN,
            )
        grad_fresh = jnp.concatenate(grad_fresh, axis=0)
        grad_grown = jnp.concatenate(grad_grown, axis=0)
        grad_tail = jnp.concatenate(grad_tail, axis=0)
        grad_w = jnp.concatenate(grad_w, axis=0)
        grad_key_in = mm(inverse, grad_w, TN)
        grad_val_in = mm(inverse, grad_fresh, TN)
        grad_coupling = jnp.where(
            strict, -(mm(grad_key_in, solved_w, NT) + mm(grad_val_in, solved_u, NT)), 0.0
        )
        grad_scores = mm(grad_low, fresh, NT)
        score_term = grad_scores * decay
        gram_term = grad_coupling * decay
        grad_beta = (
            jnp.sum(gram_term * gram, axis=1, keepdims=True)
            + grow * jnp.sum(grad_key_in * k_f, axis=1, keepdims=True)
            + jnp.sum(grad_val_in * v_f, axis=1, keepdims=True)
        )
        gram_term = gram_term * beta_col
        exponent = grad_coupling * coupling + grad_scores * scores
        tail_sum = jnp.sum(grad_tail * tail, axis=1, keepdims=True)
        grad_cum = (
            jnp.sum(exponent, axis=1, keepdims=True)
            + jnp.sum(grad_grown * grown, axis=1, keepdims=True)
            + jnp.sum(grad_key_in * key_in, axis=1, keepdims=True)
            - tail_sum
        )
        ends = []
        for block in range(per):
            part = slice(block * SPAN, (block + 1) * SPAN)
            total = jnp.sum(tail_sum[part], axis=0, keepdims=True) + carry_terms[block]
            ends.append(jnp.broadcast_to(total, (SPAN, 1)))
        grad_cum = grad_cum + jnp.where(is_last, jnp.concatenate(ends, axis=0), 0.0)
        column_sum = jnp.sum(exponent, axis=0, keepdims=True)
        cum_back = jnp.sum(jnp.where(eye, column_sum, 0.0), axis=1, keepdims=True)
        grad_cum = grad_cum - cum_back
        grad_decay_rows[tile] = jnp.sum(jnp.where(lower, grad_cum, 0.0), axis=0, keepdims=True)
        grad_beta_rows[tile] = jnp.sum(jnp.where(eye, grad_beta, 0.0), axis=0, keepdims=True)
        grad_q = mm(score_term, k) + grad_grown * grow
        grad_k = (
            mm(score_term, q, TN)
            + mm(gram_term, k)
            + mm(gram_term, k, TN)
            + grad_tail * fall
            + beta_grow * grad_key_in
        )
        grad_v = beta_col * grad_val_in
        q_u = query_unit[span]
        k_u = key_unit[span]
        grad_query_raw = (query_scale[span] * DK ** (-0.5)) * (
            grad_q - q_u * jnp.sum(grad_q * q_u, axis=1, keepdims=True)
        )
        grad_key_raw = key_scale[span] * (
            grad_k - k_u * jnp.sum(grad_k * k_u, axis=1, keepdims=True)
        )
        grad_active[tile] = jnp.concatenate([grad_query_raw, grad_key_raw, grad_v], axis=1)
    grad_gain_ref[0, 0] = jnp.broadcast_to(grad_gain, (8, DV))
    grad_summed = jnp.concatenate(grad_active, axis=0) * (sig * (1.0 + summed * (1.0 - sig)))
    grad_pre = taps[CONV - 1 : CONV] * grad_summed
    grad_taps = [None] * CONV
    grad_taps[CONV - 1] = jnp.sum(grad_summed * pre, axis=0, keepdims=True)
    for back in range(1, CONV):
        tap = CONV - 1 - back
        ahead = shifted(grad_summed, -back)
        grad_pre = grad_pre + taps[tap : tap + 1] * ahead
        grad_taps[tap] = jnp.sum(ahead * pre, axis=0, keepdims=True)
    grad_proj_ref[0, :, :PRE] = grad_pre.astype(BF16)
    grad_taps_ref[0, 0] = jnp.concatenate(grad_taps + [jnp.zeros((8 - CONV, PRE), F32)], axis=0)
    grad_beta_all = jnp.concatenate(grad_beta_rows, axis=1)
    grad_decay_all = jnp.concatenate(grad_decay_rows, axis=1)
    grad_scalar_ref[0, 0] = jnp.concatenate(
        [
            grad_beta_all * beta_all * (1.0 - beta_all),
            grad_decay_all * slope_all,
            grad_decay_all * decay_all,
            jnp.zeros((5, length), F32),
        ],
        axis=0,
    )


def mixer_backward(
    a_log, dt_bias, grad_head, projected, scalars, inverse, states, mixed, fresh, taps, gain
):
    slots, length, _ = grad_head.shape
    heads = scalars.shape[1]
    blocks = length // SPAN
    tiles = length // TILE
    unit = lambda s, h: (s, h, 0, 0)
    unit5 = lambda s, h: (s, h, 0, 0, 0)
    return pl.pallas_call(
        mixer_back_kernel,
        name="mixer_backward",
        grid=(slots, heads),
        in_specs=[
            pl.BlockSpec(memory_space=pltpu.SMEM),
            pl.BlockSpec(memory_space=pltpu.SMEM),
            pl.BlockSpec((1, length, DV), lambda s, h: (s, 0, h)),
            pl.BlockSpec((1, length, HEAD), lambda s, h: (s, 0, h)),
            pl.BlockSpec((1, 1, 8, length), unit),
            pl.BlockSpec((1, 1, tiles, TILE, TILE), unit5),
            pl.BlockSpec((1, 1, blocks, DK, DV), unit5),
            pl.BlockSpec((1, 1, length, DV), unit),
            pl.BlockSpec((1, 1, length, DV), unit),
            pl.BlockSpec((CONV, PRE), lambda s, h: (0, h)),
            pl.BlockSpec((1, DV), lambda s, h: (0, 0)),
        ],
        out_specs=[
            pl.BlockSpec((1, length, HEAD), lambda s, h: (s, 0, h)),
            pl.BlockSpec((1, 1, 8, length), unit),
            pl.BlockSpec((1, 1, 8, PRE), unit),
            pl.BlockSpec((1, 1, 8, DV), unit),
        ],
        out_shape=[
            jax.ShapeDtypeStruct((slots, length, heads * HEAD), BF16),
            jax.ShapeDtypeStruct((slots, heads, 8, length), F32),
            jax.ShapeDtypeStruct((slots, heads, 8, PRE), F32),
            jax.ShapeDtypeStruct((slots, heads, 8, DV), F32),
        ],
        cost_estimate=pl.CostEstimate(
            flops=slots * heads * length * 15_000_000,
            transcendentals=slots * heads * length * 2_000,
            bytes_accessed=slots * heads * length * 9_000,
        ),
        compiler_params=pltpu.CompilerParams(
            dimension_semantics=("arbitrary", "arbitrary"), vmem_limit_bytes=56 << 20
        ),
    )(
        a_log,
        dt_bias,
        grad_head,
        projected,
        scalars,
        inverse,
        states,
        mixed,
        fresh,
        taps,
        gain,
    )


def row_scale(values):
    return lax.rsqrt(jnp.mean(values * values, axis=-1, keepdims=True) + EPS_ROW)


def norm_back(grad_out, normed, scale, gain_vec):
    weighted = grad_out * gain_vec
    return scale * (weighted - normed * jnp.mean(weighted * normed, axis=-1, keepdims=True))


def product(left, right):
    return jnp.dot(left, right, preferred_element_type=jnp.float32)


def product_t(left, right):
    return lax.dot_general(left, right, NT, preferred_element_type=jnp.float32)


def rows_sum(lefts, rights):
    total = None
    for left, right in zip(lefts, rights):
        term = lax.dot_general(left, right, TN, preferred_element_type=jnp.float32)
        total = term if total is None else total + term
    return total


def after(value, *others):
    return lax.optimization_barrier((value, *others))[0]


def gather_rows(rows):
    if lax.axis_size("tensor") != 2:
        return lax.all_gather(rows, "tensor", axis=0, tiled=True)
    other = lax.ppermute(rows, "tensor", [(0, 1), (1, 0)])
    first = lax.axis_index("tensor") == 0
    return jnp.concatenate(
        [jnp.where(first, rows, other), jnp.where(first, other, rows)], axis=0
    )


def scatter_begin(partial):
    if lax.axis_size("tensor") != 2:
        return partial.astype(jnp.bfloat16), None
    half = partial.shape[0] // 2
    rank = lax.axis_index("tensor")
    sent = lax.dynamic_slice_in_dim(partial, (1 - rank) * half, half).astype(jnp.bfloat16)
    return sent, lax.dynamic_slice_in_dim(partial, rank * half, half)


def scatter_end(sent, kept):
    if kept is None:
        return lax.psum_scatter(sent, "tensor", scatter_dimension=0, tiled=True).astype(
            jnp.float32
        )
    other = lax.ppermute(sent, "tensor", [(0, 1), (1, 0)])
    return kept + other.astype(jnp.float32)


def pairs(ranks, bit):
    return [(rank, rank ^ bit) for rank in range(ranks)]


def halve(held, bit):
    ranks = lax.axis_size("dp")
    left = ranks // (2 * bit)
    mine = (lax.axis_index("dp") // bit) % 2
    sends, keeps = [], []
    for grads in held:
        rows = grads.reshape(left, 2, -1, grads.shape[-1])
        sends.append(lax.dynamic_index_in_dim(rows, 1 - mine, 1, keepdims=False))
        keeps.append(lax.dynamic_index_in_dim(rows, mine, 1, keepdims=False))
    join = lambda parts: parts[0] if len(parts) == 1 else jnp.concatenate(parts, axis=-1)
    return join(sends).astype(jnp.bfloat16), join(keeps)


def swap_add(sent, kept, bit):
    ranks = lax.axis_size("dp")
    got = lax.ppermute(sent, "dp", pairs(ranks, bit))
    total = kept.astype(jnp.float32) + got.astype(jnp.float32)
    return total if 2 * bit == ranks else total.astype(jnp.bfloat16)


def sum_begin(held, steps):
    bit = 1
    for _ in range(steps):
        sent, kept = halve(held, bit)
        held = [swap_add(sent, kept, bit)]
        bit *= 2
    return halve(held, bit) + (bit,)


def hold(state, *others):
    sent, kept, bit = state
    return sent, after(kept, *others), bit


def sum_step(state):
    sent, kept, bit = state
    return halve([swap_add(sent, kept, bit)], 2 * bit) + (2 * bit,)


def sum_end(state):
    sent, kept, bit = state
    held = swap_add(sent, kept, bit)
    while 2 * bit < lax.axis_size("dp"):
        bit *= 2
        held = swap_add(*halve([held], bit), bit)
    return held.reshape(-1, held.shape[-1])


def sum_all(values, axis):
    ranks = lax.axis_size(axis)
    bit = 1
    while bit < ranks:
        values = values + lax.ppermute(values, axis, pairs(ranks, bit))
        bit *= 2
    return values


def reduce_small(own_parts, shared_parts):
    own = jnp.concatenate([part.reshape(-1) for part in own_parts])
    shared = sum_all(jnp.concatenate([part.reshape(-1) for part in shared_parts]), "tensor")
    total = sum_all(jnp.concatenate([own, shared]), "dp")
    results = []
    at = 0
    for part in own_parts + shared_parts:
        results.append(total[at : at + part.size].reshape(part.shape))
        at += part.size
    return results


def scalar_rows(back, heads):
    return back[1][0, :, :2].transpose(2, 0, 1).reshape(-1, 2 * heads).astype(jnp.bfloat16)


def body(
    tokens,
    seq_counts,
    mix_gain,
    query_key_value_gate_weight,
    beta_decay_weight,
    conv_w,
    a_log,
    dt_bias,
    o_gain,
    output_weight,
    ffn_gain,
    gate_weight,
    up_weight,
    down_weight,
    cotangent,
):
    slots = tokens.shape[0]
    heads = a_log.shape[0]
    width = tokens.shape[2]
    every = range(slots)
    group = lax.axis_index("dp")
    count_here = lax.dynamic_index_in_dim(seq_counts, group, keepdims=False)
    mix_gain_f = mix_gain.astype(jnp.float32)
    ffn_gain_f = ffn_gain.astype(jnp.float32)
    o_gain_f = o_gain.astype(jnp.float32)[None]
    scalar_weight = jnp.pad(
        beta_decay_weight.T.reshape(heads, 2, width), ((0, 0), (0, 6), (0, 0))
    )
    live = [(s < count_here).astype(jnp.float32) for s in every]
    states = [tokens[s].astype(jnp.float32) for s in every]
    mix_scale = [row_scale(x) for x in states]
    mix_normed = [x * r for x, r in zip(states, mix_scale)]
    grad_out = [cotangent[s].astype(jnp.float32) * live[s] for s in every]
    first, second = 0, 1
    mix_rows = [(n * mix_gain_f).astype(jnp.bfloat16) for n in mix_normed]
    mix_full = [gather_rows(mix_rows[first])]
    mix_full.append(gather_rows(after(mix_rows[second], mix_full[first])))
    cot_rows = [g.astype(jnp.bfloat16) for g in grad_out]
    cot_full = [gather_rows(after(cot_rows[first], mix_full[first]))]
    cot_full.append(gather_rows(after(cot_rows[second], mix_full[second], cot_full[first])))

    def mix_forward(s, inputs):
        return mixer_forward(
            a_log[None],
            dt_bias[None],
            inputs[None],
            query_key_value_gate_weight,
            scalar_weight,
            conv_w,
            o_gain_f,
        )

    def mix_backward(s, grad_head):
        return mixer_backward(
            a_log[None],
            dt_bias[None],
            grad_head[None],
            *kept[s][1:],
            conv_w,
            o_gain_f,
        )

    def branch_begin(head_rows):
        return scatter_begin(product_t(head_rows, output_weight))

    def ffn_begin(branch, inputs):
        middle = inputs + branch
        scale = row_scale(middle)
        normed = middle * scale
        return middle, scale, normed, (normed * ffn_gain_f).astype(jnp.bfloat16)

    def ffn_middle(full, grad_hidden):
        gate = product(full, gate_weight)
        up = product(full, up_weight)
        sig = jax.nn.sigmoid(gate)
        act = gate * sig
        units = (act * up).astype(jnp.bfloat16)
        grad_gate = (grad_hidden * up * sig * (1.0 + gate * (1.0 - sig))).astype(jnp.bfloat16)
        grad_up = (grad_hidden * act).astype(jnp.bfloat16)
        back_part = product_t(grad_gate, gate_weight) + product_t(grad_up, up_weight)
        return units, grad_gate, grad_up, scatter_begin(back_part)

    def ffn_end(s, grad_in, gate_fact):
        middle, scale, normed, _ = gate_fact
        grad_mid = grad_in[1] + norm_back(grad_in[0], normed, scale, ffn_gain_f)
        return grad_mid, grad_mid.astype(jnp.bfloat16)

    kept = [mix_forward(first, mix_full[first])]
    head_low = [kept[first][0][0]]
    branch = [branch_begin(head_low[first])]
    kept.append(mix_forward(second, after(mix_full[second], branch[first][0], cot_full[first])))
    head_low.append(kept[second][0][0])
    facts = [
        ffn_begin(
            scatter_end(*branch[first]), after(states[first], head_low[second], cot_full[second])
        )
    ]
    branch.append(branch_begin(after(head_low[second], facts[first][3])))
    grad_hidden = [
        product(after(cot_full[s], branch[second][0]), down_weight) for s in every
    ]
    ffn_full = [after(gather_rows(facts[first][3]), grad_hidden[first], grad_hidden[second])]
    inner = [ffn_middle(ffn_full[first], grad_hidden[first])]
    facts.append(
        ffn_begin(
            scatter_end(*branch[second]), after(states[second], inner[first][3][0])
        )
    )
    parts_of = lambda s: [
        rows_sum([left], [right])
        for left, right in (
            (cot_full[s], inner[s][0]),
            (ffn_full[s], inner[s][1]),
            (ffn_full[s], inner[s][2]),
        )
    ]
    out_part = [scatter_begin(product_t(after(inner[first][0], facts[second][3]), down_weight))]
    early = parts_of(first)
    ffn_full.append(after(gather_rows(facts[second][3]), out_part[first][0], *early))
    inner.append(ffn_middle(ffn_full[second], grad_hidden[second]))
    grad_ffn_in = [scatter_end(*inner[first][3])]
    ends = [
        ffn_end(
            first, (grad_ffn_in[first], after(grad_out[first], inner[second][3][0])), facts[first]
        )
    ]
    late = [
        rows_sum([after(left, ends[first][1])], [right])
        for left, right in (
            (cot_full[second], inner[second][0]),
            (ffn_full[second], inner[second][1]),
            (ffn_full[second], inner[second][2]),
        )
    ]
    ffn_sums = [(one + two).astype(jnp.bfloat16) for one, two in zip(early, late)]
    out_part.append(scatter_begin(product_t(inner[second][0], down_weight)))
    down_begin = halve(ffn_sums[:1], 1) + (1,)
    pair_begin = halve(ffn_sums[1:], 1) + (1,)
    grad_ffn_in.append(scatter_end(*inner[second][3]))
    ends.append(
        ffn_end(
            second,
            (grad_ffn_in[second], after(grad_out[second], down_begin[0], pair_begin[0])),
            facts[second],
        )
    )
    branch_full = [gather_rows(ends[first][1])]
    down_state = sum_step(down_begin)
    grad_head = product(
        after(branch_full[first], ends[second][1], down_state[0]), output_weight
    )
    back = [mix_backward(first, grad_head)]
    proj_low = [back[first][0][0]]
    branch_full.append(after(gather_rows(ends[second][1]), proj_low[first]))
    down_state = sum_step(hold(down_state, proj_low[first]))
    pair_state = sum_step(hold(pair_begin, proj_low[first]))
    grad_head = product(branch_full[second], output_weight)
    out_state = sum_begin([rows_sum(branch_full, head_low).astype(jnp.bfloat16)], 0)
    scalar_low = [scalar_rows(back[first], heads)]
    mix_parts = [
        scatter_begin(
            product_t(proj_low[first], query_key_value_gate_weight)
            + product_t(scalar_low[first], beta_decay_weight)
        )
    ]
    grad_head = after(
        grad_head, down_state[0], pair_state[0], out_state[0], mix_parts[first][0]
    )
    back.append(mix_backward(second, grad_head))
    proj_low.append(back[second][0][0])
    scalar_low.append(scalar_rows(back[second], heads))
    chunk = heads * HEAD // 2
    qkvg_states = []
    for at in range(0, heads * HEAD, chunk):
        terms = [p[:, at : at + chunk] for p in proj_low]
        qkvg_states.append(sum_begin([rows_sum(mix_full, terms).astype(jnp.bfloat16)], 0))
    mix_parts.append(
        scatter_begin(
            product_t(after(proj_low[second], qkvg_states[0][0]), query_key_value_gate_weight)
            + product_t(scalar_low[second], beta_decay_weight)
        )
    )
    sent = [state[0] for state in qkvg_states]
    sum_down = sum_end(hold(down_state, *sent))
    sum_gate, sum_up = jnp.split(sum_end(hold(pair_state, *sent)), 2, axis=1)
    sum_out = sum_end(hold(out_state, *sent))
    qkvg_states = [sum_step(hold(state, *sent)) for state in qkvg_states]
    sent = [state[0] for state in qkvg_states]
    sum_qkvg = jnp.concatenate([sum_end(state) for state in qkvg_states], axis=1)
    taps_grads = sum(b[2] for b in back)
    scalar_grads = sum(b[1] for b in back)
    gain_grads = sum(b[3] for b in back)
    grad_conv = taps_grads[0, :, :CONV].transpose(1, 0, 2).reshape(CONV, -1)
    grad_dtb = jnp.sum(scalar_grads[0, :, 1], axis=1)
    grad_alog = jnp.sum(scalar_grads[0, :, 2], axis=1)
    o_gain_part = jnp.sum(gain_grads[0, :, 0], axis=0)
    grad_w_ba = after(rows_sum(mix_full, scalar_low), *sent)
    outputs, tokens_grad = [], []
    mix_gain_part, ffn_gain_part = 0.0, 0.0
    for s in every:
        ffn_gain_part = ffn_gain_part + jnp.sum(grad_ffn_in[s] * facts[s][2], axis=0)
        outputs.append(
            ((facts[s][0] + scatter_end(*out_part[s])) * live[s]).astype(jnp.bfloat16)
        )
        grad_mix_in = scatter_end(*mix_parts[s])
        mix_gain_part = mix_gain_part + jnp.sum(grad_mix_in * mix_normed[s], axis=0)
        back_in = norm_back(grad_mix_in, mix_normed[s], mix_scale[s], mix_gain_f)
        tokens_grad.append((ends[s][0] + back_in) * live[s])
    conv_grad, alog_grad, dtb_grad, ba_grad, mix_gain_grad, o_gain_grad, ffn_gain_grad = (
        reduce_small(
            (grad_conv, grad_alog, grad_dtb, grad_w_ba),
            (mix_gain_part, o_gain_part, ffn_gain_part),
        )
    )
    block = width // lax.axis_size("dp")
    sum_ba = lax.dynamic_slice_in_dim(ba_grad, group * block, block)
    return (
        jnp.stack(outputs),
        jnp.stack(tokens_grad),
        mix_gain_grad,
        sum_qkvg,
        sum_ba,
        conv_grad,
        alog_grad,
        dtb_grad,
        o_gain_grad,
        sum_out,
        ffn_gain_grad,
        sum_gate,
        sum_up,
        sum_down,
    )


def solution(mesh):
    return jax.shard_map(
        body,
        mesh=mesh,
        in_specs=(
            P("dp", "tensor", None),
            P(),
            P(),
            P(None, "tensor"),
            P(None, "tensor"),
            P(None, "tensor"),
            P("tensor"),
            P("tensor"),
            P(),
            P(None, "tensor"),
            P(),
            P(None, "tensor"),
            P(None, "tensor"),
            P(None, "tensor"),
            P("dp", "tensor", None),
        ),
        out_specs=(
            P("dp", "tensor", None),
            P("dp", "tensor", None),
            P(),
            P("dp", "tensor"),
            P("dp", "tensor"),
            P(None, "tensor"),
            P("tensor"),
            P("tensor"),
            P(),
            P("dp", "tensor"),
            P(),
            P("dp", "tensor"),
            P("dp", "tensor"),
            P("dp", "tensor"),
        ),
        check_vma=False,
    )
```

```python
import functools

import jax
import jax.numpy as jnp
from jax import lax
from jax.experimental import pallas as pl
from jax.experimental.pallas import tpu as pltpu
from jax.sharding import PartitionSpec as P

DK = 128
DV = 256
CONV = 4
SPAN = 64
PRE = 2 * DK + DV
HEAD = PRE + DV
TILE = 2 * SPAN
F32 = jnp.float32
BF16 = jnp.bfloat16

EPS_ROW = 1e-06
EPS_HEAD = 1e-05
EPS_UNIT = 1e-06

NN = (((1,), (0,)), ((), ()))
NT = (((1,), (1,)), ((), ()))
TN = (((0,), (0,)), ((), ()))


def mm(left, right, dims=NN):
    return lax.dot_general(
        left.astype(BF16), right.astype(BF16), dims, preferred_element_type=F32
    )


def tile_masks():
    row = lax.broadcasted_iota(jnp.int32, (TILE, TILE), 0)
    col = lax.broadcasted_iota(jnp.int32, (TILE, TILE), 1)
    return row, col, row ^ col


def shifted(rows, steps):
    length = rows.shape[0]
    if steps == 0:
        return rows
    pos = lax.broadcasted_iota(jnp.int32, rows.shape, 0)
    rolled = pltpu.roll(rows, steps % length, axis=0)
    keep = pos >= steps if steps > 0 else pos < length + steps
    return jnp.where(keep, rolled, 0.0)


def convolve(pre, taps):
    summed = taps[CONV - 1 : CONV] * pre
    for back in range(1, CONV):
        tap = CONV - 1 - back
        summed = summed + taps[tap : tap + 1] * shifted(pre, back)
    return summed


def unit_rows(raw):
    scale = lax.rsqrt(jnp.sum(raw * raw, axis=1, keepdims=True) + EPS_UNIT)
    return raw * scale, scale


def decay_rows(scalars, a_log, dt_bias):
    rate = jnp.exp(jnp.full((1, 1), a_log, F32))
    shifted_in = scalars[1:2] + dt_bias
    soft = jnp.maximum(shifted_in, 0.0) + jnp.log1p(jnp.exp(-jnp.abs(shifted_in)))
    return lax.logistic(scalars[0:1]), -rate * soft, -rate * lax.logistic(shifted_in)


def tile_scalars(row, col, apart, beta_row, decay_row):
    lower = (apart < SPAN) & (row >= col)
    eye = apart == 0
    cum_col = jnp.sum(jnp.where(lower, decay_row, 0.0), axis=1, keepdims=True)
    beta_col = jnp.sum(jnp.where(eye, beta_row, 0.0), axis=1, keepdims=True)
    cum_row = jnp.sum(jnp.where(eye, cum_col, 0.0), axis=0, keepdims=True)
    last = row | (SPAN - 1)
    last_col = jnp.sum(jnp.where(col == last, cum_row, 0.0), axis=1, keepdims=True)
    decay = jnp.where(lower, jnp.exp(jnp.where(lower, cum_col - cum_row, 0.0)), 0.0)
    return cum_col, beta_col, last_col, decay


def invert(apart, couplings):
    eye = jnp.where(apart == 0, 1.0, 0.0)
    inverses = [eye - jnp.where(apart == 1, coupling, 0.0) for coupling in couplings]
    size = 2
    while size < SPAN:
        level = (apart >= size) & (apart < 2 * size)
        inner = [
            mm(jnp.where(level, coupling, 0.0), inverse)
            for coupling, inverse in zip(couplings, inverses)
        ]
        inverses = [inverse - mm(inverse, part) for inverse, part in zip(inverses, inner)]
        size *= 2
    return inverses


def mixer_kernel(
    a_log_ref,
    dt_bias_ref,
    mix_ref,
    weight_ref,
    scalar_weight_ref,
    taps_ref,
    gain_ref,
    head_ref,
    proj_ref,
    scalar_ref,
    inverse_ref,
    state_ref,
    mixed_ref,
    fresh_ref,
):
    head = pl.program_id(1)
    inputs = mix_ref[0]
    projected = mm(inputs, weight_ref[...])
    proj_ref[0] = projected
    scalars = mm(scalar_weight_ref[0], inputs, NT)
    scalar_ref[0, 0] = scalars
    beta_all, decay_all, _ = decay_rows(scalars, a_log_ref[0, head], dt_bias_ref[0, head])
    summed = convolve(projected[:, :PRE], taps_ref[...])
    active = summed * lax.logistic(summed)
    queries = (unit_rows(active[:, :DK])[0] * DK ** (-0.5)).astype(BF16)
    keys = unit_rows(active[:, DK : 2 * DK])[0].astype(BF16)
    vals = active[:, 2 * DK :].astype(BF16)
    row, col, apart = tile_masks()
    strict = (apart < SPAN) & (row > col)
    length = inputs.shape[0]
    per = TILE // SPAN
    tiles = range(length // TILE)
    spans = [slice(tile * TILE, (tile + 1) * TILE) for tile in tiles]
    facts = [
        tile_scalars(row, col, apart, beta_all[:, span], decay_all[:, span]) for span in spans
    ]
    couplings = [
        jnp.where(strict, fact[1] * mm(keys[span], keys[span], NT) * fact[3], 0.0)
        for span, fact in zip(spans, facts)
    ]
    inverses = invert(apart, couplings)
    prepared = []
    for tile in tiles:
        span = spans[tile]
        cum_col, beta_col, last_col, decay = facts[tile]
        inverse_ref[0, 0, tile] = inverses[tile]
        k_f = keys[span].astype(F32)
        grow = jnp.exp(cum_col)
        solved_w = mm(inverses[tile], (beta_col * grow) * k_f)
        solved_u = mm(inverses[tile], beta_col * vals[span].astype(F32))
        scores = mm(queries[span], keys[span], NT) * decay
        grown = queries[span].astype(F32) * grow
        tail = k_f * jnp.exp(last_col - cum_col)
        both = jnp.concatenate([solved_w, solved_u], axis=1).astype(BF16)
        steps = [
            mm(tail[block * SPAN : (block + 1) * SPAN], both[block * SPAN : (block + 1) * SPAN], TN)
            for block in range(per)
        ]
        prepared.append((solved_w, solved_u, scores, grown, steps))
    state = jnp.zeros((DK, DV), F32)
    states = []
    for tile in tiles:
        for block in range(per):
            states.append(state.astype(BF16))
            state_ref[0, 0, tile * per + block] = state
            step = prepared[tile][4][block]
            carry = jnp.exp(facts[tile][2][block * SPAN : block * SPAN + 1])
            state = carry * state + step[:, DK:] - mm(step[:, :DK], state)
    for tile in tiles:
        span = spans[tile]
        solved_w, solved_u, scores, grown, _ = prepared[tile]
        fresh = []
        read = []
        for block in range(per):
            part = slice(block * SPAN, (block + 1) * SPAN)
            used = mm(
                jnp.concatenate([solved_w[part], grown[part]], axis=0), states[tile * per + block]
            )
            fresh.append(solved_u[part] - used[:SPAN])
            read.append(used[SPAN:])
        fresh = jnp.concatenate(fresh, axis=0)
        mixed = jnp.concatenate(read, axis=0) + mm(scores, fresh)
        fresh_ref[0, 0, span] = fresh
        mixed_ref[0, 0, span] = mixed
        scale = lax.rsqrt(jnp.mean(mixed * mixed, axis=1, keepdims=True) + EPS_HEAD)
        gate = projected[span, PRE:]
        head_ref[0, span] = (
            mixed * scale * gain_ref[...] * (gate * lax.logistic(gate))
        ).astype(BF16)


def mixer_forward(a_log, dt_bias, mix, weight, scalar_weight, taps, gain):
    slots, length, width = mix.shape
    heads = weight.shape[1] // HEAD
    blocks = length // SPAN
    tiles = length // TILE
    unit = lambda s, h: (s, h, 0, 0)
    unit5 = lambda s, h: (s, h, 0, 0, 0)
    return pl.pallas_call(
        mixer_kernel,
        name="mixer_forward",
        grid=(slots, heads),
        in_specs=[
            pl.BlockSpec(memory_space=pltpu.SMEM),
            pl.BlockSpec(memory_space=pltpu.SMEM),
            pl.BlockSpec((1, length, width), lambda s, h: (s, 0, 0)),
            pl.BlockSpec((width, HEAD), lambda s, h: (0, h)),
            pl.BlockSpec((1, 8, width), lambda s, h: (h, 0, 0)),
            pl.BlockSpec((CONV, PRE), lambda s, h: (0, h)),
            pl.BlockSpec((1, DV), lambda s, h: (0, 0)),
        ],
        out_specs=[
            pl.BlockSpec((1, length, DV), lambda s, h: (s, 0, h)),
            pl.BlockSpec((1, length, HEAD), lambda s, h: (s, 0, h)),
            pl.BlockSpec((1, 1, 8, length), unit),
            pl.BlockSpec((1, 1, tiles, TILE, TILE), unit5),
            pl.BlockSpec((1, 1, blocks, DK, DV), unit5),
            pl.BlockSpec((1, 1, length, DV), unit),
            pl.BlockSpec((1, 1, length, DV), unit),
        ],
        out_shape=[
            jax.ShapeDtypeStruct((slots, length, heads * DV), BF16),
            jax.ShapeDtypeStruct((slots, length, heads * HEAD), F32),
            jax.ShapeDtypeStruct((slots, heads, 8, length), F32),
            jax.ShapeDtypeStruct((slots, heads, tiles, TILE, TILE), F32),
            jax.ShapeDtypeStruct((slots, heads, blocks, DK, DV), F32),
            jax.ShapeDtypeStruct((slots, heads, length, DV), F32),
            jax.ShapeDtypeStruct((slots, heads, length, DV), F32),
        ],
        cost_estimate=pl.CostEstimate(
            flops=slots * heads * length * 24_000_000,
            transcendentals=slots * heads * length * 2_000,
            bytes_accessed=slots * heads * length * 9_000,
        ),
        compiler_params=pltpu.CompilerParams(
            dimension_semantics=("arbitrary", "arbitrary"), vmem_limit_bytes=56 << 20
        ),
    )(a_log, dt_bias, mix, weight, scalar_weight, taps, gain)


def mixer_back_kernel(
    start,
    a_log_ref,
    dt_bias_ref,
    grad_ref,
    proj_ref,
    scalar_ref,
    inverse_ref,
    state_ref,
    mixed_ref,
    fresh_ref,
    taps_ref,
    gain_ref,
    grad_proj_ref,
    grad_scalar_ref,
    grad_taps_ref,
    grad_gain_ref,
):
    head = start + pl.program_id(1)
    length = grad_ref.shape[1]
    pre = proj_ref[0, :, :PRE]
    taps = taps_ref[...]
    gain = gain_ref[...]
    scalars = scalar_ref[0, 0]
    beta_all, decay_all, slope_all = decay_rows(
        scalars, a_log_ref[0, head], dt_bias_ref[0, head]
    )
    summed = convolve(pre, taps)
    sig = lax.logistic(summed)
    active = summed * sig
    query_unit, query_scale = unit_rows(active[:, :DK])
    key_unit, key_scale = unit_rows(active[:, DK : 2 * DK])
    queries = (query_unit * DK ** (-0.5)).astype(BF16)
    keys = key_unit.astype(BF16)
    vals = active[:, 2 * DK :].astype(BF16)
    row, col, apart = tile_masks()
    lower = (apart < SPAN) & (row >= col)
    strict = (apart < SPAN) & (row > col)
    eye = apart == 0
    is_last = (row[:, :1] & (SPAN - 1)) == (SPAN - 1)
    per = TILE // SPAN
    grad_gain = jnp.zeros((1, DV), F32)
    carried = jnp.zeros((DK, DV), F32)
    grad_active = [None] * (length // TILE)
    grad_beta_rows = [None] * (length // TILE)
    grad_decay_rows = [None] * (length // TILE)
    for tile in reversed(range(length // TILE)):
        span = slice(tile * TILE, (tile + 1) * TILE)
        cum_col, beta_col, last_col, decay = tile_scalars(
            row, col, apart, beta_all[:, span], decay_all[:, span]
        )
        gate = proj_ref[0, span, PRE:]
        gate_sig = lax.logistic(gate)
        gate_act = gate * gate_sig
        mixed = mixed_ref[0, 0, span]
        scale = lax.rsqrt(jnp.mean(mixed * mixed, axis=1, keepdims=True) + EPS_HEAD)
        normed = mixed * scale
        grad = grad_ref[0, span]
        grad_normed = grad * normed
        grad_gain = grad_gain + jnp.sum(grad_normed * gate_act, axis=0, keepdims=True)
        grad_proj_ref[0, span, PRE:] = (
            grad_normed * gain * (gate_sig * (1.0 + gate * (1.0 - gate_sig)))
        ).astype(BF16)
        weighted = grad * gain * gate_act
        grad_mixed = scale * (
            weighted - normed * jnp.mean(weighted * normed, axis=1, keepdims=True)
        )
        q = queries[span]
        k = keys[span]
        v = vals[span]
        q_f = q.astype(F32)
        k_f = k.astype(F32)
        v_f = v.astype(F32)
        gram = mm(k, k, NT)
        coupling = jnp.where(strict, beta_col * gram * decay, 0.0)
        scores = mm(q, k, NT) * decay
        inverse = inverse_ref[0, 0, tile].astype(BF16)
        grow = jnp.exp(cum_col)
        fall = jnp.exp(last_col - cum_col)
        beta_grow = beta_col * grow
        key_in = beta_grow * k_f
        solved_w = mm(inverse, key_in)
        solved_u = mm(inverse, beta_col * v_f)
        grown = q_f * grow
        tail = k_f * fall
        fresh = fresh_ref[0, 0, span]
        grad_low = grad_mixed.astype(BF16)
        local = mm(scores, grad_low, TN)
        grad_fresh = [None] * per
        grad_grown = [None] * per
        grad_tail = [None] * per
        grad_w = [None] * per
        carry_terms = [None] * per
        for block in reversed(range(per)):
            part = slice(block * SPAN, (block + 1) * SPAN)
            state = state_ref[0, 0, tile * per + block]
            carry = jnp.exp(last_col[block * SPAN : block * SPAN + 1])
            here = local[part] + mm(tail[part], carried)
            grad_fresh[block] = here
            both = mm(jnp.concatenate([grad_low[part], here.astype(BF16)], axis=0), state, NT)
            grad_grown[block] = both[:SPAN]
            grad_w[block] = -both[SPAN:]
            grad_tail[block] = mm(fresh[part], carried, NT)
            product = jnp.sum(state * carried, axis=0, keepdims=True)
            carry_terms[block] = carry * jnp.sum(product, axis=1, keepdims=True)
            carried = carry * carried + mm(
                jnp.concatenate([grown[part], -solved_w[part]], axis=0),
                jnp.concatenate([grad_low[part], here.astype(BF16)], axis=0),
                TN,
            )
        grad_fresh = jnp.concatenate(grad_fresh, axis=0)
        grad_grown = jnp.concatenate(grad_grown, axis=0)
        grad_tail = jnp.concatenate(grad_tail, axis=0)
        grad_w = jnp.concatenate(grad_w, axis=0)
        grad_key_in = mm(inverse, grad_w, TN)
        grad_val_in = mm(inverse, grad_fresh, TN)
        grad_coupling = jnp.where(
            strict, -(mm(grad_key_in, solved_w, NT) + mm(grad_val_in, solved_u, NT)), 0.0
        )
        grad_scores = mm(grad_low, fresh, NT)
        score_term = grad_scores * decay
        gram_term = grad_coupling * decay
        grad_beta = (
            jnp.sum(gram_term * gram, axis=1, keepdims=True)
            + grow * jnp.sum(grad_key_in * k_f, axis=1, keepdims=True)
            + jnp.sum(grad_val_in * v_f, axis=1, keepdims=True)
        )
        gram_term = gram_term * beta_col
        exponent = grad_coupling * coupling + grad_scores * scores
        tail_sum = jnp.sum(grad_tail * tail, axis=1, keepdims=True)
        grad_cum = (
            jnp.sum(exponent, axis=1, keepdims=True)
            + jnp.sum(grad_grown * grown, axis=1, keepdims=True)
            + jnp.sum(grad_key_in * key_in, axis=1, keepdims=True)
            - tail_sum
        )
        ends = []
        for block in range(per):
            part = slice(block * SPAN, (block + 1) * SPAN)
            total = jnp.sum(tail_sum[part], axis=0, keepdims=True) + carry_terms[block]
            ends.append(jnp.broadcast_to(total, (SPAN, 1)))
        grad_cum = grad_cum + jnp.where(is_last, jnp.concatenate(ends, axis=0), 0.0)
        column_sum = jnp.sum(exponent, axis=0, keepdims=True)
        cum_back = jnp.sum(jnp.where(eye, column_sum, 0.0), axis=1, keepdims=True)
        grad_cum = grad_cum - cum_back
        grad_decay_rows[tile] = jnp.sum(jnp.where(lower, grad_cum, 0.0), axis=0, keepdims=True)
        grad_beta_rows[tile] = jnp.sum(jnp.where(eye, grad_beta, 0.0), axis=0, keepdims=True)
        grad_q = mm(score_term, k) + grad_grown * grow
        grad_k = (
            mm(score_term, q, TN)
            + mm(gram_term, k)
            + mm(gram_term, k, TN)
            + grad_tail * fall
            + beta_grow * grad_key_in
        )
        grad_v = beta_col * grad_val_in
        q_u = query_unit[span]
        k_u = key_unit[span]
        grad_query_raw = (query_scale[span] * DK ** (-0.5)) * (
            grad_q - q_u * jnp.sum(grad_q * q_u, axis=1, keepdims=True)
        )
        grad_key_raw = key_scale[span] * (
            grad_k - k_u * jnp.sum(grad_k * k_u, axis=1, keepdims=True)
        )
        grad_active[tile] = jnp.concatenate([grad_query_raw, grad_key_raw, grad_v], axis=1)
    grad_gain_ref[0, 0] = jnp.broadcast_to(grad_gain, (8, DV))
    grad_summed = jnp.concatenate(grad_active, axis=0) * (sig * (1.0 + summed * (1.0 - sig)))
    grad_pre = taps[CONV - 1 : CONV] * grad_summed
    grad_taps = [None] * CONV
    grad_taps[CONV - 1] = jnp.sum(grad_summed * pre, axis=0, keepdims=True)
    for back in range(1, CONV):
        tap = CONV - 1 - back
        ahead = shifted(grad_summed, -back)
        grad_pre = grad_pre + taps[tap : tap + 1] * ahead
        grad_taps[tap] = jnp.sum(ahead * pre, axis=0, keepdims=True)
    grad_proj_ref[0, :, :PRE] = grad_pre.astype(BF16)
    grad_taps_ref[0, 0] = jnp.concatenate(grad_taps + [jnp.zeros((8 - CONV, PRE), F32)], axis=0)
    grad_beta_all = jnp.concatenate(grad_beta_rows, axis=1)
    grad_decay_all = jnp.concatenate(grad_decay_rows, axis=1)
    grad_scalar_ref[0, 0] = jnp.concatenate(
        [
            grad_beta_all * beta_all * (1.0 - beta_all),
            grad_decay_all * slope_all,
            grad_decay_all * decay_all,
            jnp.zeros((5, length), F32),
        ],
        axis=0,
    )


def mixer_backward(
    start, heads, a_log, dt_bias, grad_head, projected, scalars, inverse, states, mixed, fresh,
    taps, gain
):
    slots, length, _ = grad_head.shape
    blocks = length // SPAN
    tiles = length // TILE
    own = lambda s, h: (s, h, 0, 0)
    unit = lambda s, h: (s, start + h, 0, 0)
    unit5 = lambda s, h: (s, start + h, 0, 0, 0)
    return pl.pallas_call(
        functools.partial(mixer_back_kernel, start),
        name="mixer_backward",
        grid=(slots, heads),
        in_specs=[
            pl.BlockSpec(memory_space=pltpu.SMEM),
            pl.BlockSpec(memory_space=pltpu.SMEM),
            pl.BlockSpec((1, length, DV), lambda s, h: (s, 0, start + h)),
            pl.BlockSpec((1, length, HEAD), lambda s, h: (s, 0, start + h)),
            pl.BlockSpec((1, 1, 8, length), unit),
            pl.BlockSpec((1, 1, tiles, TILE, TILE), unit5),
            pl.BlockSpec((1, 1, blocks, DK, DV), unit5),
            pl.BlockSpec((1, 1, length, DV), unit),
            pl.BlockSpec((1, 1, length, DV), unit),
            pl.BlockSpec((CONV, PRE), lambda s, h: (0, start + h)),
            pl.BlockSpec((1, DV), lambda s, h: (0, 0)),
        ],
        out_specs=[
            pl.BlockSpec((1, length, HEAD), lambda s, h: (s, 0, h)),
            pl.BlockSpec((1, 1, 8, length), own),
            pl.BlockSpec((1, 1, 8, PRE), own),
            pl.BlockSpec((1, 1, 8, DV), own),
        ],
        out_shape=[
            jax.ShapeDtypeStruct((slots, length, heads * HEAD), BF16),
            jax.ShapeDtypeStruct((slots, heads, 8, length), F32),
            jax.ShapeDtypeStruct((slots, heads, 8, PRE), F32),
            jax.ShapeDtypeStruct((slots, heads, 8, DV), F32),
        ],
        cost_estimate=pl.CostEstimate(
            flops=slots * heads * length * 15_000_000,
            transcendentals=slots * heads * length * 2_000,
            bytes_accessed=slots * heads * length * 9_000,
        ),
        compiler_params=pltpu.CompilerParams(
            dimension_semantics=("arbitrary", "arbitrary"), vmem_limit_bytes=56 << 20
        ),
    )(
        a_log,
        dt_bias,
        grad_head,
        projected,
        scalars,
        inverse,
        states,
        mixed,
        fresh,
        taps,
        gain,
    )


def row_scale(values):
    return lax.rsqrt(jnp.mean(values * values, axis=-1, keepdims=True) + EPS_ROW)


def norm_back(grad_out, normed, scale, gain_vec):
    weighted = grad_out * gain_vec
    return scale * (weighted - normed * jnp.mean(weighted * normed, axis=-1, keepdims=True))


def product(left, right):
    return jnp.dot(left, right, preferred_element_type=jnp.float32)


def product_t(left, right):
    return lax.dot_general(left, right, NT, preferred_element_type=jnp.float32)


def rows_sum(lefts, rights):
    total = None
    for left, right in zip(lefts, rights):
        term = lax.dot_general(left, right, TN, preferred_element_type=jnp.float32)
        total = term if total is None else total + term
    return total


def after(value, *others):
    return lax.optimization_barrier((value, *others))[0]


def gather_rows(rows):
    if lax.axis_size("tensor") != 2:
        return lax.all_gather(rows, "tensor", axis=0, tiled=True)
    other = lax.ppermute(rows, "tensor", [(0, 1), (1, 0)])
    first = lax.axis_index("tensor") == 0
    return jnp.concatenate(
        [jnp.where(first, rows, other), jnp.where(first, other, rows)], axis=0
    )


def scatter_begin(partial):
    if lax.axis_size("tensor") != 2:
        return partial.astype(jnp.bfloat16), None
    half = partial.shape[0] // 2
    rank = lax.axis_index("tensor")
    sent = lax.dynamic_slice_in_dim(partial, (1 - rank) * half, half).astype(jnp.bfloat16)
    return sent, lax.dynamic_slice_in_dim(partial, rank * half, half)


def scatter_end(sent, kept):
    if kept is None:
        return lax.psum_scatter(sent, "tensor", scatter_dimension=0, tiled=True).astype(
            jnp.float32
        )
    other = lax.ppermute(sent, "tensor", [(0, 1), (1, 0)])
    return kept + other.astype(jnp.float32)


def pairs(ranks, bit):
    return [(rank, rank ^ bit) for rank in range(ranks)]


def halve(held, bit):
    ranks = lax.axis_size("dp")
    left = ranks // (2 * bit)
    mine = (lax.axis_index("dp") // bit) % 2
    sends, keeps = [], []
    for grads in held:
        rows = grads.reshape(left, 2, -1, grads.shape[-1])
        sends.append(lax.dynamic_index_in_dim(rows, 1 - mine, 1, keepdims=False))
        keeps.append(lax.dynamic_index_in_dim(rows, mine, 1, keepdims=False))
    join = lambda parts: parts[0] if len(parts) == 1 else jnp.concatenate(parts, axis=-1)
    return join(sends).astype(jnp.bfloat16), join(keeps)


def swap_add(sent, kept, bit):
    ranks = lax.axis_size("dp")
    got = lax.ppermute(sent, "dp", pairs(ranks, bit))
    total = kept.astype(jnp.float32) + got.astype(jnp.float32)
    return total if 2 * bit == ranks else total.astype(jnp.bfloat16)


def sum_begin(held, steps):
    bit = 1
    for _ in range(steps):
        sent, kept = halve(held, bit)
        held = [swap_add(sent, kept, bit)]
        bit *= 2
    return halve(held, bit) + (bit,)


def hold(state, *others):
    sent, kept, bit = state
    return sent, after(kept, *others), bit


def sum_step(state):
    sent, kept, bit = state
    return halve([swap_add(sent, kept, bit)], 2 * bit) + (2 * bit,)


def sum_next(state):
    return state if 2 * state[2] >= lax.axis_size("dp") else sum_step(state)


def sum_end(state):
    sent, kept, bit = state
    held = swap_add(sent, kept, bit)
    while 2 * bit < lax.axis_size("dp"):
        bit *= 2
        held = swap_add(*halve([held], bit), bit)
    return held.reshape(-1, held.shape[-1])


def sum_all(values, axis):
    ranks = lax.axis_size(axis)
    bit = 1
    while bit < ranks:
        values = values + lax.ppermute(values, axis, pairs(ranks, bit))
        bit *= 2
    return values


def reduce_small(own_parts, shared_parts):
    own = jnp.concatenate([part.reshape(-1) for part in own_parts])
    shared = sum_all(jnp.concatenate([part.reshape(-1) for part in shared_parts]), "tensor")
    total = sum_all(jnp.concatenate([own, shared]), "dp")
    results = []
    at = 0
    for part in own_parts + shared_parts:
        results.append(total[at : at + part.size].reshape(part.shape))
        at += part.size
    return results


def scalar_rows(back, heads):
    return back[1][0, :, :2].transpose(2, 0, 1).reshape(-1, 2 * heads).astype(jnp.bfloat16)


def body(
    tokens,
    seq_counts,
    mix_gain,
    query_key_value_gate_weight,
    beta_decay_weight,
    conv_w,
    a_log,
    dt_bias,
    o_gain,
    output_weight,
    ffn_gain,
    gate_weight,
    up_weight,
    down_weight,
    cotangent,
):
    slots = tokens.shape[0]
    heads = a_log.shape[0]
    width = tokens.shape[2]
    every = range(slots)
    group = lax.axis_index("dp")
    count_here = lax.dynamic_index_in_dim(seq_counts, group, keepdims=False)
    mix_gain_f = mix_gain.astype(jnp.float32)
    ffn_gain_f = ffn_gain.astype(jnp.float32)
    o_gain_f = o_gain.astype(jnp.float32)[None]
    scalar_weight = jnp.pad(
        beta_decay_weight.T.reshape(heads, 2, width), ((0, 0), (0, 6), (0, 0))
    )
    live = [(s < count_here).astype(jnp.float32) for s in every]
    states = [tokens[s].astype(jnp.float32) for s in every]
    mix_scale = [row_scale(x) for x in states]
    mix_normed = [x * r for x, r in zip(states, mix_scale)]
    grad_out = [cotangent[s].astype(jnp.float32) * live[s] for s in every]
    first, second = 0, 1
    mix_rows = [(n * mix_gain_f).astype(jnp.bfloat16) for n in mix_normed]
    mix_full = [gather_rows(mix_rows[first])]
    mix_full.append(gather_rows(after(mix_rows[second], mix_full[first])))
    cot_rows = [g.astype(jnp.bfloat16) for g in grad_out]
    cot_full = [gather_rows(after(cot_rows[first], mix_full[first]))]
    cot_full.append(gather_rows(after(cot_rows[second], mix_full[second], cot_full[first])))

    def mix_forward(s, inputs):
        return mixer_forward(
            a_log[None],
            dt_bias[None],
            inputs[None],
            query_key_value_gate_weight,
            scalar_weight,
            conv_w,
            o_gain_f,
        )

    def mix_backward(s, grad_head, start, count):
        return mixer_backward(
            start,
            count,
            a_log[None],
            dt_bias[None],
            grad_head[None],
            *kept[s][1:],
            conv_w,
            o_gain_f,
        )

    def branch_begin(head_rows):
        return scatter_begin(product_t(head_rows, output_weight))

    def ffn_begin(branch, inputs):
        middle = inputs + branch
        scale = row_scale(middle)
        normed = middle * scale
        return middle, scale, normed, (normed * ffn_gain_f).astype(jnp.bfloat16)

    def ffn_middle(full, grad_hidden):
        gate = product(full, gate_weight)
        up = product(full, up_weight)
        sig = jax.nn.sigmoid(gate)
        act = gate * sig
        units = (act * up).astype(jnp.bfloat16)
        grad_gate = (grad_hidden * up * sig * (1.0 + gate * (1.0 - sig))).astype(jnp.bfloat16)
        grad_up = (grad_hidden * act).astype(jnp.bfloat16)
        back_part = product_t(grad_gate, gate_weight) + product_t(grad_up, up_weight)
        return units, grad_gate, grad_up, scatter_begin(back_part)

    def ffn_end(s, grad_in, gate_fact):
        middle, scale, normed, _ = gate_fact
        grad_mid = grad_in[1] + norm_back(grad_in[0], normed, scale, ffn_gain_f)
        return grad_mid, grad_mid.astype(jnp.bfloat16)

    kept = [mix_forward(first, mix_full[first])]
    head_low = [kept[first][0][0]]
    branch = [branch_begin(head_low[first])]
    kept.append(mix_forward(second, after(mix_full[second], branch[first][0], cot_full[first])))
    head_low.append(kept[second][0][0])
    facts = [
        ffn_begin(
            scatter_end(*branch[first]), after(states[first], head_low[second], cot_full[second])
        )
    ]
    branch.append(branch_begin(after(head_low[second], facts[first][3])))
    grad_hidden = [
        product(after(cot_full[s], branch[second][0]), down_weight) for s in every
    ]
    ffn_full = [after(gather_rows(facts[first][3]), grad_hidden[first], grad_hidden[second])]
    inner = [ffn_middle(ffn_full[first], grad_hidden[first])]
    facts.append(
        ffn_begin(
            scatter_end(*branch[second]), after(states[second], inner[first][3][0])
        )
    )
    parts_of = lambda s: [
        rows_sum([left], [right])
        for left, right in (
            (cot_full[s], inner[s][0]),
            (ffn_full[s], inner[s][1]),
            (ffn_full[s], inner[s][2]),
        )
    ]
    out_part = [scatter_begin(product_t(after(inner[first][0], facts[second][3]), down_weight))]
    early = parts_of(first)
    ffn_full.append(after(gather_rows(facts[second][3]), out_part[first][0], *early))
    inner.append(ffn_middle(ffn_full[second], grad_hidden[second]))
    grad_ffn_in = [scatter_end(*inner[first][3])]
    ends = [
        ffn_end(
            first, (grad_ffn_in[first], after(grad_out[first], inner[second][3][0])), facts[first]
        )
    ]
    late = [
        rows_sum([after(left, ends[first][1])], [right])
        for left, right in (
            (cot_full[second], inner[second][0]),
            (ffn_full[second], inner[second][1]),
            (ffn_full[second], inner[second][2]),
        )
    ]
    ffn_sums = [(one + two).astype(jnp.bfloat16) for one, two in zip(early, late)]
    out_part.append(scatter_begin(product_t(inner[second][0], down_weight)))
    down_begin = halve(ffn_sums[:1], 1) + (1,)
    gate_begin = halve(ffn_sums[1:2], 1) + (1,)
    up_begin = halve(ffn_sums[2:], 1) + (1,)
    grad_ffn_in.append(scatter_end(*inner[second][3]))
    ends.append(
        ffn_end(
            second,
            (grad_ffn_in[second], after(grad_out[second], down_begin[0], gate_begin[0], up_begin[0])),
            facts[second],
        )
    )
    branch_full = [gather_rows(ends[first][1])]
    flying = [sum_step(down_begin), sum_step(gate_begin)]
    grad_head = product(
        after(branch_full[first], ends[second][1], flying[0][0], flying[1][0]), output_weight
    )
    whole = mix_backward(first, grad_head, 0, heads)
    proj_first = whole[0][0]
    branch_full.append(after(gather_rows(ends[second][1]), proj_first))
    flying = [sum_step(hold(state, proj_first)) for state in flying + [up_begin]]
    grad_head = product(branch_full[second], output_weight)
    flying.append(
        sum_begin([rows_sum(branch_full, head_low).astype(jnp.bfloat16)], 0)
    )
    scalar_low = [scalar_rows(whole, heads)]
    halves = 2 if heads % 2 == 0 else 1
    count = heads // halves
    chunk = count * HEAD
    pieces, qkvg_states, mix_parts, mix_second = [], [], [], None
    for part in range(halves):
        last = part == halves - 1
        columns = slice(part * chunk, (part + 1) * chunk)
        sends = [state[0] for state in flying + qkvg_states]
        piece = mix_backward(second, after(grad_head, *sends), part * count, count)
        pieces.append(piece)
        proj_piece = piece[0][0]
        qkvg_states = [sum_next(hold(state, proj_piece)) for state in qkvg_states]
        sends = [proj_piece] + [state[0] for state in qkvg_states]
        flying = [sum_next(hold(state, *sends)) for state in flying]
        sends = [state[0] for state in flying + qkvg_states]
        rows = after(proj_piece, *sends)
        term = product_t(rows, query_key_value_gate_weight[:, columns])
        mix_second = term if part == 0 else mix_second + term
        if part == 0:
            mix_parts.append(
                scatter_begin(
                    product_t(after(proj_first, *sends), query_key_value_gate_weight)
                    + product_t(scalar_low[first], beta_decay_weight)
                )
            )
        grads = rows_sum(mix_full, [proj_first[:, columns], rows]).astype(jnp.bfloat16)
        state = sum_begin([grads], 0)
        waited = [state[0], mix_parts[first][0]]
        if last:
            back_scalars = jnp.concatenate([p[1] for p in pieces], axis=1)
            scalar_low.append(scalar_rows((None, back_scalars), heads))
            mix_parts.append(
                scatter_begin(
                    mix_second + product_t(scalar_low[second], beta_decay_weight)
                )
            )
            waited.append(mix_parts[second][0])
        qkvg_states.append(sum_step(hold(state, *waited)))
    sent = [qkvg_states[-1][0]]
    qkvg_states[:-1] = [sum_next(hold(state, *sent)) for state in qkvg_states[:-1]]
    sent += [state[0] for state in qkvg_states[:-1]]
    sum_qkvg = jnp.concatenate([sum_end(state) for state in qkvg_states], axis=1)
    sum_down, sum_gate, sum_up, sum_out = [sum_end(hold(state, *sent)) for state in flying]
    gathered = lambda at: whole[at] + jnp.concatenate([p[at] for p in pieces], axis=1)
    scalar_grads, taps_grads, gain_grads = gathered(1), gathered(2), gathered(3)
    grad_conv = taps_grads[0, :, :CONV].transpose(1, 0, 2).reshape(CONV, -1)
    grad_dtb = jnp.sum(scalar_grads[0, :, 1], axis=1)
    grad_alog = jnp.sum(scalar_grads[0, :, 2], axis=1)
    o_gain_part = jnp.sum(gain_grads[0, :, 0], axis=0)
    grad_w_ba = after(rows_sum(mix_full, scalar_low), *sent)
    outputs, tokens_grad = [], []
    mix_gain_part, ffn_gain_part = 0.0, 0.0
    for s in every:
        ffn_gain_part = ffn_gain_part + jnp.sum(grad_ffn_in[s] * facts[s][2], axis=0)
        outputs.append(
            ((facts[s][0] + scatter_end(*out_part[s])) * live[s]).astype(jnp.bfloat16)
        )
        grad_mix_in = scatter_end(*mix_parts[s])
        mix_gain_part = mix_gain_part + jnp.sum(grad_mix_in * mix_normed[s], axis=0)
        back_in = norm_back(grad_mix_in, mix_normed[s], mix_scale[s], mix_gain_f)
        tokens_grad.append((ends[s][0] + back_in) * live[s])
    conv_grad, alog_grad, dtb_grad, ba_grad, mix_gain_grad, o_gain_grad, ffn_gain_grad = (
        reduce_small(
            (grad_conv, grad_alog, grad_dtb, grad_w_ba),
            (mix_gain_part, o_gain_part, ffn_gain_part),
        )
    )
    block = width // lax.axis_size("dp")
    sum_ba = lax.dynamic_slice_in_dim(ba_grad, group * block, block)
    return (
        jnp.stack(outputs),
        jnp.stack(tokens_grad),
        mix_gain_grad,
        sum_qkvg,
        sum_ba,
        conv_grad,
        alog_grad,
        dtb_grad,
        o_gain_grad,
        sum_out,
        ffn_gain_grad,
        sum_gate,
        sum_up,
        sum_down,
    )


def solution(mesh):
    return jax.shard_map(
        body,
        mesh=mesh,
        in_specs=(
            P("dp", "tensor", None),
            P(),
            P(),
            P(None, "tensor"),
            P(None, "tensor"),
            P(None, "tensor"),
            P("tensor"),
            P("tensor"),
            P(),
            P(None, "tensor"),
            P(),
            P(None, "tensor"),
            P(None, "tensor"),
            P(None, "tensor"),
            P("dp", "tensor", None),
        ),
        out_specs=(
            P("dp", "tensor", None),
            P("dp", "tensor", None),
            P(),
            P("dp", "tensor"),
            P("dp", "tensor"),
            P(None, "tensor"),
            P("tensor"),
            P("tensor"),
            P(),
            P("dp", "tensor"),
            P(),
            P("dp", "tensor"),
            P("dp", "tensor"),
            P("dp", "tensor"),
        ),
        check_vma=False,
    )
```

```python
import functools

import jax
import jax.numpy as jnp
from jax import lax
from jax.experimental import pallas as pl
from jax.experimental.pallas import tpu as pltpu
from jax.sharding import PartitionSpec as P

DK = 128
DV = 256
CONV = 4
SPAN = 64
PRE = 2 * DK + DV
HEAD = PRE + DV
TILE = 2 * SPAN
F32 = jnp.float32
BF16 = jnp.bfloat16

EPS_ROW = 1e-06
EPS_HEAD = 1e-05
EPS_UNIT = 1e-06

NN = (((1,), (0,)), ((), ()))
NT = (((1,), (1,)), ((), ()))
TN = (((0,), (0,)), ((), ()))


def mm(left, right, dims=NN):
    return lax.dot_general(
        left.astype(BF16), right.astype(BF16), dims, preferred_element_type=F32
    )


def tile_masks():
    row = lax.broadcasted_iota(jnp.int32, (TILE, TILE), 0)
    col = lax.broadcasted_iota(jnp.int32, (TILE, TILE), 1)
    return row, col, row ^ col


def shifted(rows, steps):
    length = rows.shape[0]
    if steps == 0:
        return rows
    pos = lax.broadcasted_iota(jnp.int32, rows.shape, 0)
    rolled = pltpu.roll(rows, steps % length, axis=0)
    keep = pos >= steps if steps > 0 else pos < length + steps
    return jnp.where(keep, rolled, 0.0)


def convolve(pre, taps):
    summed = taps[CONV - 1 : CONV] * pre
    for back in range(1, CONV):
        tap = CONV - 1 - back
        summed = summed + taps[tap : tap + 1] * shifted(pre, back)
    return summed


def unit_rows(raw):
    scale = lax.rsqrt(jnp.sum(raw * raw, axis=1, keepdims=True) + EPS_UNIT)
    return raw * scale, scale


def decay_rows(scalars, a_log, dt_bias):
    rate = jnp.exp(jnp.full((1, 1), a_log, F32))
    shifted_in = scalars[1:2] + dt_bias
    soft = jnp.maximum(shifted_in, 0.0) + jnp.log1p(jnp.exp(-jnp.abs(shifted_in)))
    return lax.logistic(scalars[0:1]), -rate * soft, -rate * lax.logistic(shifted_in)


def tile_scalars(row, col, apart, beta_row, decay_row):
    lower = (apart < SPAN) & (row >= col)
    eye = apart == 0
    cum_col = jnp.sum(jnp.where(lower, decay_row, 0.0), axis=1, keepdims=True)
    beta_col = jnp.sum(jnp.where(eye, beta_row, 0.0), axis=1, keepdims=True)
    cum_row = jnp.sum(jnp.where(eye, cum_col, 0.0), axis=0, keepdims=True)
    last = row | (SPAN - 1)
    last_col = jnp.sum(jnp.where(col == last, cum_row, 0.0), axis=1, keepdims=True)
    decay = jnp.where(lower, jnp.exp(jnp.where(lower, cum_col - cum_row, 0.0)), 0.0)
    return cum_col, beta_col, last_col, decay


def invert(apart, couplings):
    eye = jnp.where(apart == 0, 1.0, 0.0)
    inverses = [eye - jnp.where(apart == 1, coupling, 0.0) for coupling in couplings]
    size = 2
    while size < SPAN:
        level = (apart >= size) & (apart < 2 * size)
        inner = [
            mm(jnp.where(level, coupling, 0.0), inverse)
            for coupling, inverse in zip(couplings, inverses)
        ]
        inverses = [inverse - mm(inverse, part) for inverse, part in zip(inverses, inner)]
        size *= 2
    return inverses


def mixer_kernel(
    a_log_ref,
    dt_bias_ref,
    mix_ref,
    weight_ref,
    scalar_weight_ref,
    taps_ref,
    gain_ref,
    head_ref,
    proj_ref,
    scalar_ref,
    inverse_ref,
    state_ref,
    mixed_ref,
    fresh_ref,
):
    head = pl.program_id(1)
    inputs = mix_ref[0]
    projected = mm(inputs, weight_ref[...])
    proj_ref[0] = projected
    scalars = mm(scalar_weight_ref[0], inputs, NT)
    scalar_ref[0, 0] = scalars
    beta_all, decay_all, _ = decay_rows(scalars, a_log_ref[0, head], dt_bias_ref[0, head])
    summed = convolve(projected[:, :PRE], taps_ref[...])
    active = summed * lax.logistic(summed)
    queries = (unit_rows(active[:, :DK])[0] * DK ** (-0.5)).astype(BF16)
    keys = unit_rows(active[:, DK : 2 * DK])[0].astype(BF16)
    vals = active[:, 2 * DK :].astype(BF16)
    row, col, apart = tile_masks()
    strict = (apart < SPAN) & (row > col)
    length = inputs.shape[0]
    per = TILE // SPAN
    tiles = range(length // TILE)
    spans = [slice(tile * TILE, (tile + 1) * TILE) for tile in tiles]
    facts = [
        tile_scalars(row, col, apart, beta_all[:, span], decay_all[:, span]) for span in spans
    ]
    couplings = [
        jnp.where(strict, fact[1] * mm(keys[span], keys[span], NT) * fact[3], 0.0)
        for span, fact in zip(spans, facts)
    ]
    inverses = invert(apart, couplings)
    prepared = []
    for tile in tiles:
        span = spans[tile]
        cum_col, beta_col, last_col, decay = facts[tile]
        inverse_ref[0, 0, tile] = inverses[tile]
        k_f = keys[span].astype(F32)
        grow = jnp.exp(cum_col)
        solved_w = mm(inverses[tile], (beta_col * grow) * k_f)
        solved_u = mm(inverses[tile], beta_col * vals[span].astype(F32))
        scores = mm(queries[span], keys[span], NT) * decay
        grown = queries[span].astype(F32) * grow
        tail = k_f * jnp.exp(last_col - cum_col)
        both = jnp.concatenate([solved_w, solved_u], axis=1).astype(BF16)
        steps = [
            mm(tail[block * SPAN : (block + 1) * SPAN], both[block * SPAN : (block + 1) * SPAN], TN)
            for block in range(per)
        ]
        prepared.append((solved_w, solved_u, scores, grown, steps))
    state = jnp.zeros((DK, DV), F32)
    states = []
    for tile in tiles:
        for block in range(per):
            states.append(state.astype(BF16))
            state_ref[0, 0, tile * per + block] = state
            step = prepared[tile][4][block]
            carry = jnp.exp(facts[tile][2][block * SPAN : block * SPAN + 1])
            state = carry * state + step[:, DK:] - mm(step[:, :DK], state)
    for tile in tiles:
        span = spans[tile]
        solved_w, solved_u, scores, grown, _ = prepared[tile]
        fresh = []
        read = []
        for block in range(per):
            part = slice(block * SPAN, (block + 1) * SPAN)
            used = mm(
                jnp.concatenate([solved_w[part], grown[part]], axis=0), states[tile * per + block]
            )
            fresh.append(solved_u[part] - used[:SPAN])
            read.append(used[SPAN:])
        fresh = jnp.concatenate(fresh, axis=0)
        mixed = jnp.concatenate(read, axis=0) + mm(scores, fresh)
        fresh_ref[0, 0, span] = fresh
        mixed_ref[0, 0, span] = mixed
        scale = lax.rsqrt(jnp.mean(mixed * mixed, axis=1, keepdims=True) + EPS_HEAD)
        gate = projected[span, PRE:]
        head_ref[0, span] = (
            mixed * scale * gain_ref[...] * (gate * lax.logistic(gate))
        ).astype(BF16)


def mixer_forward(a_log, dt_bias, mix, weight, scalar_weight, taps, gain):
    slots, length, width = mix.shape
    heads = weight.shape[1] // HEAD
    blocks = length // SPAN
    tiles = length // TILE
    unit = lambda s, h: (s, h, 0, 0)
    unit5 = lambda s, h: (s, h, 0, 0, 0)
    return pl.pallas_call(
        mixer_kernel,
        name="mixer_forward",
        grid=(slots, heads),
        in_specs=[
            pl.BlockSpec(memory_space=pltpu.SMEM),
            pl.BlockSpec(memory_space=pltpu.SMEM),
            pl.BlockSpec((1, length, width), lambda s, h: (s, 0, 0)),
            pl.BlockSpec((width, HEAD), lambda s, h: (0, h)),
            pl.BlockSpec((1, 8, width), lambda s, h: (h, 0, 0)),
            pl.BlockSpec((CONV, PRE), lambda s, h: (0, h)),
            pl.BlockSpec((1, DV), lambda s, h: (0, 0)),
        ],
        out_specs=[
            pl.BlockSpec((1, length, DV), lambda s, h: (s, 0, h)),
            pl.BlockSpec((1, length, HEAD), lambda s, h: (s, 0, h)),
            pl.BlockSpec((1, 1, 8, length), unit),
            pl.BlockSpec((1, 1, tiles, TILE, TILE), unit5),
            pl.BlockSpec((1, 1, blocks, DK, DV), unit5),
            pl.BlockSpec((1, 1, length, DV), unit),
            pl.BlockSpec((1, 1, length, DV), unit),
        ],
        out_shape=[
            jax.ShapeDtypeStruct((slots, length, heads * DV), BF16),
            jax.ShapeDtypeStruct((slots, length, heads * HEAD), F32),
            jax.ShapeDtypeStruct((slots, heads, 8, length), F32),
            jax.ShapeDtypeStruct((slots, heads, tiles, TILE, TILE), F32),
            jax.ShapeDtypeStruct((slots, heads, blocks, DK, DV), F32),
            jax.ShapeDtypeStruct((slots, heads, length, DV), F32),
            jax.ShapeDtypeStruct((slots, heads, length, DV), F32),
        ],
        cost_estimate=pl.CostEstimate(
            flops=slots * heads * length * 24_000_000,
            transcendentals=slots * heads * length * 2_000,
            bytes_accessed=slots * heads * length * 9_000,
        ),
        compiler_params=pltpu.CompilerParams(
            dimension_semantics=("arbitrary", "arbitrary"), vmem_limit_bytes=56 << 20
        ),
    )(a_log, dt_bias, mix, weight, scalar_weight, taps, gain)


def mixer_back_kernel(
    start,
    a_log_ref,
    dt_bias_ref,
    grad_ref,
    proj_ref,
    scalar_ref,
    inverse_ref,
    state_ref,
    mixed_ref,
    fresh_ref,
    taps_ref,
    gain_ref,
    grad_proj_ref,
    grad_scalar_ref,
    grad_taps_ref,
    grad_gain_ref,
):
    head = start + pl.program_id(1)
    length = grad_ref.shape[1]
    pre = proj_ref[0, :, :PRE]
    taps = taps_ref[...]
    gain = gain_ref[...]
    scalars = scalar_ref[0, 0]
    beta_all, decay_all, slope_all = decay_rows(
        scalars, a_log_ref[0, head], dt_bias_ref[0, head]
    )
    summed = convolve(pre, taps)
    sig = lax.logistic(summed)
    active = summed * sig
    query_unit, query_scale = unit_rows(active[:, :DK])
    key_unit, key_scale = unit_rows(active[:, DK : 2 * DK])
    queries = (query_unit * DK ** (-0.5)).astype(BF16)
    keys = key_unit.astype(BF16)
    vals = active[:, 2 * DK :].astype(BF16)
    row, col, apart = tile_masks()
    lower = (apart < SPAN) & (row >= col)
    strict = (apart < SPAN) & (row > col)
    eye = apart == 0
    is_last = (row[:, :1] & (SPAN - 1)) == (SPAN - 1)
    per = TILE // SPAN
    grad_gain = jnp.zeros((1, DV), F32)
    carried = jnp.zeros((DK, DV), F32)
    grad_active = [None] * (length // TILE)
    grad_beta_rows = [None] * (length // TILE)
    grad_decay_rows = [None] * (length // TILE)
    for tile in reversed(range(length // TILE)):
        span = slice(tile * TILE, (tile + 1) * TILE)
        cum_col, beta_col, last_col, decay = tile_scalars(
            row, col, apart, beta_all[:, span], decay_all[:, span]
        )
        gate = proj_ref[0, span, PRE:]
        gate_sig = lax.logistic(gate)
        gate_act = gate * gate_sig
        mixed = mixed_ref[0, 0, span]
        scale = lax.rsqrt(jnp.mean(mixed * mixed, axis=1, keepdims=True) + EPS_HEAD)
        normed = mixed * scale
        grad = grad_ref[0, span]
        grad_normed = grad * normed
        grad_gain = grad_gain + jnp.sum(grad_normed * gate_act, axis=0, keepdims=True)
        grad_proj_ref[0, span, PRE:] = (
            grad_normed * gain * (gate_sig * (1.0 + gate * (1.0 - gate_sig)))
        ).astype(BF16)
        weighted = grad * gain * gate_act
        grad_mixed = scale * (
            weighted - normed * jnp.mean(weighted * normed, axis=1, keepdims=True)
        )
        q = queries[span]
        k = keys[span]
        v = vals[span]
        q_f = q.astype(F32)
        k_f = k.astype(F32)
        v_f = v.astype(F32)
        gram = mm(k, k, NT)
        coupling = jnp.where(strict, beta_col * gram * decay, 0.0)
        scores = mm(q, k, NT) * decay
        inverse = inverse_ref[0, 0, tile].astype(BF16)
        grow = jnp.exp(cum_col)
        fall = jnp.exp(last_col - cum_col)
        beta_grow = beta_col * grow
        key_in = beta_grow * k_f
        solved_w = mm(inverse, key_in)
        solved_u = mm(inverse, beta_col * v_f)
        grown = q_f * grow
        tail = k_f * fall
        fresh = fresh_ref[0, 0, span]
        grad_low = grad_mixed.astype(BF16)
        local = mm(scores, grad_low, TN)
        grad_fresh = [None] * per
        grad_grown = [None] * per
        grad_tail = [None] * per
        grad_w = [None] * per
        carry_terms = [None] * per
        for block in reversed(range(per)):
            part = slice(block * SPAN, (block + 1) * SPAN)
            state = state_ref[0, 0, tile * per + block]
            carry = jnp.exp(last_col[block * SPAN : block * SPAN + 1])
            here = local[part] + mm(tail[part], carried)
            grad_fresh[block] = here
            both = mm(jnp.concatenate([grad_low[part], here.astype(BF16)], axis=0), state, NT)
            grad_grown[block] = both[:SPAN]
            grad_w[block] = -both[SPAN:]
            grad_tail[block] = mm(fresh[part], carried, NT)
            product = jnp.sum(state * carried, axis=0, keepdims=True)
            carry_terms[block] = carry * jnp.sum(product, axis=1, keepdims=True)
            carried = carry * carried + mm(
                jnp.concatenate([grown[part], -solved_w[part]], axis=0),
                jnp.concatenate([grad_low[part], here.astype(BF16)], axis=0),
                TN,
            )
        grad_fresh = jnp.concatenate(grad_fresh, axis=0)
        grad_grown = jnp.concatenate(grad_grown, axis=0)
        grad_tail = jnp.concatenate(grad_tail, axis=0)
        grad_w = jnp.concatenate(grad_w, axis=0)
        grad_key_in = mm(inverse, grad_w, TN)
        grad_val_in = mm(inverse, grad_fresh, TN)
        grad_coupling = jnp.where(
            strict, -(mm(grad_key_in, solved_w, NT) + mm(grad_val_in, solved_u, NT)), 0.0
        )
        grad_scores = mm(grad_low, fresh, NT)
        score_term = grad_scores * decay
        gram_term = grad_coupling * decay
        grad_beta = (
            jnp.sum(gram_term * gram, axis=1, keepdims=True)
            + grow * jnp.sum(grad_key_in * k_f, axis=1, keepdims=True)
            + jnp.sum(grad_val_in * v_f, axis=1, keepdims=True)
        )
        gram_term = gram_term * beta_col
        exponent = grad_coupling * coupling + grad_scores * scores
        tail_sum = jnp.sum(grad_tail * tail, axis=1, keepdims=True)
        grad_cum = (
            jnp.sum(exponent, axis=1, keepdims=True)
            + jnp.sum(grad_grown * grown, axis=1, keepdims=True)
            + jnp.sum(grad_key_in * key_in, axis=1, keepdims=True)
            - tail_sum
        )
        ends = []
        for block in range(per):
            part = slice(block * SPAN, (block + 1) * SPAN)
            total = jnp.sum(tail_sum[part], axis=0, keepdims=True) + carry_terms[block]
            ends.append(jnp.broadcast_to(total, (SPAN, 1)))
        grad_cum = grad_cum + jnp.where(is_last, jnp.concatenate(ends, axis=0), 0.0)
        column_sum = jnp.sum(exponent, axis=0, keepdims=True)
        cum_back = jnp.sum(jnp.where(eye, column_sum, 0.0), axis=1, keepdims=True)
        grad_cum = grad_cum - cum_back
        grad_decay_rows[tile] = jnp.sum(jnp.where(lower, grad_cum, 0.0), axis=0, keepdims=True)
        grad_beta_rows[tile] = jnp.sum(jnp.where(eye, grad_beta, 0.0), axis=0, keepdims=True)
        grad_q = mm(score_term, k) + grad_grown * grow
        grad_k = (
            mm(score_term, q, TN)
            + mm(gram_term, k)
            + mm(gram_term, k, TN)
            + grad_tail * fall
            + beta_grow * grad_key_in
        )
        grad_v = beta_col * grad_val_in
        q_u = query_unit[span]
        k_u = key_unit[span]
        grad_query_raw = (query_scale[span] * DK ** (-0.5)) * (
            grad_q - q_u * jnp.sum(grad_q * q_u, axis=1, keepdims=True)
        )
        grad_key_raw = key_scale[span] * (
            grad_k - k_u * jnp.sum(grad_k * k_u, axis=1, keepdims=True)
        )
        grad_active[tile] = jnp.concatenate([grad_query_raw, grad_key_raw, grad_v], axis=1)
    grad_gain_ref[0, 0] = jnp.broadcast_to(grad_gain, (8, DV))
    grad_summed = jnp.concatenate(grad_active, axis=0) * (sig * (1.0 + summed * (1.0 - sig)))
    grad_pre = taps[CONV - 1 : CONV] * grad_summed
    grad_taps = [None] * CONV
    grad_taps[CONV - 1] = jnp.sum(grad_summed * pre, axis=0, keepdims=True)
    for back in range(1, CONV):
        tap = CONV - 1 - back
        ahead = shifted(grad_summed, -back)
        grad_pre = grad_pre + taps[tap : tap + 1] * ahead
        grad_taps[tap] = jnp.sum(ahead * pre, axis=0, keepdims=True)
    grad_proj_ref[0, :, :PRE] = grad_pre.astype(BF16)
    grad_taps_ref[0, 0] = jnp.concatenate(grad_taps + [jnp.zeros((8 - CONV, PRE), F32)], axis=0)
    grad_beta_all = jnp.concatenate(grad_beta_rows, axis=1)
    grad_decay_all = jnp.concatenate(grad_decay_rows, axis=1)
    grad_scalar_ref[0, 0] = jnp.concatenate(
        [
            grad_beta_all * beta_all * (1.0 - beta_all),
            grad_decay_all * slope_all,
            grad_decay_all * decay_all,
            jnp.zeros((5, length), F32),
        ],
        axis=0,
    )


def mixer_backward(
    start, heads, a_log, dt_bias, grad_head, projected, scalars, inverse, states, mixed, fresh,
    taps, gain
):
    slots, length, _ = grad_head.shape
    blocks = length // SPAN
    tiles = length // TILE
    own = lambda s, h: (s, h, 0, 0)
    unit = lambda s, h: (s, start + h, 0, 0)
    unit5 = lambda s, h: (s, start + h, 0, 0, 0)
    return pl.pallas_call(
        functools.partial(mixer_back_kernel, start),
        name="mixer_backward",
        grid=(slots, heads),
        in_specs=[
            pl.BlockSpec(memory_space=pltpu.SMEM),
            pl.BlockSpec(memory_space=pltpu.SMEM),
            pl.BlockSpec((1, length, DV), lambda s, h: (s, 0, start + h)),
            pl.BlockSpec((1, length, HEAD), lambda s, h: (s, 0, start + h)),
            pl.BlockSpec((1, 1, 8, length), unit),
            pl.BlockSpec((1, 1, tiles, TILE, TILE), unit5),
            pl.BlockSpec((1, 1, blocks, DK, DV), unit5),
            pl.BlockSpec((1, 1, length, DV), unit),
            pl.BlockSpec((1, 1, length, DV), unit),
            pl.BlockSpec((CONV, PRE), lambda s, h: (0, start + h)),
            pl.BlockSpec((1, DV), lambda s, h: (0, 0)),
        ],
        out_specs=[
            pl.BlockSpec((1, length, HEAD), lambda s, h: (s, 0, h)),
            pl.BlockSpec((1, 1, 8, length), own),
            pl.BlockSpec((1, 1, 8, PRE), own),
            pl.BlockSpec((1, 1, 8, DV), own),
        ],
        out_shape=[
            jax.ShapeDtypeStruct((slots, length, heads * HEAD), BF16),
            jax.ShapeDtypeStruct((slots, heads, 8, length), F32),
            jax.ShapeDtypeStruct((slots, heads, 8, PRE), F32),
            jax.ShapeDtypeStruct((slots, heads, 8, DV), F32),
        ],
        cost_estimate=pl.CostEstimate(
            flops=slots * heads * length * 15_000_000,
            transcendentals=slots * heads * length * 2_000,
            bytes_accessed=slots * heads * length * 9_000,
        ),
        compiler_params=pltpu.CompilerParams(
            dimension_semantics=("arbitrary", "arbitrary"), vmem_limit_bytes=56 << 20
        ),
    )(
        a_log,
        dt_bias,
        grad_head,
        projected,
        scalars,
        inverse,
        states,
        mixed,
        fresh,
        taps,
        gain,
    )


def row_scale(values):
    return lax.rsqrt(jnp.mean(values * values, axis=-1, keepdims=True) + EPS_ROW)


def norm_back(grad_out, normed, scale, gain_vec):
    weighted = grad_out * gain_vec
    return scale * (weighted - normed * jnp.mean(weighted * normed, axis=-1, keepdims=True))


def product(left, right):
    return jnp.dot(left, right, preferred_element_type=jnp.float32)


def product_t(left, right):
    return lax.dot_general(left, right, NT, preferred_element_type=jnp.float32)


def rows_sum(lefts, rights):
    total = None
    for left, right in zip(lefts, rights):
        term = lax.dot_general(left, right, TN, preferred_element_type=jnp.float32)
        total = term if total is None else total + term
    return total


def after(value, *others):
    return lax.optimization_barrier((value, *others))[0]


def gather_rows(rows):
    if lax.axis_size("tensor") != 2:
        return lax.all_gather(rows, "tensor", axis=0, tiled=True)
    other = lax.ppermute(rows, "tensor", [(0, 1), (1, 0)])
    first = lax.axis_index("tensor") == 0
    return jnp.concatenate(
        [jnp.where(first, rows, other), jnp.where(first, other, rows)], axis=0
    )


def scatter_begin(partial):
    if lax.axis_size("tensor") != 2:
        return partial.astype(jnp.bfloat16), None
    half = partial.shape[0] // 2
    rank = lax.axis_index("tensor")
    sent = lax.dynamic_slice_in_dim(partial, (1 - rank) * half, half).astype(jnp.bfloat16)
    return sent, lax.dynamic_slice_in_dim(partial, rank * half, half)


def scatter_end(sent, kept):
    if kept is None:
        return lax.psum_scatter(sent, "tensor", scatter_dimension=0, tiled=True).astype(
            jnp.float32
        )
    other = lax.ppermute(sent, "tensor", [(0, 1), (1, 0)])
    return kept + other.astype(jnp.float32)


def pairs(ranks, bit):
    return [(rank, rank ^ bit) for rank in range(ranks)]


def halve(held, bit):
    ranks = lax.axis_size("dp")
    left = ranks // (2 * bit)
    mine = (lax.axis_index("dp") // bit) % 2
    sends, keeps = [], []
    for grads in held:
        rows = grads.reshape(left, 2, -1, grads.shape[-1])
        sends.append(lax.dynamic_index_in_dim(rows, 1 - mine, 1, keepdims=False))
        keeps.append(lax.dynamic_index_in_dim(rows, mine, 1, keepdims=False))
    join = lambda parts: parts[0] if len(parts) == 1 else jnp.concatenate(parts, axis=-1)
    return join(sends).astype(jnp.bfloat16), join(keeps)


def swap_add(sent, kept, bit):
    ranks = lax.axis_size("dp")
    got = lax.ppermute(sent, "dp", pairs(ranks, bit))
    total = kept.astype(jnp.float32) + got.astype(jnp.float32)
    return total if 2 * bit == ranks else total.astype(jnp.bfloat16)


def sum_begin(held, steps):
    bit = 1
    for _ in range(steps):
        sent, kept = halve(held, bit)
        held = [swap_add(sent, kept, bit)]
        bit *= 2
    return halve(held, bit) + (bit,)


def hold(state, *others):
    sent, kept, bit = state
    return sent, after(kept, *others), bit


def sum_step(state):
    sent, kept, bit = state
    return halve([swap_add(sent, kept, bit)], 2 * bit) + (2 * bit,)


def sum_next(state):
    return state if 2 * state[2] >= lax.axis_size("dp") else sum_step(state)


def sum_end(state):
    sent, kept, bit = state
    held = swap_add(sent, kept, bit)
    while 2 * bit < lax.axis_size("dp"):
        bit *= 2
        held = swap_add(*halve([held], bit), bit)
    return held.reshape(-1, held.shape[-1])


def sum_all(values, axis):
    ranks = lax.axis_size(axis)
    bit = 1
    while bit < ranks:
        values = values + lax.ppermute(values, axis, pairs(ranks, bit))
        bit *= 2
    return values


def reduce_small(own_parts, shared_parts):
    own = jnp.concatenate([part.reshape(-1) for part in own_parts])
    shared = sum_all(jnp.concatenate([part.reshape(-1) for part in shared_parts]), "tensor")
    total = sum_all(jnp.concatenate([own, shared]), "dp")
    results = []
    at = 0
    for part in own_parts + shared_parts:
        results.append(total[at : at + part.size].reshape(part.shape))
        at += part.size
    return results


def scalar_rows(back, heads):
    return back[1][0, :, :2].transpose(2, 0, 1).reshape(-1, 2 * heads).astype(jnp.bfloat16)


def body(
    tokens,
    seq_counts,
    mix_gain,
    query_key_value_gate_weight,
    beta_decay_weight,
    conv_w,
    a_log,
    dt_bias,
    o_gain,
    output_weight,
    ffn_gain,
    gate_weight,
    up_weight,
    down_weight,
    cotangent,
):
    slots = tokens.shape[0]
    heads = a_log.shape[0]
    width = tokens.shape[2]
    every = range(slots)
    group = lax.axis_index("dp")
    count_here = lax.dynamic_index_in_dim(seq_counts, group, keepdims=False)
    mix_gain_f = mix_gain.astype(jnp.float32)
    ffn_gain_f = ffn_gain.astype(jnp.float32)
    o_gain_f = o_gain.astype(jnp.float32)[None]
    scalar_weight = jnp.pad(
        beta_decay_weight.T.reshape(heads, 2, width), ((0, 0), (0, 6), (0, 0))
    )
    live = [(s < count_here).astype(jnp.float32) for s in every]
    states = [tokens[s].astype(jnp.float32) for s in every]
    mix_scale = [row_scale(x) for x in states]
    mix_normed = [x * r for x, r in zip(states, mix_scale)]
    grad_out = [cotangent[s].astype(jnp.float32) * live[s] for s in every]
    first, second = 0, 1
    mix_rows = [(n * mix_gain_f).astype(jnp.bfloat16) for n in mix_normed]
    mix_full = [gather_rows(mix_rows[first])]
    mix_full.append(gather_rows(after(mix_rows[second], mix_full[first])))
    cot_rows = [g.astype(jnp.bfloat16) for g in grad_out]
    cot_full = [gather_rows(after(cot_rows[first], mix_full[first]))]
    cot_full.append(gather_rows(after(cot_rows[second], mix_full[second], cot_full[first])))

    def mix_forward(s, inputs):
        return mixer_forward(
            a_log[None],
            dt_bias[None],
            inputs[None],
            query_key_value_gate_weight,
            scalar_weight,
            conv_w,
            o_gain_f,
        )

    def mix_backward(s, grad_head, start, count):
        return mixer_backward(
            start,
            count,
            a_log[None],
            dt_bias[None],
            grad_head[None],
            *kept[s][1:],
            conv_w,
            o_gain_f,
        )

    def branch_begin(head_rows):
        return scatter_begin(product_t(head_rows, output_weight))

    def ffn_begin(branch, inputs):
        middle = inputs + branch
        scale = row_scale(middle)
        normed = middle * scale
        return middle, scale, normed, (normed * ffn_gain_f).astype(jnp.bfloat16)

    def ffn_middle(full, grad_hidden):
        gate = product(full, gate_weight)
        up = product(full, up_weight)
        sig = jax.nn.sigmoid(gate)
        act = gate * sig
        units = (act * up).astype(jnp.bfloat16)
        grad_gate = (grad_hidden * up * sig * (1.0 + gate * (1.0 - sig))).astype(jnp.bfloat16)
        grad_up = (grad_hidden * act).astype(jnp.bfloat16)
        back_part = product_t(grad_gate, gate_weight) + product_t(grad_up, up_weight)
        return units, grad_gate, grad_up, scatter_begin(back_part)

    def ffn_end(s, grad_in, gate_fact):
        middle, scale, normed, _ = gate_fact
        grad_mid = grad_in[1] + norm_back(grad_in[0], normed, scale, ffn_gain_f)
        return grad_mid, grad_mid.astype(jnp.bfloat16)

    kept = [mix_forward(first, mix_full[first])]
    head_low = [kept[first][0][0]]
    branch = [branch_begin(head_low[first])]
    kept.append(mix_forward(second, after(mix_full[second], branch[first][0], cot_full[first])))
    head_low.append(kept[second][0][0])
    facts = [
        ffn_begin(
            scatter_end(*branch[first]), after(states[first], head_low[second], cot_full[second])
        )
    ]
    branch.append(branch_begin(after(head_low[second], facts[first][3])))
    grad_hidden = [
        product(after(cot_full[s], branch[second][0]), down_weight) for s in every
    ]
    ffn_full = [after(gather_rows(facts[first][3]), grad_hidden[first], grad_hidden[second])]
    inner = [ffn_middle(ffn_full[first], grad_hidden[first])]
    facts.append(
        ffn_begin(
            scatter_end(*branch[second]), after(states[second], inner[first][3][0])
        )
    )
    parts_of = lambda s: [
        rows_sum([left], [right])
        for left, right in (
            (cot_full[s], inner[s][0]),
            (ffn_full[s], inner[s][1]),
            (ffn_full[s], inner[s][2]),
        )
    ]
    out_part = [scatter_begin(product_t(after(inner[first][0], facts[second][3]), down_weight))]
    early = parts_of(first)
    ffn_full.append(after(gather_rows(facts[second][3]), out_part[first][0], *early))
    inner.append(ffn_middle(ffn_full[second], grad_hidden[second]))
    grad_ffn_in = [scatter_end(*inner[first][3])]
    ends = [
        ffn_end(
            first, (grad_ffn_in[first], after(grad_out[first], inner[second][3][0])), facts[first]
        )
    ]
    late = [
        rows_sum([after(left, ends[first][1])], [right])
        for left, right in (
            (cot_full[second], inner[second][0]),
            (ffn_full[second], inner[second][1]),
            (ffn_full[second], inner[second][2]),
        )
    ]
    ffn_sums = [(one + two).astype(jnp.bfloat16) for one, two in zip(early, late)]
    out_part.append(scatter_begin(product_t(inner[second][0], down_weight)))
    down_begin = halve(ffn_sums[:1], 1) + (1,)
    gate_begin = halve(ffn_sums[1:2], 1) + (1,)
    up_begin = halve(ffn_sums[2:], 1) + (1,)
    grad_ffn_in.append(scatter_end(*inner[second][3]))
    ends.append(
        ffn_end(
            second,
            (grad_ffn_in[second], after(grad_out[second], down_begin[0], gate_begin[0], up_begin[0])),
            facts[second],
        )
    )
    branch_full = [gather_rows(ends[first][1])]
    flying = [sum_step(down_begin), sum_step(gate_begin)]
    grad_head = product(
        after(branch_full[first], ends[second][1], flying[0][0], flying[1][0]), output_weight
    )
    whole = mix_backward(first, grad_head, 0, heads)
    proj_first = whole[0][0]
    branch_full.append(after(gather_rows(ends[second][1]), proj_first))
    flying = [sum_step(hold(state, proj_first)) for state in flying + [up_begin]]
    grad_head = product(branch_full[second], output_weight)
    flying.append(
        sum_begin([rows_sum(branch_full, head_low).astype(jnp.bfloat16)], 0)
    )
    scalar_low = [scalar_rows(whole, heads)]
    halves = 2 if heads % 2 == 0 else 1
    count = heads // halves
    chunk = count * HEAD
    pieces, qkvg_states, mix_parts, mix_second = [], [], [], None
    for part in range(halves):
        last = part == halves - 1
        columns = slice(part * chunk, (part + 1) * chunk)
        sends = [state[0] for state in flying + qkvg_states]
        piece = mix_backward(second, after(grad_head, *sends), part * count, count)
        pieces.append(piece)
        proj_piece = piece[0][0]
        qkvg_states = [sum_next(hold(state, proj_piece)) for state in qkvg_states]
        sends = [proj_piece] + [state[0] for state in qkvg_states]
        flying = [sum_next(hold(state, *sends)) for state in flying]
        sends = [state[0] for state in flying + qkvg_states]
        rows = after(proj_piece, *sends)
        term = product_t(rows, query_key_value_gate_weight[:, columns])
        mix_second = term if part == 0 else mix_second + term
        if part == 0:
            mix_parts.append(
                scatter_begin(
                    product_t(after(proj_first, *sends), query_key_value_gate_weight)
                    + product_t(scalar_low[first], beta_decay_weight)
                )
            )
        grads = rows_sum(mix_full, [proj_first[:, columns], rows]).astype(jnp.bfloat16)
        state = sum_begin([grads], 0)
        waited = [state[0], mix_parts[first][0]]
        if last:
            back_scalars = jnp.concatenate([p[1] for p in pieces], axis=1)
            scalar_low.append(scalar_rows((None, back_scalars), heads))
            mix_parts.append(
                scatter_begin(
                    mix_second + product_t(scalar_low[second], beta_decay_weight)
                )
            )
            waited.append(mix_parts[second][0])
        qkvg_states.append(sum_step(hold(state, *waited)))
    sent = [qkvg_states[-1][0]]
    qkvg_states[:-1] = [sum_next(hold(state, *sent)) for state in qkvg_states[:-1]]
    sent += [state[0] for state in qkvg_states[:-1]]
    sum_qkvg = jnp.concatenate([sum_end(state) for state in qkvg_states], axis=1)
    sum_down, sum_gate, sum_up, sum_out = [sum_end(hold(state, *sent)) for state in flying]
    gathered = lambda at: whole[at] + jnp.concatenate([p[at] for p in pieces], axis=1)
    scalar_grads, taps_grads, gain_grads = gathered(1), gathered(2), gathered(3)
    grad_conv = taps_grads[0, :, :CONV].transpose(1, 0, 2).reshape(CONV, -1)
    grad_dtb = jnp.sum(scalar_grads[0, :, 1], axis=1)
    grad_alog = jnp.sum(scalar_grads[0, :, 2], axis=1)
    o_gain_part = jnp.sum(gain_grads[0, :, 0], axis=0)
    grad_w_ba = after(rows_sum(mix_full, scalar_low), *sent)
    outputs, tokens_grad = [], []
    mix_gain_part, ffn_gain_part = 0.0, 0.0
    for s in every:
        ffn_gain_part = ffn_gain_part + jnp.sum(grad_ffn_in[s] * facts[s][2], axis=0)
        outputs.append(
            ((facts[s][0] + scatter_end(*out_part[s])) * live[s]).astype(jnp.bfloat16)
        )
        grad_mix_in = scatter_end(mix_parts[s][0], after(mix_parts[s][1], sent[0]))
        mix_gain_part = mix_gain_part + jnp.sum(grad_mix_in * mix_normed[s], axis=0)
        back_in = norm_back(grad_mix_in, mix_normed[s], mix_scale[s], mix_gain_f)
        tokens_grad.append((ends[s][0] + back_in) * live[s])
    conv_grad, alog_grad, dtb_grad, ba_grad, mix_gain_grad, o_gain_grad, ffn_gain_grad = (
        reduce_small(
            (grad_conv, grad_alog, grad_dtb, grad_w_ba),
            (mix_gain_part, o_gain_part, ffn_gain_part),
        )
    )
    block = width // lax.axis_size("dp")
    sum_ba = lax.dynamic_slice_in_dim(ba_grad, group * block, block)
    return (
        jnp.stack(outputs),
        jnp.stack(tokens_grad),
        mix_gain_grad,
        sum_qkvg,
        sum_ba,
        conv_grad,
        alog_grad,
        dtb_grad,
        o_gain_grad,
        sum_out,
        ffn_gain_grad,
        sum_gate,
        sum_up,
        sum_down,
    )


def solution(mesh):
    return jax.shard_map(
        body,
        mesh=mesh,
        in_specs=(
            P("dp", "tensor", None),
            P(),
            P(),
            P(None, "tensor"),
            P(None, "tensor"),
            P(None, "tensor"),
            P("tensor"),
            P("tensor"),
            P(),
            P(None, "tensor"),
            P(),
            P(None, "tensor"),
            P(None, "tensor"),
            P(None, "tensor"),
            P("dp", "tensor", None),
        ),
        out_specs=(
            P("dp", "tensor", None),
            P("dp", "tensor", None),
            P(),
            P("dp", "tensor"),
            P("dp", "tensor"),
            P(None, "tensor"),
            P("tensor"),
            P("tensor"),
            P(),
            P("dp", "tensor"),
            P(),
            P("dp", "tensor"),
            P("dp", "tensor"),
            P("dp", "tensor"),
        ),
        check_vma=False,
    )
```
